32 devices in a mesh: rep: 16 (over z, y, core), shard: 2 (over x).
Axes of the slice: x: 2, y: 2, z: 4, core: 2. Of those that a mesh axis runs over, the one named last changes fastest.
Arguments:
- layer_in: bfloat16 [64, 1024, 768], P(('rep', 'shard')), may hold values from -6 to 6
- cotangent: bfloat16 [64, 1024, 768], P(('rep', 'shard')), may hold values from -6 to 6
- lengths: int32 [16, 4], P('rep'), may hold values from 1 to 1024, 2048 in all within a row
- dealing: int32 [16, 4], P('rep'), may hold values from 0 to 3, each once within a row
- ln1_gain: bfloat16 [768], P('shard'), may hold values from 0.5 to 1.5
- ln1_bias: bfloat16 [768], P('shard'), may hold values from -0.125 to 0.125
- w_qkv: bfloat16 [768, 2304], P('shard'), may hold values from -0.21875 to 0.21875
- q_bias: bfloat16 [768], P('shard'), may hold values from -3 to 3
- v_bias: bfloat16 [768], P('shard'), may hold values from -0.125 to 0.125
- w_out: bfloat16 [768, 768], P('shard'), may hold values from -2.5 to 2.5
- out_bias: bfloat16 [768], P('shard'), may hold values from -0.625 to 0.625
- ln2_gain: bfloat16 [768], P('shard'), may hold values from 0.5 to 1.5
- ln2_bias: bfloat16 [768], P('shard'), may hold values from -0.625 to 0.625
- w_fc: bfloat16 [768, 3072], P('shard'), may hold values from -0.21875 to 0.21875
- fc_bias: bfloat16 [3072], P('shard'), may hold values from -1.75 to 1.75
- w_proj: bfloat16 [3072, 768], P('shard'), may hold values from -0.109375 to 0.109375
- proj_bias: bfloat16 [768], P('shard'), may hold values from -0.625 to 0.625
Outputs:
- layer_out: bfloat16 [64, 1024, 768], P(('rep', 'shard'))
- input_grad: bfloat16 [64, 1024, 768], P(('rep', 'shard'))
- grad_ln1_gain: float32 [768], P('shard')
- grad_ln1_bias: float32 [768], P('shard')
- grad_w_qkv: float32 [768, 2304], P('shard')
- grad_q_bias: float32 [768], P('shard')
- grad_v_bias: float32 [768], P('shard')
- grad_w_out: float32 [768, 768], P('shard')
- grad_out_bias: float32 [768], P('shard')
- grad_ln2_gain: float32 [768], P('shard')
- grad_ln2_bias: float32 [768], P('shard')
- grad_w_fc: float32 [768, 3072], P('shard')
- grad_fc_bias: float32 [3072], P('shard')
- grad_w_proj: float32 [3072, 768], P('shard')
- grad_proj_bias: float32 [768], P('shard')
The draws below stay inside these ranges and needn't reach their ends.
Inputs may be any that keep to these rules, and one draw needn't show every extreme that they name: In every row the 4 lengths sum to 2048 and one of them is 1024. `dealing`: every row is a permutation of 0 to 3.
All inputs are finite; a program needn't handle non-finite values.
Results may differ from the reference program's by a relative error of at most 0.013.
Values may be sent and summed in bfloat16 or wider, within the bound.
A program may use at most 384 MiB of HBM per device.

```python
import math
import jax
import jax.numpy as jnp
import numpy as np
from jax import lax

D = 768
HD = 64
FF = 3072
L = 1024
HALF = 512
GSEQ = 4
SEQS = 64
N_REP = 16


def levels(rng, dims, cuts, least, largest):
    loudness, own = 1.0, jax.random.fold_in(rng, 6)
    for dim, parts in cuts:
        steps = jnp.exp(jax.random.uniform(jax.random.fold_in(own, dim), (parts,), jnp.float32, least / len(cuts), largest / len(cuts)))
        loudness = loudness * jnp.repeat(steps, dims[dim] // parts).reshape([-1 if axis == dim else 1 for axis in range(len(dims))])
    return loudness


def profile(number_of, total, bound, skew):
    loads = [(1 << 20) // math.isqrt(standing ** skew) + 1 for standing in range(2, number_of + 1)]
    rest, holding = total - bound - (number_of - 1), [1] * (number_of - 1)
    while rest > 0:
        movable = [i for i in range(number_of - 1) if holding[i] < bound]
        pool, budget = sum([loads[i] for i in movable]), rest
        for i in movable:
            extra = min(bound - holding[i], max(1, budget * loads[i] // pool), rest)
            holding[i] = holding[i] + extra
            rest = rest - extra
    return np.array([bound] + holding)


def uneven(rng, amount, total, reach, slope):
    if amount == 2:
        one = jax.random.randint(rng, (), max(1, total - reach), min(reach, total - 1) + 1)
        return jnp.stack([one, total - one])
    sizes = jnp.asarray(profile(amount, total, reach, slope), jnp.int32)
    twos = (amount - 1) // 2
    donor, sink = sizes[1:1 + 2 * twos:2], sizes[2:2 + 2 * twos:2]
    room = jnp.minimum(donor - 1, reach - sink)
    passed = jax.random.randint(jax.random.fold_in(rng, 1), (twos,), 0, 1 << 20) % (room + 1)
    sizes = sizes.at[1:1 + 2 * twos:2].set(donor - passed).at[2:2 + 2 * twos:2].set(sink + passed)
    return sizes[jax.random.permutation(jax.random.fold_in(rng, 2), amount)]


def scatter_about(rng, extent, scale, limit, split=(), kind=jnp.bfloat16):
    factor_of = levels(rng, extent, split, -0.22, 0.18) if split else 1.0
    entries = jax.random.normal(rng, extent, jnp.float32) * scale * factor_of
    return jnp.minimum(jnp.maximum(entries, -limit), limit).astype(kind)


def setup_inputs(seed: int = 0) -> dict:
    key_of = jax.random.split(jax.random.key(seed), 18)
    return {
        "layer_in": scatter_about(key_of[0], (SEQS, L, D), 1.0, 6.0, ((0, 32),)),
        "cotangent": scatter_about(key_of[1], (SEQS, L, D), 1.0, 6.0, ((0, 32),)),
        "lengths": jax.vmap(lambda own: uneven(own, GSEQ, GSEQ * L // 2, L, 2))(jax.random.split(key_of[2], N_REP)).reshape((N_REP, GSEQ)).astype(jnp.int32),
        "dealing": jax.vmap(lambda own: jax.random.permutation(own, GSEQ))(jax.random.split(key_of[3], N_REP)).reshape((N_REP, GSEQ)).astype(jnp.int32),
        "ln1_gain": jnp.clip(1.0 + 0.1 * jax.random.normal(key_of[4], (D,), jnp.float32), 0.5, 1.5).astype(jnp.bfloat16),
        "ln1_bias": scatter_about(key_of[5], (D,), 0.02, 0.125, ((0, 2),)),
        "w_qkv": scatter_about(key_of[6], (D, 3 * D), D ** -0.5, 0.21875, ((0, 2),)),
        "q_bias": scatter_about(key_of[7], (D,), 0.5, 3.0, ((0, 2),)),
        "v_bias": scatter_about(key_of[8], (D,), 0.02, 0.125, ((0, 2),)),
        "w_out": scatter_about(key_of[9], (D, D), (max(D // 128, 1)) ** -0.5, 2.5, ((0, 2),)),
        "out_bias": scatter_about(key_of[10], (D,), 0.1, 0.625, ((0, 2),)),
        "ln2_gain": jnp.clip(1.0 + 0.1 * jax.random.normal(key_of[11], (D,), jnp.float32), 0.5, 1.5).astype(jnp.bfloat16),
        "ln2_bias": scatter_about(key_of[12], (D,), 0.1, 0.625, ((0, 2),)),
        "w_fc": scatter_about(key_of[13], (D, FF), D ** -0.5, 0.21875, ((0, 2),)),
        "fc_bias": scatter_about(key_of[14], (FF,), 0.3, 1.75, ((0, 2),)),
        "w_proj": scatter_about(key_of[15], (FF, D), FF ** -0.5, 0.109375, ((0, 2),)),
        "proj_bias": scatter_about(key_of[16], (D,), 0.1, 0.625, ((0, 2),)),
    }


epsilon = 1e-05
highest = lax.Precision.HIGHEST

@jax.custom_vjp
def low(v):
    return lax.optimization_barrier(v.astype(jnp.bfloat16)).astype(jnp.float32)

@jax.custom_vjp
def low_back(v):
    return v

def low_keep(v):
    return (low(v), None)

def low_pass(kept, grad):
    return (grad,)

def back_keep(v):
    return (v, None)

def back_low(kept, grad):
    return (low(grad),)
low.defvjp(low_keep, low_pass)
low_back.defvjp(back_keep, back_low)

def layer_norm(row_data, norm_gain, norm_shift):
    average = lax.optimization_barrier(jnp.mean(row_data, axis=-1, keepdims=True))
    centered = row_data - average
    variance = lax.optimization_barrier(jnp.mean(centered * centered, axis=-1, keepdims=True))
    return centered * lax.rsqrt(variance + epsilon) * norm_gain + norm_shift

def sequence_forward(params, row_data, seq_len):
    gain_one, shift_one, weight_qkv, query_bias, value_bias, weight_out, bias_out, gain_two, shift_two, weight_fc, bias_fc, weight_proj, bias_proj = params
    row_count = row_data.shape[0]
    model_width = row_data.shape[1]
    normed_one = low(layer_norm(row_data, gain_one, shift_one))
    joined_bias = jnp.concatenate([query_bias, jnp.zeros_like(query_bias), value_bias])
    joined = low(low_back(jnp.dot(normed_one, weight_qkv, precision=highest) + joined_bias))
    queries = joined[:, :model_width].reshape(row_count, -1, HD)
    keys_all = joined[:, model_width:2 * model_width].reshape(row_count, -1, HD)
    values_all = joined[:, 2 * model_width:].reshape(row_count, -1, HD)
    positions = jnp.arange(row_count, dtype=jnp.int32)

    def attend(row_begin):
        block_q = lax.dynamic_slice_in_dim(queries, row_begin, HALF, 0)
        scores = jnp.einsum('thd,shd->hts', block_q, keys_all, precision=highest) * HD ** (-0.5)
        scores = low_back(scores)
        query_pos = row_begin + jnp.arange(HALF, dtype=jnp.int32)
        allowed = (positions[None, :] <= query_pos[:, None]) & (positions[None, :] < seq_len)
        scores = jnp.where(allowed[None, :, :], scores, -1e+30)
        prob_rows = low(jax.nn.softmax(scores, axis=-1))
        return jnp.einsum('hts,shd->thd', prob_rows, values_all, precision=highest)
    starts = jnp.arange(row_count // HALF, dtype=jnp.int32) * HALF
    attended = lax.map(jax.checkpoint(attend), starts).reshape(row_count, model_width)
    attended = low(low_back(attended))
    hidden = row_data + low_back(jnp.dot(attended, weight_out, precision=highest) + bias_out)
    normed_two = low(layer_norm(hidden, gain_two, shift_two))
    pre_act = low_back(jnp.dot(normed_two, weight_fc, precision=highest) + bias_fc)
    activated = low(jax.nn.gelu(pre_act, approximate=True))
    mixed = hidden + low_back(jnp.dot(activated, weight_proj, precision=highest) + bias_proj)
    live_rows = (positions < seq_len)[:, None]
    return jnp.where(live_rows, mixed, 0.0)

def reference(layer_in, cotangent, lengths, dealing, ln1_gain, ln1_bias, w_qkv, q_bias, v_bias, w_out, out_bias, ln2_gain, ln2_bias, w_fc, fc_bias, w_proj, proj_bias):
    params = tuple((weight.astype(jnp.float32) for weight in (ln1_gain, ln1_bias, w_qkv, q_bias, v_bias, w_out, out_bias, ln2_gain, ln2_bias, w_fc, fc_bias, w_proj, proj_bias)))
    seq_lengths = lengths.reshape(-1).astype(jnp.int32)
    zero_grads = tuple((jnp.zeros_like(weight) for weight in params))

    def one_step(totals, inputs):
        row_data, cot_rows, seq_len = inputs

        def forward(param_list, layer_rows):
            return sequence_forward(param_list, layer_rows, seq_len)
        outputs, pullback = jax.vjp(forward, params, row_data.astype(jnp.float32))
        param_grads, row_grad = pullback(cot_rows.astype(jnp.float32))
        totals = jax.tree.map(lambda running, update: running + update, totals, param_grads)
        return (totals, (outputs.astype(jnp.bfloat16), row_grad.astype(jnp.bfloat16)))
    totals, (mixed_out, input_grad) = lax.scan(one_step, zero_grads, (layer_in, cotangent, seq_lengths))
    grouped = mixed_out.reshape(-1, GSEQ, L, D)
    picked = jnp.take_along_axis(grouped, dealing.astype(jnp.int32)[:, :, None, None], axis=1)
    layer_out = picked.reshape(-1, L, D)
    return (layer_out, input_grad, totals[0], totals[1], totals[2], totals[3], totals[4], totals[5], totals[6], totals[7], totals[8], totals[9], totals[10], totals[11], totals[12])
```

```python
import functools

import jax
import jax.numpy as jnp
from jax import lax
from jax.experimental import pallas as pl
from jax.experimental.pallas import tpu as pltpu
from jax.sharding import PartitionSpec as P

HD = 64
BQ = 256
EPS = 1e-05
BF = jnp.bfloat16
F32 = jnp.float32
NEG = -1e30
LOG2E = 1.4426950408889634
SCALE = HD**-0.5
EXPC = SCALE * LOG2E
VLIM = 62 * 1024 * 1024
GELU_A = 0.7978845608028654
GELU_B = 0.044715
MESH = pl.DeviceIdType.MESH
PIECE = 512
WINDOW = 384


def dot(a, b):
    return jnp.dot(a, b, preferred_element_type=F32)


def dot_tn(a, b):
    return lax.dot_general(a, b, (((0,), (0,)), ((), ())), preferred_element_type=F32)


def dot_nt(a, b):
    return lax.dot_general(a, b, (((1,), (1,)), ((), ())), preferred_element_type=F32)


def norm_stats(v):
    mean = jnp.mean(v, axis=-1, keepdims=True)
    cen = v - mean
    inv = lax.rsqrt(jnp.mean(cen * cen, axis=-1, keepdims=True) + EPS)
    return cen * inv, inv


def norm_back(grad, unit, inv, gain):
    e = grad * gain
    m1 = jnp.mean(e, axis=-1, keepdims=True)
    m2 = jnp.mean(e * unit, axis=-1, keepdims=True)
    return inv * (e - m1 - unit * m2)


def rows_of(i, size):
    return pl.ds(pl.multiple_of(i * size, size), size)


def lane_half(shape):
    return lax.broadcasted_iota(jnp.int32, shape, 1) < HD


def split3(v):
    hi = v.astype(BF).astype(F32)
    rest = v - hi
    mid = rest.astype(BF).astype(F32)
    return hi, mid, rest - mid


def extra(base, v, first):
    hi, mid, lo = split3(v)
    lane = lax.broadcasted_iota(jnp.int32, base.shape, 1) % HD
    out = jnp.where(lane == first, hi, base)
    out = jnp.where(lane == first + 1, mid, out)
    return jnp.where(lane == first + 2, lo, out)


def segments(meta_ref, first, rows):
    row = first + lax.broadcasted_iota(jnp.int32, (rows, 128), 0)
    seg = (row >= meta_ref[0]).astype(jnp.int32) + (row >= meta_ref[1]).astype(jnp.int32)
    lane = lax.broadcasted_iota(jnp.int32, (rows, 128), 1) % HD
    return lane, seg


def own_segment(meta_ref, first, rows):
    lane, seg = segments(meta_ref, first, rows)
    return jnp.where(lane == seg, 1.0, 0.0)


def other_segment(meta_ref, first, rows):
    lane, seg = segments(meta_ref, first, rows)
    return jnp.where((lane < 3) & (lane != seg), NEG, 0.0)


def vspecs(n):
    return [pl.BlockSpec(memory_space=pltpu.VMEM)] * n


def anyspecs(n):
    return [pl.BlockSpec(memory_space=pl.ANY)] * n


SMEM = pl.BlockSpec(memory_space=pltpu.SMEM)


def params(**kw):
    return pltpu.CompilerParams(vmem_limit_bytes=VLIM, **kw)


def cost(flops, moved, trans=0):
    return pl.CostEstimate(flops=int(flops), bytes_accessed=int(moved), transcendentals=int(trans))


G1, B1, QB, VB, OB, G2, B2, PB = range(8)


def shifted(src_ref, first, count, offset):
    total = src_ref.shape[0]
    low = jnp.clip(((first + offset) // 128) * 128, 0, total - WINDOW)
    low = pl.multiple_of(low, 128)
    want = first + offset - low + lax.broadcasted_iota(jnp.int32, (count, WINDOW), 0)
    pick = want == lax.broadcasted_iota(jnp.int32, (count, WINDOW), 1)
    return pick, src_ref[pl.ds(low, WINDOW), :]


def pack_body(meta_ref, a_ref, b_ref, c_ref, out_ref):
    i = pl.program_id(0)
    rows = out_ref.shape[0]
    acc = jnp.zeros(out_ref.shape, F32)
    for k, src in enumerate((a_ref, b_ref, c_ref)):
        start, size = meta_ref[2 + 2 * k], meta_ref[3 + 2 * k]
        pick, window = shifted(src, i * rows, rows, -start)
        row = i * rows + lax.broadcasted_iota(jnp.int32, pick.shape, 0)
        pick = pick & (row >= start) & (row < start + size)
        acc = acc + dot(jnp.where(pick, 1.0, 0.0).astype(BF), window)
    out_ref[...] = acc.astype(BF)


def pack(meta, a, b, c):
    rows, width = a.shape
    whole = pl.BlockSpec((rows, width), lambda i: (0, 0), pipeline_mode=pl.Buffered(1))
    return pl.pallas_call(
        pack_body,
        name="pack_rows",
        grid=(rows // BQ,),
        out_shape=jax.ShapeDtypeStruct((rows, width), BF),
        in_specs=[SMEM, whole, whole, whole],
        out_specs=pl.BlockSpec((BQ, width), lambda i: (i, 0)),
        compiler_params=params(),
        cost_estimate=cost(2e9, 6e6),
    )(meta, a, b, c)


def unpack_body(base, meta_ref, own_ref, other_ref, out_ref):
    j, i = pl.program_id(0), pl.program_id(1)
    rows = out_ref.shape[1]
    side, offset, size = meta_ref[base + 3 * j], meta_ref[base + 3 * j + 1], meta_ref[base + 3 * j + 2]
    for value, src in ((0, own_ref), (1, other_ref)):

        @pl.when(side == value)
        def _():
            pick, window = shifted(src, i * rows, rows, offset)
            row = i * rows + lax.broadcasted_iota(jnp.int32, pick.shape, 0)
            pick = pick & (row < size)
            out_ref[0] = dot(jnp.where(pick, 1.0, 0.0).astype(BF), window).astype(BF)


def unpack(meta, base, own, other, slots):
    rows, width = own.shape
    whole = pl.BlockSpec((rows, width), lambda j, i: (0, 0), pipeline_mode=pl.Buffered(1))
    return pl.pallas_call(
        functools.partial(unpack_body, base),
        name="unpack_rows",
        grid=(slots, rows // BQ),
        out_shape=jax.ShapeDtypeStruct((slots, rows, width), BF),
        in_specs=[SMEM, whole, whole],
        out_specs=pl.BlockSpec((1, BQ, width), lambda j, i: (j, i, 0)),
        compiler_params=params(),
        cost_estimate=cost(2e9, 6e6),
    )(meta, own, other)


def layer_norm_rows(src_ref, vecs_ref, gain_row, dst_ref):
    rows = src_ref.shape[0]
    gain, shift = vecs_ref[gain_row : gain_row + 1, :], vecs_ref[gain_row + 1 : gain_row + 2, :]

    @pl.loop(0, rows // BQ)
    def _(i):
        r = rows_of(i, BQ)
        unit, _inv = norm_stats(src_ref[r, :].astype(F32))
        dst_ref[r, :] = (unit * gain + shift).astype(BF)


def stage_a_body(meta_ref, x_ref, vecs_ref, wqkv_ref, wout_ref, joined_ref, att_ref, ext_ref, hid_ref, n1_ref):
    rows, width = x_ref.shape
    nb = rows // BQ
    layer_norm_rows(x_ref, vecs_ref, G1, n1_ref)
    for b, row in ((0, QB), (1, None), (2, VB)):

        @pl.loop(0, width // 256)
        def _(j):
            c = pl.ds(pl.multiple_of(b * width + j * 256, 256), 256)
            value = dot(n1_ref[...], wqkv_ref[:, c])
            if row is not None:
                value = value + vecs_ref[row : row + 1, rows_of(j, 256)]
            joined_ref[:, c] = value.astype(BF)

    @pl.loop(0, width // 128)
    def _(h):
        cq = pl.ds(pl.multiple_of(h * 128, 128), 128)
        ck = pl.ds(pl.multiple_of(width + h * 128, 128), 128)
        cv = pl.ds(pl.multiple_of(2 * width + h * 128, 128), 128)
        left = lane_half((rows, 128))
        k2 = joined_ref[:, ck]
        v2 = joined_ref[:, cv]
        neg = other_segment(meta_ref, 0, rows).astype(BF)
        one = jnp.ones_like(v2)
        ks = [jnp.where(left, k2, neg), jnp.where(left, neg, k2)]
        vs = [jnp.where(left, v2, one), jnp.where(left, one, v2)]
        tri = lax.broadcasted_iota(jnp.int32, (BQ, BQ), 1) <= lax.broadcasted_iota(jnp.int32, (BQ, BQ), 0)
        lq = lane_half((BQ, 128))
        for i in range(nb):
            n = (i + 1) * BQ
            r = slice(i * BQ, n)
            q2 = joined_ref[r, cq]
            ohf = own_segment(meta_ref, i * BQ, BQ)
            oh = ohf.astype(BF)
            qs = [jnp.where(lq, q2, oh), jnp.where(lq, oh, q2)]
            outs, exts = [], []
            for e in range(2):
                sd = jnp.where(tri, dot_nt(qs[e], ks[e][n - BQ : n]), NEG)
                peak = jnp.max(sd, axis=1, keepdims=True)
                if i:
                    so = dot_nt(qs[e], ks[e][: n - BQ])
                    peak = jnp.maximum(peak, jnp.max(so, axis=1, keepdims=True))
                    po = jnp.exp2((so - peak) * EXPC).astype(BF)
                pd = jnp.exp2((sd - peak) * EXPC).astype(BF)
                acc = dot(pd, vs[e][n - BQ : n])
                if i:
                    acc = acc + dot(po, vs[e][: n - BQ])
                outs.append(acc)
                tot = acc[:, HD : HD + 1] if e == 0 else acc[:, 0:1]
                exts.append(extra(ohf, -(peak + jnp.log(tot) * (1.0 / SCALE)), 3))
            num = jnp.where(lq, outs[0], outs[1])
            den = pltpu.roll(jnp.where(lq, outs[1], outs[0]), HD, 1)
            att_ref[r, cq] = (num / den).astype(BF)
            ext_ref[r, cq] = jnp.where(lq, exts[1], exts[0]).astype(BF)

    bias = vecs_ref[OB : OB + 1, :]

    @pl.loop(0, nb)
    def _(i):
        r = rows_of(i, BQ)
        hid_ref[r, :] = x_ref[r, :].astype(F32) + (dot(att_ref[r, :], wout_ref[...]) + bias)


def stage_a(meta, x, vecs, wqkv, wout):
    rows, width = x.shape
    s = jax.ShapeDtypeStruct
    return pl.pallas_call(
        stage_a_body,
        name="stage_a",
        out_shape=(s((rows, 3 * width), BF), s((rows, width), BF), s((rows, width), BF), s((rows, width), F32)),
        in_specs=[SMEM] + vspecs(4),
        out_specs=tuple(vspecs(4)),
        scratch_shapes=[pltpu.VMEM((rows, width), BF)],
        compiler_params=params(),
        cost_estimate=cost(30e9, 16e6, 8e6),
    )(meta, x, vecs, wqkv, wout)


def gelu_both(v):
    v2 = v * v
    t = jnp.tanh(v * (GELU_A + (GELU_A * GELU_B) * v2))
    half = 0.5 + 0.5 * t
    return v * half, half + (0.5 * v) * (1.0 - t * t) * (GELU_A + (3.0 * GELU_A * GELU_B) * v2)


def quarter(dst_ref, row0, value):
    hr, hc = value.shape[0] // 2, value.shape[1] // 2
    for h in range(2):
        for c in range(2):
            dst_ref[h, c, pl.ds(row0, hr), :] = value[h * hr : (h + 1) * hr, c * hc : (c + 1) * hc]


def stage_b_body(
    hid_ref, cot_ref, att_ref, vecs_ref, bfc_ref, wfc_ref, wproj_ref, wout_ref,
    out_ref, gfc_ref, gproj_ref, gout_ref, gatt_ref, ghid_ref, small_ref, gbfc_ref,
    wf_ref, wp_ref, fbuf_ref, pbuf_ref, n2_ref, act_ref, gpre_ref, oacc_ref, nacc_ref, wsem, gsem,
):
    rows, width = hid_ref.shape
    nb = rows // BQ
    hw = width // 2
    nj = wf_ref.shape[0]
    gain, shift = vecs_ref[G2 : G2 + 1, :], vecs_ref[B2 : B2 + 1, :]

    def loads(j):
        for part in range(2):
            here = pl.ds((part * nj + j) * hw, hw)
            yield pltpu.make_async_copy(wfc_ref.at[:, here], wf_ref.at[j, :, pl.ds(part * hw, hw)], wsem.at[0, part, j])
            yield pltpu.make_async_copy(wproj_ref.at[here, :], wp_ref.at[j, pl.ds(part * hw, hw), :], wsem.at[1, part, j])

    def stores(j):
        here = pl.ds(j * hw, hw)
        yield pltpu.make_async_copy(fbuf_ref.at[j], gfc_ref.at[:, :, here, :], gsem.at[0, j])
        yield pltpu.make_async_copy(pbuf_ref.at[j], gproj_ref.at[:, :, here, :], gsem.at[1, j])

    for j in range(nj):
        for copy in loads(j):
            copy.start()

    @pl.loop(0, nb)
    def _(i):
        r = rows_of(i, BQ)
        hid = hid_ref[r, :]
        unit, _inv = norm_stats(hid)
        n2_ref[r, :] = (unit * gain + shift).astype(BF)
        oacc_ref[r, :] = hid + vecs_ref[PB : PB + 1, :]
        nacc_ref[r, :] = jnp.zeros((BQ, width), F32)

    gbfc_ref[...] = jnp.zeros_like(gbfc_ref)
    for j in range(nj):
        for copy in loads(j):
            copy.wait()

        @pl.loop(0, nb)
        def _(i):
            r = rows_of(i, BQ)
            pre = dot(n2_ref[r, :], wf_ref[j]) + bfc_ref[j : j + 1, :]
            act, der = gelu_both(pre)
            act = act.astype(BF)
            act_ref[r, :] = act
            gact = dot_nt(cot_ref[r, :], wp_ref[j])
            gpre = (gact * der).astype(BF)
            gpre_ref[r, :] = gpre
            gbfc_ref[j : j + 1, :] += jnp.sum(gpre.astype(F32), axis=0, keepdims=True)
            oacc_ref[r, :] += dot(act, wp_ref[j])
            nacc_ref[r, :] += dot_nt(gpre, wf_ref[j])

        for h in range(2):
            gp = dot_tn(act_ref[:, h * hw : (h + 1) * hw], cot_ref[...]).astype(BF)
            gf = dot_tn(n2_ref[:, h * hw : (h + 1) * hw], gpre_ref[...]).astype(BF)
            for c in range(2):
                pbuf_ref[j, h, c] = gp[:, c * hw : (c + 1) * hw]
                fbuf_ref[j, h, c] = gf[:, c * hw : (c + 1) * hw]
        for copy in stores(j):
            copy.start()

    small_ref[...] = jnp.zeros_like(small_ref)

    @pl.loop(0, nb)
    def _(i):
        r = rows_of(i, BQ)
        out_ref[r, :] = oacc_ref[r, :].astype(BF)
        unit, inv = norm_stats(hid_ref[r, :])
        gn2 = nacc_ref[r, :]
        gy = cot_ref[r, :].astype(F32)
        ghid = gy + norm_back(gn2, unit, inv, gain)
        ghid_ref[r, :] = ghid
        low = ghid.astype(BF)
        n2_ref[r, :] = low
        gatt_ref[r, :] = dot_nt(low, wout_ref[...]).astype(BF)
        small_ref[0:1, :] += jnp.sum(gn2 * unit, axis=0, keepdims=True)
        small_ref[1:2, :] += jnp.sum(gn2, axis=0, keepdims=True)
        small_ref[2:3, :] += jnp.sum(gy, axis=0, keepdims=True)
        small_ref[3:4, :] += jnp.sum(low.astype(F32), axis=0, keepdims=True)

    for h in range(2):
        go = dot_tn(att_ref[:, h * hw : (h + 1) * hw], n2_ref[...]).astype(BF)
        for c in range(2):
            gout_ref[h, c] = go[:, c * hw : (c + 1) * hw]
    for j in range(nj):
        for copy in stores(j):
            copy.wait()


def stage_b(hid, cot, att, vecs, bfc, wfc, wproj, wout):
    rows, width = hid.shape
    ff = wfc.shape[1]
    hw = width // 2
    nj = ff // width
    s = jax.ShapeDtypeStruct
    v = pltpu.VMEM
    return pl.pallas_call(
        stage_b_body,
        name="stage_b",
        out_shape=(
            s((rows, width), BF), s((2, 2, nj * hw, hw), BF), s((2, 2, nj * hw, hw), BF), s((2, 2, hw, hw), BF),
            s((rows, width), BF), s((rows, width), F32), s((8, width), F32), s((nj, width), F32),
        ),
        in_specs=vspecs(5) + anyspecs(2) + vspecs(1),
        out_specs=tuple(vspecs(1) + anyspecs(2) + vspecs(5)),
        scratch_shapes=[
            v((nj, width, width), BF), v((nj, width, width), BF), v((nj, 2, 2, hw, hw), BF), v((nj, 2, 2, hw, hw), BF),
            v((rows, width), BF), v((rows, width), BF), v((rows, width), BF), v((rows, width), F32), v((rows, width), F32),
            pltpu.SemaphoreType.DMA((2, 2, nj)), pltpu.SemaphoreType.DMA((2, nj)),
        ],
        compiler_params=params(),
        cost_estimate=cost(40e9, 45e6, 3e6),
    )(hid, cot, att, vecs, bfc, wfc, wproj, wout)


def attention_back(meta_ref, joined_ref, cols, ext_ref, att_ref, gatt_ref, dst_ref, dk_ref, dv_ref):
    cq, ck, cv = cols
    rows = joined_ref.shape[0]
    nb = rows // BQ
    left = lane_half((rows, 128))
    lane = lax.broadcasted_iota(jnp.int32, (rows, 128), 1) % HD
    k2 = joined_ref[:, ck]
    v2 = joined_ref[:, cv]
    zero = jnp.zeros_like(k2)
    ones = (lane >= 3) & (lane < 6)
    kx = jnp.where(ones, 1.0, other_segment(meta_ref, 0, rows)).astype(BF)
    vx = jnp.where(ones, 1.0, 0.0).astype(BF)
    ks = [jnp.where(left, k2, kx), jnp.where(left, kx, k2)]
    vs = [jnp.where(left, v2, vx), jnp.where(left, vx, v2)]
    km = [jnp.where(left, k2, zero), jnp.where(left, zero, k2)]
    dk_ref[...] = jnp.zeros_like(dk_ref)
    dv_ref[...] = jnp.zeros_like(dv_ref)
    lq = lane_half((BQ, 128))
    tri = lax.broadcasted_iota(jnp.int32, (BQ, BQ), 0) <= lax.broadcasted_iota(jnp.int32, (BQ, BQ), 1)
    for i in range(nb):
        r = slice(i * BQ, (i + 1) * BQ)
        q2 = joined_ref[r, cq]
        g2 = gatt_ref[r, cq]
        ext = ext_ref[r, cq]
        zq = jnp.zeros_like(q2)
        prod = g2.astype(F32) * att_ref[r, cq].astype(F32)
        d0 = jnp.sum(jnp.where(lq, prod, 0.0), axis=1, keepdims=True)
        d1 = jnp.sum(jnp.where(lq, 0.0, prod), axis=1, keepdims=True)
        zf = jnp.zeros((BQ, 128), F32)
        qs = [jnp.where(lq, q2, ext), jnp.where(lq, ext, q2)]
        gs = [jnp.where(lq, g2, extra(zf, -d0, 3).astype(BF)), jnp.where(lq, extra(zf, -d1, 3).astype(BF), g2)]
        qm = [jnp.where(lq, q2, zq), jnp.where(lq, zq, q2)]
        gm = [jnp.where(lq, g2, zq), jnp.where(lq, zq, g2)]
        dq = None
        for u in range(i + 1):
            b = slice(u * BQ, (u + 1) * BQ)
            dk = dv = None
            for e in range(2):
                st = dot_nt(ks[e][b], qs[e])
                if u == i:
                    st = jnp.where(tri, st, NEG)
                pt = jnp.exp2(st * EXPC)
                dst = (pt * dot_nt(vs[e][b], gs[e])).astype(BF)
                one, two, three = dot(pt.astype(BF), gm[e]), dot(dst, qm[e]), dot_tn(dst, km[e][b])
                dv = one if dv is None else dv + one
                dk = two if dk is None else dk + two
                dq = three if dq is None else dq + three
            dv_ref[b, :] += dv
            dk_ref[b, :] += dk
        dst_ref[r, cq] = (dq * SCALE).astype(BF)
    dst_ref[:, ck] = (dk_ref[...] * SCALE).astype(BF)
    dst_ref[:, cv] = dv_ref[...].astype(BF)


def stage_c_body(
    meta_ref, x_ref, joined_ref, ext_ref, att_ref, gatt_ref, ghid_ref, vecs_ref, wqkv_ref, gout_ref,
    dx_ref, gqkvo_ref, small_ref, n1_ref, dj_ref, dk_ref, dv_ref,
):
    rows, width = x_ref.shape
    hw = width // 2
    nb = rows // BQ
    gain = vecs_ref[G1 : G1 + 1, :]
    small_ref[...] = jnp.zeros_like(small_ref)
    layer_norm_rows(x_ref, vecs_ref, G1, n1_ref)

    @pl.loop(0, width // 128)
    def _(h):
        cols = [pl.ds(pl.multiple_of(b * width + h * 128, 128), 128) for b in range(3)]
        attention_back(meta_ref, joined_ref, cols, ext_ref, att_ref, gatt_ref, dj_ref, dk_ref, dv_ref)

    for b in range(3):
        here = dj_ref[:, b * width : (b + 1) * width]
        small_ref[b : b + 1, :] = jnp.sum(here.astype(F32), axis=0, keepdims=True)
        for h in range(2):
            gw = dot_tn(n1_ref[:, h * hw : (h + 1) * hw], here).astype(BF)
            for c in range(2):
                gqkvo_ref[h, c, b * hw : (b + 1) * hw, :] = gw[:, c * hw : (c + 1) * hw]
    gqkvo_ref[:, :, 3 * hw :, :] = gout_ref[...]

    @pl.loop(0, nb)
    def _(i):
        r = rows_of(i, BQ)
        gn1 = dot_nt(dj_ref[r, :], wqkv_ref[...])
        unit, inv = norm_stats(x_ref[r, :].astype(F32))
        dx_ref[r, :] = (ghid_ref[r, :] + norm_back(gn1, unit, inv, gain)).astype(BF)
        small_ref[3:4, :] += jnp.sum(gn1 * unit, axis=0, keepdims=True)
        small_ref[4:5, :] += jnp.sum(gn1, axis=0, keepdims=True)


def stage_c(meta, x, joined, ext, att, gatt, ghid, vecs, wqkv, gout):
    rows, width = x.shape
    hw = width // 2
    s = jax.ShapeDtypeStruct
    v = pltpu.VMEM
    return pl.pallas_call(
        stage_c_body,
        name="stage_c",
        out_shape=(s((rows, width), BF), s((2, 2, 4 * hw, hw), BF), s((8, width), F32)),
        in_specs=[SMEM] + vspecs(9),
        out_specs=tuple(vspecs(3)),
        scratch_shapes=[v((rows, width), BF), v((rows, 3 * width), BF), v((rows, 128), F32), v((rows, 128), F32)],
        compiler_params=params(),
        cost_estimate=cost(50e9, 22e6, 8e6),
    )(meta, x, joined, ext, att, gatt, ghid, vecs, wqkv, gout)


def place():
    return lax.axis_index("rep"), lax.axis_index("shard")


def greet(partners):
    barrier = pltpu.get_barrier_semaphore()
    for partner in partners:
        pl.semaphore_signal(barrier, inc=1, device_id=partner, device_id_type=MESH)
    pl.semaphore_wait(barrier, len(partners))


def remote(src, dst, ssem, rsem, to):
    return pltpu.make_async_remote_copy(
        src_ref=src, dst_ref=dst, send_sem=ssem, recv_sem=rsem, device_id=to, device_id_type=MESH
    )


def fetch_body(x_ref, small_ref, wq_ref, wo_ref, wf_ref, wp_ref, xr_ref, sr_ref, q_ref, o_ref, f_ref, p_ref, xs, ws, wr, ls):
    rep, shard = place()
    across, core, side = (rep, 1 - shard), (rep ^ 1, shard), (rep ^ 2, shard)
    greet((across, core, side))
    mine = rep & 3
    pairs = ((wq_ref, q_ref), (wo_ref, o_ref), (wf_ref, f_ref), (wp_ref, p_ref))

    def part(ref, index):
        size = ref.shape[0] // 4
        return ref.at[pl.ds(pl.multiple_of(index * size, 16), size), :]

    def direct(n):
        src, dst = pairs[n]
        return remote(part(src, mine), part(dst.at[shard], mine), ws.at[n, 0], wr.at[n, 0], across)

    def forward(n, step):
        dst = pairs[n][1].at[1 - shard]
        if step == 1:
            return remote(part(dst, mine), part(dst, mine), ws.at[n, 1], wr.at[n, 1], core)
        if step == 2:
            return remote(part(dst, mine), part(dst, mine), ws.at[n, 2], wr.at[n, 2], side)
        return remote(part(dst, mine ^ 2), part(dst, mine ^ 2), ws.at[n, 3], wr.at[n, 3], core)

    keep = [pltpu.make_async_copy(src, dst.at[shard], ls.at[n]) for n, (src, dst) in enumerate(pairs)]
    keep.append(pltpu.make_async_copy(small_ref, sr_ref.at[shard], ls.at[4]))
    small = remote(small_ref, sr_ref.at[shard], xs.at[0], xs.at[1], across)
    rows = remote(x_ref, xr_ref, xs.at[2], xs.at[3], across)
    small.start()
    direct(0).start()
    rows.start()
    for n in range(1, 4):
        direct(n).start()
    for copy in keep:
        copy.start()
    for n in range(4):
        direct(n).wait_recv()
        forward(n, 1).start()
        forward(n, 2).start()
        if n:
            forward(n - 1, 2).wait_recv()
            forward(n - 1, 3).start()
    forward(3, 2).wait_recv()
    forward(3, 3).start()
    for n in range(4):
        direct(n).wait_send()
        forward(n, 1).wait()
        forward(n, 2).wait_send()
        forward(n, 3).wait()
    small.wait()
    rows.wait()
    for copy in keep:
        copy.wait()


def fetch(x, small, wq, wo, wf, wp):
    s = jax.ShapeDtypeStruct
    dma = pltpu.SemaphoreType.DMA
    both = lambda a: s((2,) + a.shape, a.dtype)
    return pl.pallas_call(
        fetch_body,
        name="fetch",
        out_shape=(s(x.shape, x.dtype), both(small), both(wq), both(wo), both(wf), both(wp)),
        in_specs=anyspecs(1) + vspecs(5),
        out_specs=tuple(anyspecs(6)),
        scratch_shapes=[dma((4,)), dma((4, 4)), dma((4, 4)), dma((5,))],
        compiler_params=params(collective_id=0, has_side_effects=True),
        cost_estimate=cost(1e6, 60e6),
    )(x, small, wq, wo, wf, wp)


def reduce_body(
    bits, gf_ref, gp_ref, gq_ref, sm_ref, dx_ref, res_ref, smo_ref, dxr_ref,
    loc_ref, r0_ref, r1_ref, rb_ref, smb_ref, smr_ref, lsem, ssem, rsem, msem, mrem, xsem,
):
    rep, shard = place()
    core = rep & 1
    sibling, across = (rep ^ 1, shard), (rep, 1 - shard)
    peers = [(rep ^ (1 << t), shard) for t in range(1, bits)]
    greet([sibling, across] + peers)
    m = len(peers)
    arrays = (gf_ref, gp_ref, gq_ref)
    per = gf_ref.shape[2] // PIECE
    count = per * len(arrays)
    last = 3 + 2 * m

    def source(k, side):
        return arrays[k // per].at[:, side, pl.ds((k % per) * PIECE, PIECE), :]

    def span(t):
        first, size = 0, PIECE
        for n in range(t):
            size //= 2
            first = first + ((rep >> (n + 1)) & 1) * size
        return first, size

    def rows(ref, first, size):
        return ref.at[pl.ds(pl.multiple_of(first, 16), size), :]

    def copy(k, step):
        sems = (ssem.at[step, k], rsem.at[step, k])
        if step == 0:
            return remote(source(k, 1 - core), r0_ref.at[k], *sems, sibling)
        if step == 1:
            return remote(loc_ref.at[k, 1 - shard], r1_ref.at[k], *sems, across)
        if step < 2 + m:
            t = step - 2
            first, size = span(t)
            half = size // 2
            away = first + (1 - ((rep >> (t + 1)) & 1)) * half
            return remote(rows(loc_ref.at[k, shard], away, half), rb_ref.at[t, k, pl.ds(0, half), :], *sems, peers[t])
        if step < 2 + 2 * m:
            t = m - 1 - (step - 2 - m)
            first, size = span(t + 1)
            return remote(rows(res_ref.at[core, k], first, size), rows(res_ref.at[core, k], first, size), *sems, peers[t])
        return remote(res_ref.at[core, k], res_ref.at[core, k], *sems, sibling)

    def local(k):
        return pltpu.make_async_copy(source(k, core), loc_ref.at[k], lsem.at[k])

    def add(dst, first, other, size, out=None):
        chunk = min(size, 64)

        @pl.loop(0, size // chunk)
        def _(i):
            at = pl.ds(pl.multiple_of(first + i * chunk, 16), chunk)
            total = dst[at, :].astype(F32) + other[rows_of(i, chunk), :].astype(F32)
            (dst if out is None else out)[at, :] = total.astype(BF)

    def act(k, step):
        if step == 0:
            copy(k, 0).start()
            local(k).start()
            return
        copy(k, step - 1).wait_recv()
        if step == 1:
            local(k).wait()
            for h in range(2):
                add(loc_ref.at[k, h], 0, r0_ref.at[k, h], PIECE)
        elif step == 2:
            add(loc_ref.at[k, shard], 0, r1_ref.at[k], PIECE)
        elif step < 3 + m:
            t = step - 3
            first, size = span(t + 1)
            final = res_ref.at[core, k] if t == m - 1 else None
            add(loc_ref.at[k, shard], first, rb_ref.at[t, k], size, final)
        if step < last:
            copy(k, step).start()

    def small_copy(step):
        to = ([sibling, across] + peers)[step]
        src = sm_ref if step == 0 else smb_ref.at[step - 1]
        return remote(src, smr_ref.at[step], msem.at[step], mrem.at[step], to)

    def small(step):
        if step:
            small_copy(step - 1).wait_recv()
            before = sm_ref[...] if step == 1 else smb_ref[step - 2]
            total = before + smr_ref[step - 1]
            if step == 2 + m:
                smo_ref[...] = total
            else:
                smb_ref[step - 1] = total
        if step < 2 + m:
            small_copy(step).start()

    dxc = remote(dx_ref, dxr_ref, xsem.at[0], xsem.at[1], across)
    for k in range(count):
        act(k, 0)
    for tick in range(1, count + last):
        for step in range(1, last + 1):
            k = tick - step
            if 0 <= k < count:
                act(k, step)
                if k == count - 1 and step == 1:
                    dxc.start()
        if tick <= 3 + m:
            small(tick - 1)
    for k in range(count):
        for step in range(last):
            copy(k, step).wait_send()
    for step in range(2 + m):
        small_copy(step).wait_send()
    dxc.wait()


def reduce(bits, gf, gp, gq, sm, dx):
    hw = gf.shape[3]
    count = 3 * (gf.shape[2] // PIECE)
    m = bits - 1
    s = jax.ShapeDtypeStruct
    v = pltpu.VMEM
    dma = pltpu.SemaphoreType.DMA
    return pl.pallas_call(
        functools.partial(reduce_body, bits),
        name="reduce",
        out_shape=(s((2, count, PIECE, hw), BF), s(sm.shape, F32), s(dx.shape, BF)),
        in_specs=anyspecs(3) + vspecs(1) + anyspecs(1),
        out_specs=tuple(vspecs(2) + anyspecs(1)),
        scratch_shapes=[
            v((count, 2, PIECE, hw), BF), v((count, 2, PIECE, hw), BF), v((count, PIECE, hw), BF),
            v((m, count, PIECE // 2, hw), BF), v((m + 1,) + sm.shape, F32), v((m + 2,) + sm.shape, F32),
            dma((count,)), dma((3 + 2 * m, count)), dma((3 + 2 * m, count)), dma((m + 2,)), dma((m + 2,)), dma((2,)),
        ],
        compiler_params=params(collective_id=1, has_side_effects=True),
        cost_estimate=cost(1e6, 60e6),
    )(gf, gp, gq, sm, dx)


def describe(lens, deal, shard, rows):
    group = lens.shape[0]
    half = group // 2
    ids = jnp.arange(group, dtype=jnp.int32)
    long = jnp.sum(jnp.where(lens == rows, ids, 0))
    home = long // half
    stays = shard == home
    moved = long ^ 1
    first = half * (1 - home)
    size = lambda q: jnp.sum(jnp.where(ids == q, lens, 0))
    s0, s1 = size(first), size(first + 1)
    sm = size(moved)
    mark = lambda a, b: jnp.where(stays, a, b)
    slot = long & 1
    out = [mark(rows, s0), mark(rows, s0 + s1)]
    out += [0, mark(jnp.where(slot == 0, rows, 0), s0)]
    out += [mark(0, s0), mark(jnp.where(slot == 1, rows, 0), s1)]
    out += [mark(0, s0 + s1), mark(0, sm)]

    def where(q):
        start = jnp.where(q == first, 0, jnp.where(q == first + 1, s0, s0 + s1))
        side = jnp.where(q == long, home, 1 - home) != shard
        return [side.astype(jnp.int32), jnp.where(q == long, 0, start), size(q)]

    for j in range(half):
        out += where(jnp.sum(jnp.where(ids == half * shard + j, deal, 0)))
    for j in range(half):
        out += where(half * shard + j)
    return jnp.stack([jnp.asarray(v, jnp.int32) for v in out]), jnp.where(stays, 1 - slot, 0)


def local(bits, layer_in, cotangent, lengths, dealing, g1, b1, wqkv, qb, vb, wout, ob, g2, b2, wfc, bfc, wproj, pb):
    shard = lax.axis_index("shard")
    slots, rows, width = layer_in.shape
    hw = width // 2
    meta, slot = describe(lengths[0], dealing[0], shard, rows)
    pick = lambda a: lax.dynamic_index_in_dim(a, slot, 0, keepdims=False)
    x_away, c_away = pick(layer_in), pick(cotangent)
    swap = [(0, 1), (1, 0)]
    nj = bfc.shape[0] // hw
    small = jnp.concatenate([jnp.stack([g1, b1, qb, vb, ob, g2, b2, pb]), bfc.reshape(nj, hw)])
    small = jnp.pad(small, ((0, 16 - small.shape[0]), (0, 0)))
    c_in = lax.ppermute(c_away, "shard", swap)
    x_in, smalls, wq, wo, wf, wp = fetch(x_away, small, wqkv, wout, wfc, wproj)
    wq, wo, wf, wp = (w.reshape(2 * w.shape[1], w.shape[2]) for w in (wq, wo, wf, wp))
    smalls = smalls.astype(F32).transpose(1, 0, 2).reshape(16, width)
    vecs, bias = smalls[:8], smalls[8 : 8 + nj]
    x = pack(meta, layer_in[0], layer_in[1], x_in)
    joined, att, ext, hid = stage_a(meta, x, vecs, wq, wo)
    cot = pack(meta, cotangent[0], cotangent[1], c_in)
    out, gf, gp, go, gatt, ghid, sb, gbfc = stage_b(hid, cot, att, vecs, bias, wf, wp, wo)
    out_in = lax.ppermute(out, "shard", swap)
    dx, gq, sc = stage_c(meta, x, joined, ext, att, gatt, ghid, vecs, wq, go)
    sums = jnp.concatenate([sb, sc, gbfc, jnp.zeros((8 - nj % 8, width), F32)])
    layer_out = unpack(meta, 8, out, out_in, slots)
    res, sums, dx_in = reduce(bits, gf, gp, gq, sums, dx)
    input_grad = unpack(meta, 8 + 3 * slots, dx, dx_in, slots)
    res = res.reshape(2, 3, 4, hw, hw).astype(F32)
    fc = res[:, 0].transpose(2, 0, 1, 3).reshape(hw, 2 * nj * hw)
    proj = res[:, 1].transpose(1, 2, 0, 3).reshape(nj * hw, width)
    qkv = res[:, 2, :3].transpose(2, 1, 0, 3).reshape(hw, 3 * width)
    wo_g = res[:, 2, 3].transpose(1, 0, 2).reshape(hw, width)
    own = lambda v: lax.dynamic_slice_in_dim(v, shard * hw, hw)
    fb = lax.dynamic_slice_in_dim(sums[16 : 16 + nj].reshape(nj, 2, hw), shard, 1, axis=1).reshape(nj * hw)
    return (
        layer_out, input_grad, own(sums[11]), own(sums[12]), qkv, own(sums[8]), own(sums[10]), wo_g, own(sums[3]),
        own(sums[0]), own(sums[1]), fc, fb, proj, own(sums[2]),
    )


def solution(mesh):
    both, one = P(("rep", "shard"), None, None), P("shard")
    mat = P("shard", None)
    in_specs = (both, both, P("rep", None), P("rep", None), one, one, mat, one, one, mat, one, one, one, mat, one, mat, one)
    out_specs = (both, both, one, one, mat, one, one, mat, one, one, one, mat, one, mat, one)
    bits = mesh.shape["rep"].bit_length() - 1
    return jax.shard_map(functools.partial(local, bits), mesh=mesh, in_specs=in_specs, out_specs=out_specs, check_vma=False)
```

```python
import functools

import jax
import jax.numpy as jnp
from jax import lax
from jax.experimental import pallas as pl
from jax.experimental.pallas import tpu as pltpu
from jax.sharding import PartitionSpec as P

HD = 64
BQ = 256
EPS = 1e-05
BF = jnp.bfloat16
F32 = jnp.float32
NEG = -1e30
LOG2E = 1.4426950408889634
SCALE = HD**-0.5
EXPC = SCALE * LOG2E
VLIM = 66_900_000
GELU_A = 0.7978845608028654
GELU_B = 0.044715
MESH = pl.DeviceIdType.MESH
PIECE = 512
WINDOW = 384
G1, B1, QB, VB, OB, G2, B2, PB, FB = range(9)


def dot(a, b):
    return jnp.dot(a, b, preferred_element_type=F32)


def dot_tn(a, b):
    return lax.dot_general(a, b, (((0,), (0,)), ((), ())), preferred_element_type=F32)


def dot_nt(a, b):
    return lax.dot_general(a, b, (((1,), (1,)), ((), ())), preferred_element_type=F32)


def norm_stats(v):
    mean = jnp.mean(v, axis=-1, keepdims=True)
    cen = v - mean
    inv = lax.rsqrt(jnp.mean(cen * cen, axis=-1, keepdims=True) + EPS)
    return cen * inv, inv


def norm_back(grad, unit, inv, gain):
    e = grad * gain
    m1 = jnp.mean(e, axis=-1, keepdims=True)
    m2 = jnp.mean(e * unit, axis=-1, keepdims=True)
    return inv * (e - m1 - unit * m2)


def rows_of(i, size):
    return pl.ds(pl.multiple_of(i * size, size), size)


def lane_half(shape):
    return lax.broadcasted_iota(jnp.int32, shape, 1) < HD


def extra(base, v, first):
    hi = v.astype(BF).astype(F32)
    mid = (v - hi).astype(BF).astype(F32)
    lane = lax.broadcasted_iota(jnp.int32, base.shape, 1) % HD
    out = jnp.where(lane == first, hi, base)
    out = jnp.where(lane == first + 1, mid, out)
    return jnp.where(lane == first + 2, v - hi - mid, out)


def vspecs(n):
    return [pl.BlockSpec(memory_space=pltpu.VMEM)] * n


def anyspecs(n):
    return [pl.BlockSpec(memory_space=pl.ANY)] * n


SMEM = pl.BlockSpec(memory_space=pltpu.SMEM)
DMA = pltpu.SemaphoreType.DMA


def params(**kw):
    return pltpu.CompilerParams(vmem_limit_bytes=VLIM, **kw)


def cost(flops, moved, trans=0):
    return pl.CostEstimate(flops=int(flops), bytes_accessed=int(moved), transcendentals=int(trans))


class Plan:
    def __init__(self, lens_ref, shard, rows):
        group = lens_ref.shape[1]
        half = group // 2
        self.half, self.shard, self.rows = half, shard, rows
        self.lens = [lens_ref[0, q] for q in range(group)]
        long = jnp.int32(0)
        for q in range(1, group):
            long = jnp.where(self.lens[q] == rows, q, long)
        self.long = long
        self.home = lax.div(long, jnp.int32(half))
        self.stays = shard == self.home
        self.slot = long & 1
        self.first = half * (1 - self.home)
        self.s0, self.s1 = self.size(self.first), self.size(self.first + 1)
        self.moved = self.size(long ^ 1)

    def size(self, q):
        out = self.lens[0]
        for n in range(1, len(self.lens)):
            out = jnp.where(q == n, self.lens[n], out)
        return out

    def away(self):
        return jnp.where(self.stays, 1 - self.slot, 0)

    def bounds(self):
        return jnp.where(self.stays, self.rows, self.s0), jnp.where(self.stays, self.rows, self.s0 + self.s1)

    def where(self, q):
        start = jnp.where(q == self.first, 0, jnp.where(q == self.first + 1, self.s0, self.s0 + self.s1))
        start = jnp.where(q == self.long, 0, start)
        side = jnp.where(q == self.long, self.home, 1 - self.home) ^ self.shard
        return side, start, self.size(q)


def window_pick(total, first, count):
    low = jnp.clip((first >> 7) << 7, 0, total - WINDOW)
    want = first - low + lax.broadcasted_iota(jnp.int32, (count, WINDOW), 0)
    return pl.multiple_of(low, 128), want == lax.broadcasted_iota(jnp.int32, (count, WINDOW), 1)


def moved_pick(start, i):
    shape = (BQ, (i + 1) * BQ)
    want = i * BQ - start + lax.broadcasted_iota(jnp.int32, shape, 0)
    return jnp.where(want == lax.broadcasted_iota(jnp.int32, shape, 1), 1.0, 0.0).astype(BF)


def lane_and_segment(bounds, first, rows):
    row = first + lax.broadcasted_iota(jnp.int32, (rows, 128), 0)
    seg = (row >= bounds[0]).astype(jnp.int32) + (row >= bounds[1]).astype(jnp.int32)
    return lax.broadcasted_iota(jnp.int32, (rows, 128), 1) % HD, seg


def own_segment(bounds, first, rows):
    lane, seg = lane_and_segment(bounds, first, rows)
    return jnp.where(lane == seg, 1.0, 0.0)


def other_segment(bounds, first, rows):
    lane, seg = lane_and_segment(bounds, first, rows)
    return jnp.where((lane < 3) & (lane != seg), NEG, 0.0)


def gelu_both(v):
    v2 = v * v
    t = jnp.tanh(v * (GELU_A + (GELU_A * GELU_B) * v2))
    half = 0.5 + 0.5 * t
    return v * half, half + (0.5 * v) * (1.0 - t * t) * (GELU_A + (3.0 * GELU_A * GELU_B) * v2)


def place():
    return lax.axis_index("rep"), lax.axis_index("shard")


def greet(partners):
    barrier = pltpu.get_barrier_semaphore()
    for partner in partners:
        pl.semaphore_signal(barrier, inc=1, device_id=partner, device_id_type=MESH)
    pl.semaphore_wait(barrier, len(partners))


def remote(src, dst, ssem, rsem, to):
    return pltpu.make_async_remote_copy(
        src_ref=src, dst_ref=dst, send_sem=ssem, recv_sem=rsem, device_id=to, device_id_type=MESH
    )


def front_body(
    lens_ref, xin_ref, cin_ref, small_ref, wq_in, wo_in, wf_in, wp_in,
    x_out, joined_out, att_out, ext_out, hid_out, n2_out, act_out, der_out, out_out, cot_out, wq_out, wo_out, wf_out, wp_out, vecs_ref,
    wq_ref, wo_ref, wf_ref, wp_ref, xo_ref, xs_ref, xr_ref, co_ref, cs_ref, cr_ref, x_ref, cot_ref, sm_ref,
    jn_ref, ks_ref, vs_ref, att_ref, ext_ref, hid_ref, n2_ref, act_ref, der_ref, acc_ref, obf_ref,
    wsend, wrecv, wload, wsave, xsend, xrecv, csem, ssem, lsem, osem, jsem, asem,
):
    rep, shard = place()
    rows, width = x_ref.shape
    nb = rows // BQ
    npair = width // 128
    nf = act_out.shape[0]
    across = (rep, 1 - shard)
    peers = [(rep ^ 8, shard), (rep ^ 4, shard), (rep ^ 2, shard), (rep ^ 1, shard)]
    core = rep & 1
    part8 = ((rep >> 1) & 1) * 4 + ((rep >> 2) & 1) * 2 + ((rep >> 3) & 1)
    plan = Plan(lens_ref, shard, rows)
    bounds, slot = plan.bounds(), plan.away()

    parts = []
    for src, dst, save, ncols in ((wq_in, wq_ref, wq_out, 3), (wo_in, wo_ref, wo_out, 1), (wf_in, wf_ref, wf_out, 2), (wp_in, wp_ref, wp_out, 1)):
        cols = src.shape[1] // ncols
        for n in range(ncols):
            parts.append((src, dst, save, n * cols, cols))
    nparts = len(parts)

    def chain(n, step):
        src, dst, _save, col, cols = parts[n]
        half = src.shape[0]
        unit = half // 8
        count = 1 if step == 0 else 1 << (step - 1)
        first = (part8 & ~(count - 1)) * unit
        here = pl.ds(pl.multiple_of(first, 16), count * unit)
        side = pl.ds(pl.multiple_of(col + core * (cols // 2), 128), cols // 2)
        sems = (wsend.at[n, step], wrecv.at[n, step])
        if step == 0:
            into = pl.ds(pl.multiple_of(shard * half + first, 16), count * unit)
            return remote(src.at[here, side], dst.at[into, side], *sems, across)
        into = pl.ds(pl.multiple_of((1 - shard) * half + first, 16), count * unit)
        return remote(dst.at[into, side], dst.at[into, side], *sems, peers[step - 1])

    def advance(n, step):
        chain(n, step).wait_recv()
        if step < 4:
            chain(n, step + 1).start()

    whole = [(wq_in, wq_ref, wq_out), (wo_in, wo_ref, wo_out), (wf_in, wf_ref, wf_out), (wp_in, wp_ref, wp_out)]

    def half_rows(src, which):
        return pl.ds(pl.multiple_of(which * src.shape[0], 16), src.shape[0])

    def own_load(n):
        src, dst, _ = whole[n]
        return pltpu.make_async_copy(src, dst.at[half_rows(src, shard), :], wload.at[n])

    def other_save(n):
        src, dst, save = whole[n]
        return pltpu.make_async_copy(dst.at[half_rows(src, 1 - shard), :], save, wsave.at[n])

    x_load = pltpu.make_async_copy(xin_ref, xo_ref, lsem.at[0])
    c_load = pltpu.make_async_copy(cin_ref, co_ref, lsem.at[1])
    x_load.start()
    for n in range(4):
        own_load(n).start()
    c_load.start()
    greet([across] + peers)
    small = remote(small_ref, sm_ref.at[shard], ssem.at[0], ssem.at[1], across)
    small.start()
    for n in range(4):
        chain(n, 0).start()

    tail = plan.s0 + plan.s1
    theirs = jnp.where(plan.stays, rows, tail)
    split = jnp.where(plan.stays, rows, plan.s0)
    whole_one = jnp.where(plan.stays & (plan.slot == 1), 1, 0)

    def pack_sent(dst_ref, src_ref, i):
        n = (i + 1) * BQ
        total = None
        for k in range(2):
            part = dot(moved_pick(jnp.where(slot == k, tail, rows), i), src_ref[k, 0:n, :])
            total = part if total is None else total + part
        dst_ref[i * BQ : n, :] = total.astype(BF)

    def pack_own(dst_ref, src_ref, i):
        n = (i + 1) * BQ
        r = slice(i * BQ, n)
        row = i * BQ + lax.broadcasted_iota(jnp.int32, (BQ, width), 0)
        base = jnp.where(whole_one == 1, src_ref[1, r, :].astype(F32), src_ref[0, r, :].astype(F32))
        dst_ref[r, :] = jnp.where(row >= split, dot(moved_pick(split, i), src_ref[1, 0:n, :]), base).astype(BF)

    def merged(own_ref, got_ref, i):
        r = rows_of(i, BQ)
        row = i * BQ + lax.broadcasted_iota(jnp.int32, (BQ, width), 0)
        return jnp.where(row >= theirs, got_ref[r, :].astype(F32), own_ref[r, :].astype(F32)).astype(BF)

    def x_chunk(i):
        r = pl.ds(i * BQ, BQ)
        return remote(xs_ref.at[r, :], xr_ref.at[r, :], xsend.at[i], xrecv.at[i], across)

    c_copy = remote(cs_ref, cr_ref, csem.at[0], csem.at[1], across)
    x_load.wait()
    pack_sent(xs_ref, xo_ref, 0)
    x_chunk(0).start()
    for n in range(4, nparts):
        chain(n, 0).start()
    for i in range(1, nb):
        pack_sent(xs_ref, xo_ref, i)
        x_chunk(i).start()
    sm_ref[shard] = small_ref[...]
    small.wait()
    first, second = sm_ref[0].astype(F32), sm_ref[1].astype(F32)
    hw = width // 2
    vecs_ref[0:8, 0:hw] = first[0:8]
    vecs_ref[0:8, hw:] = second[0:8]
    for n in range(nf):
        here = (first if n < nf // 2 else second)[8 + 2 * (n % (nf // 2)) : 10 + 2 * (n % (nf // 2))]
        vecs_ref[8 + n : 9 + n, 0:hw] = here[0:1]
        vecs_ref[8 + n : 9 + n, hw:] = here[1:2]
    vecs_ref[8 + nf : 16, :] = jnp.zeros((8 - nf, width), F32)
    c_load.wait()

    for i in range(nb):
        pack_sent(cs_ref, co_ref, i)
        pack_own(x_ref, xo_ref, i)

    c_copy.start()
    for tick in range(4 + 4):
        for n in range(4):
            if 0 <= tick - n < 5:
                advance(n, tick - n)
    own_load(0).wait()
    own_load(1).wait()
    other_save(0).start()
    other_save(1).start()
    late = list(range(4, nparts))
    moves = [(n, t - k) for t in range(len(late) + 4) for k, n in enumerate(late) if 0 <= t - k < 5]
    done = {"moves": 0}

    def move(count):
        for n, step in moves[done["moves"] : done["moves"] + count]:
            advance(n, step)
        done["moves"] += count

    gain, shift = vecs_ref[G1 : G1 + 1, :], vecs_ref[B1 : B1 + 1, :]
    lq = lane_half((BQ, 128))
    tri = lax.broadcasted_iota(jnp.int32, (BQ, BQ), 1) <= lax.broadcasted_iota(jnp.int32, (BQ, BQ), 0)
    def joined_save(i, b):
        r = pl.ds(i * BQ, BQ)
        return pltpu.make_async_copy(jn_ref.at[r, pl.ds(b * width, width)], joined_out.at[b, r, :], jsem.at[i, b])

    for i in range(nb):
        x_chunk(i).wait_recv()
        n = (i + 1) * BQ
        r = slice(i * BQ, n)
        xb = merged(x_ref, xr_ref, i)
        x_ref[r, :] = xb
        unit, _inv = norm_stats(xb.astype(F32))
        n1 = (unit * gain + shift).astype(BF)
        for b, row in ((0, QB), (1, None), (2, VB)):
            value = dot(n1, wq_ref[:, b * width : (b + 1) * width])
            if row is not None:
                value = value + vecs_ref[row : row + 1, :]
            jn_ref[r, b * width : (b + 1) * width] = value.astype(BF)
        for b in range(3):
            joined_save(i, b).start()
        ohf = own_segment(bounds, i * BQ, BQ)
        oh = ohf.astype(BF)
        neg = other_segment(bounds, i * BQ, BQ).astype(BF)

        @pl.loop(0, npair)
        def _(h):
            k2 = jn_ref[r, pl.ds(pl.multiple_of(width + h * 128, 128), 128)]
            v2 = jn_ref[r, pl.ds(pl.multiple_of(2 * width + h * 128, 128), 128)]
            one = jnp.ones_like(v2)
            ks_ref[h, 0, r, :] = jnp.where(lq, k2, neg)
            ks_ref[h, 1, r, :] = jnp.where(lq, neg, k2)
            vs_ref[h, 0, r, :] = jnp.where(lq, v2, one)
            vs_ref[h, 1, r, :] = jnp.where(lq, one, v2)

        @pl.loop(0, npair)
        def _(h):
            cq = pl.ds(pl.multiple_of(h * 128, 128), 128)
            q2 = jn_ref[r, cq]
            qs = [jnp.where(lq, q2, oh), jnp.where(lq, oh, q2)]
            outs, exts = [], []
            for e in range(2):
                sd = jnp.where(tri, dot_nt(qs[e], ks_ref[h, e, r, :]), NEG)
                peak = jnp.max(sd, axis=1, keepdims=True)
                if i:
                    so = dot_nt(qs[e], ks_ref[h, e, 0 : n - BQ, :])
                    peak = jnp.maximum(peak, jnp.max(so, axis=1, keepdims=True))
                    po = jnp.exp2((so - peak) * EXPC).astype(BF)
                pd = jnp.exp2((sd - peak) * EXPC).astype(BF)
                acc = dot(pd, vs_ref[h, e, r, :])
                if i:
                    acc = acc + dot(po, vs_ref[h, e, 0 : n - BQ, :])
                outs.append(acc)
                tot = acc[:, HD : HD + 1] if e == 0 else acc[:, 0:1]
                exts.append(extra(ohf, -(peak + jnp.log(tot) * (1.0 / SCALE)), 3))
            num = jnp.where(lq, outs[0], outs[1])
            den = pltpu.roll(jnp.where(lq, outs[1], outs[0]), HD, 1)
            att_ref[r, cq] = (num / den).astype(BF)
            ext_ref[r, cq] = jnp.where(lq, exts[1], exts[0]).astype(BF)
            if i == nb - 1:
                for hh in range(npair):
                    todo = moves[MOVES_AT[nb - 2] + 2 * hh : MOVES_AT[nb - 2] + 2 * hh + 2]
                    if todo:

                        @pl.when(h == hh)
                        def _():
                            for n_, step in todo:
                                advance(n_, step)

        if i < nb - 1:
            move(MOVES_AT[i] - done["moves"])
    done["moves"] = min(len(moves), MOVES_AT[nb - 2] + 2 * npair)
    move(len(moves) - done["moves"])
    x_save = pltpu.make_async_copy(x_ref, x_out, osem.at[0])
    att_save = pltpu.make_async_copy(att_ref, att_out, osem.at[1])
    ext_save = pltpu.make_async_copy(ext_ref, ext_out, osem.at[2])
    for copy in (x_save, att_save, ext_save):
        copy.start()
    own_load(2).wait()
    own_load(3).wait()
    other_save(2).start()
    other_save(3).start()

    gain2, shift2 = vecs_ref[G2 : G2 + 1, :], vecs_ref[B2 : B2 + 1, :]

    @pl.loop(0, nb)
    def _(i):
        r = rows_of(i, BQ)
        hid = x_ref[r, :].astype(F32) + (dot(att_ref[r, :], wo_ref[...]) + vecs_ref[OB : OB + 1, :])
        hid_ref[r, :] = hid
        unit, _inv = norm_stats(hid)
        n2_ref[r, :] = (unit * gain2 + shift2).astype(BF)
        acc_ref[r, :] = hid + vecs_ref[PB : PB + 1, :]

    hid_save = pltpu.make_async_copy(hid_ref, hid_out, osem.at[3])
    n2_save = pltpu.make_async_copy(n2_ref, n2_out, osem.at[4])
    hid_save.start()
    n2_save.start()

    def gelu_save(n):
        return (
            pltpu.make_async_copy(act_ref.at[n % 2], act_out.at[n], asem.at[0, n]),
            pltpu.make_async_copy(der_ref.at[n % 2], der_out.at[n], asem.at[1, n]),
        )

    for n in range(nf):
        if n >= 2:
            for copy in gelu_save(n - 2):
                copy.wait()
        c = slice(n * width, (n + 1) * width)

        @pl.loop(0, nb)
        def _(i):
            r = rows_of(i, BQ)
            act, der = gelu_both(dot(n2_ref[r, :], wf_ref[:, c]) + vecs_ref[FB + n : FB + n + 1, :])
            act = act.astype(BF)
            act_ref[n % 2, r, :] = act
            der_ref[n % 2, r, :] = der.astype(BF)
            total = acc_ref[r, :] + dot(act, wp_ref[c, :])
            if n < nf - 1:
                acc_ref[r, :] = total
            else:
                obf_ref[r, :] = total.astype(BF)

        for copy in gelu_save(n):
            copy.start()
    out_save = pltpu.make_async_copy(obf_ref, out_out, osem.at[5])
    out_save.start()

    for i in range(nb):
        pack_own(cot_ref, co_ref, i)

    c_copy.wait_recv()

    @pl.loop(0, nb)
    def _(i):
        cot_ref[rows_of(i, BQ), :] = merged(cot_ref, cr_ref, i)

    cot_save = pltpu.make_async_copy(cot_ref, cot_out, osem.at[6])
    cot_save.start()
    for n in range(nparts):
        for step in range(5):
            chain(n, step).wait_send()
    for i in range(nb):
        x_chunk(i).wait_send()
        for b in range(3):
            joined_save(i, b).wait()
    c_copy.wait_send()
    for n in range(4):
        other_save(n).wait()
    for n in range(max(0, nf - 2), nf):
        for copy in gelu_save(n):
            copy.wait()
    for copy in (x_save, att_save, ext_save, hid_save, n2_save, out_save, cot_save):
        copy.wait()


MOVES_AT = (2, 4, 7)


def front(lens, xin, cin, small, wq, wo, wf, wp):
    slots, rows, width = xin.shape
    ff = wf.shape[1]
    nf = ff // width
    nb = rows // BQ
    s = jax.ShapeDtypeStruct
    v = pltpu.VMEM
    act = s((rows, width), BF)
    nparts = 7
    return pl.pallas_call(
        front_body,
        name="front",
        out_shape=(
            act, s((3, rows, width), BF), act, act, s((rows, width), F32), act, s((nf, rows, width), BF), s((nf, rows, width), BF),
            act, act, s(wq.shape, BF), s(wo.shape, BF), s(wf.shape, BF), s(wp.shape, BF), s((16, width), F32),
        ),
        in_specs=[SMEM] + anyspecs(2) + vspecs(1) + anyspecs(4),
        out_specs=tuple(anyspecs(14) + vspecs(1)),
        scratch_shapes=[
            v((width, 3 * width), BF), v((width, width), BF), v((width, ff), BF), v((ff, width), BF),
            v((slots, rows, width), BF), v((rows, width), BF), v((rows, width), BF),
            v((slots, rows, width), BF), v((rows, width), BF), v((rows, width), BF),
            v((rows, width), BF), v((rows, width), BF), v((2,) + small.shape, BF),
            v((rows, 3 * width), BF), v((width // 128, 2, rows, 128), BF), v((width // 128, 2, rows, 128), BF),
            v((rows, width), BF), v((rows, width), BF), v((rows, width), F32), v((rows, width), BF),
            v((2, rows, width), BF), v((2, rows, width), BF), v((rows, width), F32), v((rows, width), BF),
            DMA((nparts, 5)), DMA((nparts, 5)), DMA((4,)), DMA((4,)), DMA((nb,)), DMA((nb,)), DMA((2,)), DMA((2,)), DMA((2,)),
            DMA((7,)), DMA((nb, 3)), DMA((2, nf)),
        ],
        compiler_params=params(collective_id=0, has_side_effects=True),
        cost_estimate=cost(40e9, 60e6, 12e6),
    )(lens, xin, cin, small, wq, wo, wf, wp)


def back_body(
    bits, lens_ref, vecs_ref, x_in, joined_in, att_in, ext_in, hid_in, n2_in, act_in, der_in, out_in, cot_in,
    wq_own, wo_own, wf_own, wp_own, wq_oth, wo_oth, wf_oth, wp_oth,
    res_out, dx_out, dxr_out, outr_out, sums_ref,
    wf_ref, wp_ref, wo_ref, wq_ref, cot_ref, n2_ref, act_ref, der_ref, gpre_ref, acc_ref, hid_ref, att_ref,
    gm_ref, r0_ref, rb_ref, res_ref, dk_ref, dv_ref, sm_ref, smb_ref, smr_ref,
    wsem, lsem, asem, hsem, ssem, rsem, msem, mrem, osem, dsem, drem, vsem, fsem,
):
    rep, shard = place()
    core = rep & 1
    rows, width = cot_ref.shape
    hw = width // 2
    nb = rows // BQ
    nf = act_in.shape[0]
    npair = width // 128
    m = bits - 1
    sibling, across = (rep ^ 1, shard), (rep, 1 - shard)
    peers = {0: across}
    for t in range(1, bits):
        peers[t] = (rep ^ (1 << t), shard)
    plan = Plan(lens_ref, shard, rows)
    bounds = plan.bounds()

    def weight_loads(own, oth, dst, into):
        half = own.shape[0]
        for n, (src, which) in enumerate(((own, shard), (oth, 1 - shard))):
            yield n, src, dst.at[pl.ds(pl.multiple_of(into + which * half, 16), half), :]

    def fc_loads(j):
        for n, src, dst in weight_loads(wf_own, wf_oth, wf_ref, j * width):
            for part in range(2):
                here = pl.ds((part * nf + j) * hw, hw)
                yield pltpu.make_async_copy(src.at[:, here], dst.at[:, pl.ds(part * hw, hw)], wsem.at[0, n, part, j])

    def proj_loads(j):
        for n, (src, which) in enumerate(((wp_own, shard), (wp_oth, 1 - shard))):
            into = pl.ds(pl.multiple_of(j * width + which * hw, 16), hw)
            yield pltpu.make_async_copy(src.at[pl.ds(j * hw, hw), :], wp_ref.at[into, :], wsem.at[1, n, 0, j])

    def gelu_loads(j):
        for k, (src, dst) in enumerate(((act_in, act_ref), (der_in, der_ref))):
            for part in range(2):
                block = part * (nf // 2) + j // 2
                here = pl.ds((j % 2) * hw, hw)
                yield pltpu.make_async_copy(src.at[block, :, here], dst.at[j % 2, :, pl.ds(part * hw, hw)], asem.at[k, part, j])

    def plain(n, src, dst):
        return pltpu.make_async_copy(src, dst, lsem.at[n])

    cot_load, n2_load, att_load = plain(0, cot_in, cot_ref), plain(1, n2_in, n2_ref), plain(2, att_in, att_ref)
    wo_loads = [pltpu.make_async_copy(s_, d_, wsem.at[2, n, 0, 0]) for n, s_, d_ in weight_loads(wo_own, wo_oth, wo_ref, 0)]
    wq_loads = [pltpu.make_async_copy(s_, d_, wsem.at[2, n, 0, 1]) for n, s_, d_ in weight_loads(wq_own, wq_oth, wq_ref, 0)]
    x_load, ext_load = plain(3, x_in, act_ref.at[0]), plain(4, ext_in, der_ref.at[0])
    joined_loads = [plain(5 + b, joined_in.at[b], wf_ref.at[pl.ds(b * rows, rows), :]) for b in range(3)]

    def hid_load(i):
        return pltpu.make_async_copy(hid_in.at[pl.ds(i * BQ, BQ), :], hid_ref.at[i % 2], hsem.at[i])

    cot_load.start()
    for j in range(2):
        for copy in list(proj_loads(j)) + list(gelu_loads(j)) + list(fc_loads(j)):
            copy.start()
        if j == 0:
            n2_load.start()
    greet([sibling, across] + [peers[t] for t in range(1, bits)])

    per = gm_ref.shape[3] // PIECE
    count = 3 * per
    last = 3 + 2 * m
    by_x = (0,) + tuple(range(1, bits))
    by_y = tuple(range(1, bits)) + (0,)
    by_z = (2, 1) + tuple(range(3, bits)) + (0,)
    orders = [by_x] * per + [by_y] * per + [by_y, by_z, by_y]

    def source(k, away):
        a, at = k // per, pl.ds((k % per) * PIECE, PIECE)
        return gm_ref.at[away, a, :, at, :] if a < 2 else gm_ref.at[1, away, :, at, :]

    def held(k, i):
        half, first, size = None, 0, PIECE
        for d in orders[k][:i]:
            if d == 0:
                half = shard
            else:
                size //= 2
                first = first + ((rep >> d) & 1) * size
        return half, first, size

    def at_rows(first, size):
        return pl.ds(pl.multiple_of(first, 16), size)

    def landing(k, i):
        d = orders[k][i]
        half, _first, size = held(k, i + 1)
        before = sum(PIECE >> (n + 1) for n in range(len([e for e in orders[k][:i] if e])))
        if d == 0:
            return rb_ref.at[k, 0, pl.ds(before, size), :]
        at = pl.ds(before, size)
        return rb_ref.at[k, :, at, :] if half is None else rb_ref.at[k, 1, at, :]

    def leaving(k, i):
        d = orders[k][i]
        half, first, size = held(k, i)
        own = source(k, 0)
        if d == 0:
            return own.at[1 - shard, at_rows(first, size), :]
        size //= 2
        at = at_rows(first + (1 - ((rep >> d) & 1)) * size, size)
        return own.at[:, at, :] if half is None else own.at[half, at, :]

    def copy(k, step):
        sems = (ssem.at[step, k], rsem.at[step, k])
        if step == 0:
            return remote(source(k, 1), r0_ref.at[k], *sems, sibling)
        if step <= m + 1:
            return remote(leaving(k, step - 1), landing(k, step - 1), *sems, peers[orders[k][step - 1]])
        if step <= 2 * m + 1:
            back = [d for d in orders[k] if d]
            t = m - (step - m - 2)
            size = PIECE >> t
            first = 0
            for n in range(t):
                first = first + ((rep >> back[n]) & 1) * (PIECE >> (n + 1))
            here = res_ref.at[k, at_rows(first, size), :]
            return remote(here, here, *sems, peers[back[t - 1]])
        return remote(res_ref.at[k], res_out.at[core, k], *sems, sibling)

    def keep(k):
        return pltpu.make_async_copy(res_ref.at[k], res_out.at[core, k], fsem.at[k])

    def add(dst, first, other, base, size, out=None):
        chunk = min(size, 64)

        @pl.loop(0, size // chunk)
        def _(i):
            at = pl.ds(pl.multiple_of(first + i * chunk, 16), chunk)
            total = dst[at, :].astype(F32) + other[pl.ds(pl.multiple_of(base + i * chunk, 16), chunk), :].astype(F32)
            (dst if out is None else out)[at, :] = total.astype(BF)

    def act_step(k, step):
        if step:
            copy(k, step - 1).wait_recv()
        own = source(k, 0)
        if step == 1:
            for h in range(2):
                add(own.at[h], 0, r0_ref.at[k, h], 0, PIECE)
        elif 2 <= step <= m + 2:
            i = step - 2
            half, first, size = held(k, i + 1)
            land = landing(k, i)
            if half is None:
                for h in range(2):
                    add(own.at[h], first, land.at[h], 0, size)
            else:
                add(own.at[half], first, land, 0, size, res_ref.at[k] if i == m else None)
        if step < last:
            copy(k, step).start()
        if step == last - 1:
            keep(k).start()

    delay = [0, 1] + list(range(3, last + 1)) + [last + 2]
    groups = [(n, [n, per + n]) for n in range(per)]
    state = {"tick": 0}

    def due(tick):
        for start, ks in groups:
            for k in ks:
                for step in range(last + 1):
                    if start + delay[step] == tick:
                        yield k, step

    def tick():
        for k, step in due(state["tick"]):
            act_step(k, step)
        state["tick"] += 1

    gbase = 16
    sm_ref[...] = jnp.zeros_like(sm_ref)

    @pl.loop(0, nb)
    def _(i):
        acc_ref[rows_of(i, BQ), :] = jnp.zeros((BQ, width), F32)

    cot_load.wait()
    n2_load.wait()
    for j in range(nf):
        for c in list(proj_loads(j)) + list(gelu_loads(j)) + list(fc_loads(j)):
            c.wait()
        if j + 2 < nf:
            for c in list(proj_loads(j + 2)) + list(fc_loads(j + 2)):
                c.start()
        here = slice(j * width, (j + 1) * width)

        @pl.loop(0, nb)
        def _(i):
            r = rows_of(i, BQ)
            gact = dot_nt(cot_ref[r, :], wp_ref[here, :])
            gpre = (gact * der_ref[j % 2, r, :].astype(F32)).astype(BF)
            gpre_ref[r, :] = gpre
            sm_ref[gbase + j : gbase + j + 1, :] += jnp.sum(gpre.astype(F32), axis=0, keepdims=True)
            acc_ref[r, :] += dot_nt(gpre, wf_ref[here, :])

        for h in range(2):
            gp = dot_tn(act_ref[j % 2, :, h * hw : (h + 1) * hw], cot_ref[...]).astype(BF)
            gf = dot_tn(n2_ref[:, h * hw : (h + 1) * hw], gpre_ref[...]).astype(BF)
            for c in range(2):
                gm_ref[c ^ core, 1, h, j * hw : (j + 1) * hw, :] = gp[:, c * hw : (c + 1) * hw]
                gm_ref[c ^ core, 0, h, j * hw : (j + 1) * hw, :] = gf[:, c * hw : (c + 1) * hw]
        if j + 2 < nf:
            for c in gelu_loads(j + 2):
                c.start()
        elif j + 2 == nf:
            for c in [x_load, ext_load, att_load] + wo_loads + wq_loads:
                c.start()
            hid_load(0).start()
            hid_load(1).start()
        if j:
            tick()

    for c in joined_loads:
        c.start()
    for c in [att_load] + wo_loads:
        c.wait()
    gain2 = vecs_ref[G2 : G2 + 1, :]
    gatt_ref = cot_ref
    for i in range(nb):
        r = slice(i * BQ, (i + 1) * BQ)
        hid_load(i).wait()
        unit, inv = norm_stats(hid_ref[i % 2])
        gn2 = acc_ref[r, :]
        gy = cot_ref[r, :].astype(F32)
        ghid = gy + norm_back(gn2, unit, inv, gain2)
        if i + 2 < nb:
            hid_load(i + 2).start()
        acc_ref[r, :] = ghid
        low = ghid.astype(BF)
        gpre_ref[r, :] = low
        gatt_ref[r, :] = dot_nt(low, wo_ref[...]).astype(BF)
        sm_ref[0:1, :] += jnp.sum(gn2 * unit, axis=0, keepdims=True)
        sm_ref[1:2, :] += jnp.sum(gn2, axis=0, keepdims=True)
        sm_ref[2:3, :] += jnp.sum(gy, axis=0, keepdims=True)
        sm_ref[3:4, :] += jnp.sum(low.astype(F32), axis=0, keepdims=True)
    x_load.wait()
    gain1, shift1 = vecs_ref[G1 : G1 + 1, :], vecs_ref[B1 : B1 + 1, :]
    xb_ref, eb_ref, n1_ref, dxb_ref = act_ref.at[0], der_ref.at[0], der_ref.at[1], act_ref.at[1]

    @pl.loop(0, nb)
    def _(i):
        r = rows_of(i, BQ)
        unit, _inv = norm_stats(xb_ref[r, :].astype(F32))
        n1_ref[r, :] = (unit * gain1 + shift1).astype(BF)

    for start, ks in groups:
        for k in ks:
            copy(k, 0).wait_send()
    for h in range(2):
        go = dot_tn(att_ref[:, h * hw : (h + 1) * hw], gpre_ref[...]).astype(BF)
        for c in range(2):
            gm_ref[1, c ^ core, h, 3 * hw : 4 * hw, :] = go[:, c * hw : (c + 1) * hw]
    tick()

    out_copy = remote(out_in, outr_out, osem.at[0], osem.at[1], across)
    for c in joined_loads + [ext_load]:
        c.wait()

    lq = lane_half((BQ, 128))
    tri = lax.broadcasted_iota(jnp.int32, (BQ, BQ), 0) <= lax.broadcasted_iota(jnp.int32, (BQ, BQ), 1)
    left = lane_half((rows, 128))
    ones = lax.broadcasted_iota(jnp.int32, (rows, 128), 1) % HD
    ones = (ones >= 3) & (ones < 6)
    first_tick = state["tick"]
    slots = [(hh, i) for hh in range(npair) for i in range(nb)]
    when = {slots[2 * n + 1]: first_tick + n for n in range(len(slots) // 2)}
    total_ticks = max(start + delay[last] for start, _ in groups) + 1

    @pl.loop(0, npair)
    def _(h):
        col = pl.ds(pl.multiple_of(h * 128, 128), 128)
        k2 = wf_ref[rows : 2 * rows, col]
        v2 = wf_ref[2 * rows : 3 * rows, col]
        zero = jnp.zeros_like(k2)
        kx = jnp.where(ones, 1.0, other_segment(bounds, 0, rows)).astype(BF)
        vx = jnp.where(ones, 1.0, 0.0).astype(BF)
        ks = [jnp.where(left, k2, kx), jnp.where(left, kx, k2)]
        vs = [jnp.where(left, v2, vx), jnp.where(left, vx, v2)]
        km = [jnp.where(left, k2, zero), jnp.where(left, zero, k2)]
        dk_ref[...] = jnp.zeros_like(dk_ref)
        dv_ref[...] = jnp.zeros_like(dv_ref)
        for i in range(nb):
            r = slice(i * BQ, (i + 1) * BQ)
            q2 = wf_ref[r, col]
            g2 = gatt_ref[r, col]
            ext = eb_ref[r, col]
            zq = jnp.zeros_like(q2)
            prod = g2.astype(F32) * att_ref[r, col].astype(F32)
            d0 = jnp.sum(jnp.where(lq, prod, 0.0), axis=1, keepdims=True)
            d1 = jnp.sum(jnp.where(lq, 0.0, prod), axis=1, keepdims=True)
            zf = jnp.zeros((BQ, 128), F32)
            qs = [jnp.where(lq, q2, ext), jnp.where(lq, ext, q2)]
            gs = [jnp.where(lq, g2, extra(zf, -d0, 3).astype(BF)), jnp.where(lq, extra(zf, -d1, 3).astype(BF), g2)]
            qm = [jnp.where(lq, q2, zq), jnp.where(lq, zq, q2)]
            gm = [jnp.where(lq, g2, zq), jnp.where(lq, zq, g2)]
            dq = None
            for u in range(i + 1):
                b = slice(u * BQ, (u + 1) * BQ)
                dk = dv = None
                for e in range(2):
                    st = dot_nt(ks[e][b], qs[e])
                    if u == i:
                        st = jnp.where(tri, st, NEG)
                    pt = jnp.exp2(st * EXPC)
                    dst = (pt * dot_nt(vs[e][b], gs[e])).astype(BF)
                    one, two, three = dot(pt.astype(BF), gm[e]), dot(dst, qm[e]), dot_tn(dst, km[e][b])
                    dv = one if dv is None else dv + one
                    dk = two if dk is None else dk + two
                    dq = three if dq is None else dq + three
                dv_ref[b, :] += dv
                dk_ref[b, :] += dk
            wp_ref[r, col] = (dq * SCALE).astype(BF)
            for hh in range(npair):
                now = when.get((hh, i))
                if now is not None and now < total_ticks:

                    @pl.when(h == hh)
                    def _():
                        for k, step in due(now):
                            act_step(k, step)
                        if now == OUT_TICK:
                            out_copy.start()

        wp_ref[rows : 2 * rows, col] = (dk_ref[...] * SCALE).astype(BF)
        wp_ref[2 * rows : 3 * rows, col] = dv_ref[...].astype(BF)

    state["tick"] = min(total_ticks, first_tick + len(when))
    assert first_tick <= OUT_TICK < first_tick + len(when)

    for c in wq_loads:
        c.wait()

    def dx_chunk(i):
        at = pl.ds(i * BQ, BQ)
        return remote(dxb_ref.at[at, :], dxr_out.at[at, :], dsem.at[i], drem.at[i], across)

    for i in range(nb):
        r = slice(i * BQ, (i + 1) * BQ)
        gn1 = dot_nt(wp_ref[0:rows][r], wq_ref[:, 0:width])
        for b in (1, 2):
            gn1 = gn1 + dot_nt(wp_ref[b * rows + i * BQ : b * rows + (i + 1) * BQ, :], wq_ref[:, b * width : (b + 1) * width])
        unit, inv = norm_stats(xb_ref[r, :].astype(F32))
        dxb_ref[r, :] = (acc_ref[r, :] + norm_back(gn1, unit, inv, gain1)).astype(BF)
        dx_chunk(i).start()
        sm_ref[11:12, :] += jnp.sum(gn1 * unit, axis=0, keepdims=True)
        sm_ref[12:13, :] += jnp.sum(gn1, axis=0, keepdims=True)
    dx_save = plain(8, dxb_ref, dx_out)
    dx_save.start()

    base = max(state["tick"], total_ticks)
    tail = []
    for b in range(3):
        here = wp_ref[b * rows : (b + 1) * rows, :]
        sm_ref[8 + b : 9 + b, :] = jnp.sum(here.astype(F32), axis=0, keepdims=True)
        for h in range(2):
            gw = dot_tn(n1_ref[:, h * hw : (h + 1) * hw], here).astype(BF)
            for c in range(2):
                gm_ref[1, c ^ core, h, b * hw : (b + 1) * hw, :] = gw[:, c * hw : (c + 1) * hw]
        if b == 1:
            act_step(2 * per, 0)
    act_step(2 * per + 1, 0)
    act_step(2 * per + 2, 0)

    small_peers = [sibling, across] + [peers[t] for t in range(1, bits)]

    def small_copy(step):
        src = sm_ref if step == 0 else smb_ref.at[step - 1]
        return remote(src, smr_ref.at[step], msem.at[step], mrem.at[step], small_peers[step])

    def small(step):
        if step:
            small_copy(step - 1).wait_recv()
            before = sm_ref[...] if step == 1 else smb_ref[step - 2]
            total = before + smr_ref[step - 1]
            if step == 2 + m:
                sums_ref[...] = total
            else:
                smb_ref[step - 1] = total
        if step < 2 + m:
            small_copy(step).start()

    for n in range(state["tick"], total_ticks):
        for k, step in due(n):
            act_step(k, step)
    for n in range(last + per):
        if n <= 2 + m:
            small(n)
        for p in range(per):
            if 1 <= n + 1 - p <= last:
                act_step(2 * per + p, n + 1 - p)
    for k in range(count):
        for step in range(last):
            if step or k >= 2 * per:
                copy(k, step).wait_send()
        keep(k).wait()
    for step in range(2 + m):
        small_copy(step).wait_send()
    out_copy.wait()
    for i in range(nb):
        dx_chunk(i).wait()
    dx_save.wait()


OUT_TICK = 7


def back(bits, lens, vecs, saved, own, oth):
    x, joined, att, ext, hid, n2, act, der, out, cot = saved
    rows, width = x.shape
    nf = act.shape[0]
    nb = rows // BQ
    hw = width // 2
    m = bits - 1
    count = 3 * (nf * hw // PIECE)
    s = jax.ShapeDtypeStruct
    v = pltpu.VMEM
    sums = (24, width)
    return pl.pallas_call(
        functools.partial(back_body, bits),
        name="back",
        out_shape=(s((2, count, PIECE, hw), BF), s((rows, width), BF), s((rows, width), BF), s((rows, width), BF), s(sums, F32)),
        in_specs=[SMEM] + vspecs(1) + anyspecs(18),
        out_specs=tuple(anyspecs(4) + vspecs(1)),
        scratch_shapes=[
            v((nf * width, width), BF), v((nf * width, width), BF), v((width, width), BF), v((width, 3 * width), BF),
            v((rows, width), BF), v((rows, width), BF), v((2, rows, width), BF), v((2, rows, width), BF), v((rows, width), BF),
            v((rows, width), F32), v((2, BQ, width), F32), v((rows, width), BF),
            v((2, 2, 2, nf * hw, hw), BF), v((count, 2, PIECE, hw), BF), v((count, 2, PIECE, hw), BF), v((count, PIECE, hw), BF),
            v((rows, 128), F32), v((rows, 128), F32), v(sums, F32), v((m + 1,) + sums, F32), v((m + 2,) + sums, F32),
            DMA((3, 2, 2, nf)), DMA((9,)), DMA((2, 2, nf)), DMA((nb,)), DMA((3 + 2 * m, count)), DMA((3 + 2 * m, count)),
            DMA((m + 2,)), DMA((m + 2,)), DMA((2,)), DMA((nb,)), DMA((nb,)), DMA((1,)), DMA((count,)),
        ],
        compiler_params=params(collective_id=1, has_side_effects=True),
        cost_estimate=cost(60e9, 60e6, 8e6),
    )(lens, vecs, *saved, *own, *oth)


def finish_body(
    lens_ref, deal_ref, sums_ref, res_in, dx_in, dxr_in, out_in, outr_in, y_out, d_out, *rest
):
    outs, scratch = rest[:13], rest[13:]
    (o_g1, o_b1, o_qkv, o_qb, o_vb, o_wo, o_ob, o_g2, o_b2, o_fc, o_fb, o_proj, o_pb) = outs
    res_ref, src_ref, y_ref, qkv_ref, wo_ref, fc_ref, proj_ref, lsem, ssem = scratch
    shard = lax.axis_index("shard")
    rows, width = src_ref.shape[1:]
    hw = width // 2
    nb = rows // BQ
    slots = y_ref.shape[1]
    nf = fc_ref.shape[1] // width
    plan = Plan(lens_ref, shard, rows)
    loads = [pltpu.make_async_copy(a, src_ref.at[n], lsem.at[n]) for n, a in enumerate((out_in, outr_in, dx_in, dxr_in))]
    per = res_in.shape[1] // 3
    pieces = [pltpu.make_async_copy(res_in.at[:, pl.ds(per * a, per)], res_ref.at[:, pl.ds(per * a, per)], lsem.at[4 + a]) for a in range(3)]
    for copy in loads + pieces:
        copy.start()
    own = pl.ds(pl.multiple_of(shard * hw, 128), hw)
    for ref, row in ((o_g1, 11), (o_b1, 12), (o_qb, 8), (o_vb, 10), (o_ob, 3), (o_g2, 0), (o_b2, 1), (o_pb, 2)):
        ref[...] = sums_ref[row : row + 1, own]
    for j in range(nf):
        o_fb[:, j * hw : (j + 1) * hw] = sums_ref[16 + j : 17 + j, own]

    def save(n, src, dst):
        return pltpu.make_async_copy(src, dst, ssem.at[n])

    saves = []
    for g in range(2):
        loads[2 * g].wait()
        loads[2 * g + 1].wait()
        for j in range(slots):
            q = slots * shard + j
            if g == 0:
                q = sum(jnp.where(q == n, deal_ref[0, n], 0) for n in range(2 * slots))
            side, offset, size = plan.where(q)

            @pl.loop(0, nb)
            def _(i):
                low, pick = window_pick(rows, i * BQ + offset, BQ)
                row = i * BQ + lax.broadcasted_iota(jnp.int32, pick.shape, 0)
                pick = jnp.where(pick & (row < size), 1.0, 0.0).astype(BF)
                y_ref[g, j, rows_of(i, BQ), :] = dot(pick, src_ref[2 * g + side, pl.ds(low, WINDOW), :]).astype(BF)

            saves.append(save(2 * g + j, y_ref.at[g, j], (y_out, d_out)[g].at[j]))
            saves[-1].start()
    block = lambda c, a, n, r, size: res_ref[c, a * per + (n * hw + r) // PIECE, (n * hw + r) % PIECE : (n * hw + r) % PIECE + size, :]
    for a, (dst, out) in enumerate(((fc_ref, o_fc), (proj_ref, o_proj), (qkv_ref, o_qkv))):
        pieces[a].wait()
        for n in range(nf):
            for c in range(2):
                for r in range(0, hw, 128):
                    value = block(c, a, n, r, 128).astype(F32)
                    at = slice(r, r + 128)
                    if a == 0:
                        fc_ref[at, (c * nf + n) * hw : (c * nf + n + 1) * hw] = value
                    elif a == 1:
                        proj_ref[n * hw + r : n * hw + r + 128, c * hw : (c + 1) * hw] = value
                    elif n < 3:
                        qkv_ref[at, n * width + c * hw : n * width + (c + 1) * hw] = value
                    else:
                        wo_ref[at, c * hw : (c + 1) * hw] = value
        saves.append(save(4 + a, dst, out))
        saves[-1].start()
    saves.append(save(7, wo_ref, o_wo))
    saves[-1].start()
    for copy in saves:
        copy.wait()


def finish(lens, deal, sums, res, dx, dxr, out, outr, slots):
    rows, width = dx.shape
    hw = width // 2
    nf = res.shape[1] * PIECE // 3 // hw
    s = jax.ShapeDtypeStruct
    v = pltpu.VMEM
    vec, act = s((1, hw), F32), s((slots, rows, width), BF)
    wide = lambda a, b: s((a, b), F32)
    vs, an = vspecs(1), anyspecs(1)
    return pl.pallas_call(
        finish_body,
        name="finish",
        out_shape=(act, act, vec, vec, wide(hw, 3 * width), vec, vec, wide(hw, width), vec, vec, vec, wide(hw, nf * width),
                   wide(1, nf * hw), wide(nf * hw, width), vec),
        in_specs=[SMEM, SMEM] + vs + anyspecs(5),
        out_specs=tuple(an * 2 + vs * 2 + an + vs * 2 + an + vs * 3 + an + vs + an + vs),
        scratch_shapes=[
            v(res.shape, BF), v((4, rows, width), BF), v((2, slots, rows, width), BF),
            v((hw, 3 * width), F32), v((hw, width), F32), v((hw, nf * width), F32), v((nf * hw, width), F32), DMA((7,)), DMA((8,)),
        ],
        compiler_params=params(),
        cost_estimate=cost(8e9, 34e6),
    )(lens, deal, sums, res, dx, dxr, out, outr)


def local(bits, layer_in, cotangent, lengths, dealing, g1, b1, wqkv, qb, vb, wout, ob, g2, b2, wfc, bfc, wproj, pb):
    slots, rows, width = layer_in.shape
    hw = width // 2
    nj = bfc.shape[0] // hw
    small = jnp.concatenate([g1, b1, qb, vb, ob, g2, b2, pb, bfc, jnp.zeros(((8 - nj) * hw,), BF)]).reshape(16, hw)
    own = (wqkv, wout, wfc, wproj)
    got = front(lengths, layer_in, cotangent, small, *own)
    saved, oth, vecs = got[:10], got[10:14], got[14]
    res, dx, dxr, outr, sums = back(bits, lengths, vecs, saved, own, oth)
    done = finish(lengths, dealing, sums, res, dx, dxr, saved[8], outr, slots)
    shapes = {2, 3, 5, 6, 8, 9, 10, 12, 14}
    return tuple(v.reshape(-1) if n in shapes else v for n, v in enumerate(done))


def solution(mesh):
    both, one = P(("rep", "shard"), None, None), P("shard")
    mat = P("shard", None)
    in_specs = (both, both, P("rep", None), P("rep", None), one, one, mat, one, one, mat, one, one, one, mat, one, mat, one)
    out_specs = (both, both, one, one, mat, one, one, mat, one, one, one, mat, one, mat, one)
    bits = mesh.shape["rep"].bit_length() - 1
    return jax.shard_map(functools.partial(local, bits), mesh=mesh, in_specs=in_specs, out_specs=out_specs, check_vma=False)
```

```python
import functools

import jax
import jax.numpy as jnp
from jax import lax
from jax.experimental import pallas as pl
from jax.experimental.pallas import tpu as pltpu
from jax.sharding import PartitionSpec as P

HD = 64
BQ = 256
EPS = 1e-05
BF = jnp.bfloat16
F32 = jnp.float32
NEG = -1e30
LOG2E = 1.4426950408889634
SCALE = HD**-0.5
EXPC = SCALE * LOG2E
VLIM = 66_900_000
GELU_A = 0.7978845608028654
GELU_B = 0.044715
MESH = pl.DeviceIdType.MESH
PIECE = 512
WINDOW = 384
G1, B1, QB, VB, OB, G2, B2, PB, FB = range(9)


def dot(a, b):
    return jnp.dot(a, b, preferred_element_type=F32)


def dot_tn(a, b):
    return lax.dot_general(a, b, (((0,), (0,)), ((), ())), preferred_element_type=F32)


def dot_nt(a, b):
    return lax.dot_general(a, b, (((1,), (1,)), ((), ())), preferred_element_type=F32)


def norm_stats(v):
    mean = jnp.mean(v, axis=-1, keepdims=True)
    cen = v - mean
    inv = lax.rsqrt(jnp.mean(cen * cen, axis=-1, keepdims=True) + EPS)
    return cen * inv, inv


def norm_back(grad, unit, inv, gain):
    e = grad * gain
    m1 = jnp.mean(e, axis=-1, keepdims=True)
    m2 = jnp.mean(e * unit, axis=-1, keepdims=True)
    return inv * (e - m1 - unit * m2)


def rows_of(i, size):
    return pl.ds(pl.multiple_of(i * size, size), size)


def lane_half(shape):
    return lax.broadcasted_iota(jnp.int32, shape, 1) < HD


def extra(base, v, first):
    hi = v.astype(BF).astype(F32)
    mid = (v - hi).astype(BF).astype(F32)
    lane = lax.broadcasted_iota(jnp.int32, base.shape, 1) % HD
    out = jnp.where(lane == first, hi, base)
    out = jnp.where(lane == first + 1, mid, out)
    return jnp.where(lane == first + 2, v - hi - mid, out)


def vspecs(n):
    return [pl.BlockSpec(memory_space=pltpu.VMEM)] * n


def anyspecs(n):
    return [pl.BlockSpec(memory_space=pl.ANY)] * n


SMEM = pl.BlockSpec(memory_space=pltpu.SMEM)
DMA = pltpu.SemaphoreType.DMA


def params(**kw):
    return pltpu.CompilerParams(vmem_limit_bytes=VLIM, **kw)


def cost(flops, moved, trans=0):
    return pl.CostEstimate(flops=int(flops), bytes_accessed=int(moved), transcendentals=int(trans))


class Plan:
    def __init__(self, lens_ref, shard, rows):
        group = lens_ref.shape[1]
        half = group // 2
        self.half, self.shard, self.rows = half, shard, rows
        self.lens = [lens_ref[0, q] for q in range(group)]
        long = jnp.int32(0)
        for q in range(1, group):
            long = jnp.where(self.lens[q] == rows, q, long)
        self.long = long
        self.home = lax.div(long, jnp.int32(half))
        self.stays = shard == self.home
        self.slot = long & 1
        self.first = half * (1 - self.home)
        self.s0, self.s1 = self.size(self.first), self.size(self.first + 1)
        self.moved = self.size(long ^ 1)

    def size(self, q):
        out = self.lens[0]
        for n in range(1, len(self.lens)):
            out = jnp.where(q == n, self.lens[n], out)
        return out

    def away(self):
        return jnp.where(self.stays, 1 - self.slot, 0)

    def bounds(self):
        return jnp.where(self.stays, self.rows, self.s0), jnp.where(self.stays, self.rows, self.s0 + self.s1)

    def where(self, q):
        start = jnp.where(q == self.first, 0, jnp.where(q == self.first + 1, self.s0, self.s0 + self.s1))
        start = jnp.where(q == self.long, 0, start)
        side = jnp.where(q == self.long, self.home, 1 - self.home) ^ self.shard
        return side, start, self.size(q)


def window_pick(total, first, count):
    low = jnp.clip((first >> 7) << 7, 0, total - WINDOW)
    want = first - low + lax.broadcasted_iota(jnp.int32, (count, WINDOW), 0)
    return pl.multiple_of(low, 128), want == lax.broadcasted_iota(jnp.int32, (count, WINDOW), 1)


def moved_pick(start, i):
    shape = (BQ, (i + 1) * BQ)
    want = i * BQ - start + lax.broadcasted_iota(jnp.int32, shape, 0)
    return jnp.where(want == lax.broadcasted_iota(jnp.int32, shape, 1), 1.0, 0.0).astype(BF)


def lane_and_segment(bounds, first, rows):
    row = first + lax.broadcasted_iota(jnp.int32, (rows, 128), 0)
    seg = (row >= bounds[0]).astype(jnp.int32) + (row >= bounds[1]).astype(jnp.int32)
    return lax.broadcasted_iota(jnp.int32, (rows, 128), 1) % HD, seg


def own_segment(bounds, first, rows):
    lane, seg = lane_and_segment(bounds, first, rows)
    return jnp.where(lane == seg, 1.0, 0.0)


def other_segment(bounds, first, rows):
    lane, seg = lane_and_segment(bounds, first, rows)
    return jnp.where((lane < 3) & (lane != seg), NEG, 0.0)


def gelu_both(v):
    v2 = v * v
    t = jnp.tanh(v * (GELU_A + (GELU_A * GELU_B) * v2))
    half = 0.5 + 0.5 * t
    return v * half, half + (0.5 * v) * (1.0 - t * t) * (GELU_A + (3.0 * GELU_A * GELU_B) * v2)


def place():
    return lax.axis_index("rep"), lax.axis_index("shard")


def greet(partners):
    barrier = pltpu.get_barrier_semaphore()
    for partner in partners:
        pl.semaphore_signal(barrier, inc=1, device_id=partner, device_id_type=MESH)
    pl.semaphore_wait(barrier, len(partners))


def remote(src, dst, ssem, rsem, to):
    return pltpu.make_async_remote_copy(
        src_ref=src, dst_ref=dst, send_sem=ssem, recv_sem=rsem, device_id=to, device_id_type=MESH
    )


def link_of(d):
    return ((d + 2) // 2 if d else 0), (2 if d > 2 and d % 2 else 1)


def timetable(points, chains, ready, busy):
    free, at, step = dict(busy), {}, {c: 0 for c in chains}
    plan, tail = {name: [] for name, _ in points}, []

    def take(c, now, dest):
        dest.append((c, step[c]))
        if step[c] < len(chains[c]):
            link, long, lag = chains[c][step[c]]
            free[link] = max(now, free.get(link, 0.0)) + long
            at[c] = free[link] + lag
        step[c] += 1

    left = lambda: [c for c in chains if c in at and step[c] <= len(chains[c])]
    for name, now in points:
        for c in chains:
            if ready[c] == name:
                at[c] = now
        while True:
            due = [c for c in left() if at[c] <= now]
            if not due:
                break
            take(min(due, key=lambda c: at[c]), now, plan[name])
    now = points[-1][1]
    while left():
        c = min(left(), key=lambda c: at[c])
        now = max(now, at[c])
        take(c, now, tail)
    return plan, tail


def front_body(
    lens_ref, xin_ref, cin_ref, g1_in, b1_in, qb_in, vb_in, ob_in, g2_in, b2_in, pb_in, fb_in, wq_in, wo_in, wf_in, wp_in,
    x_out, joined_out, att_out, ext_out, hid_out, n2_out, act_out, der_out, out_out, cot_out, wq_out, wo_out, wf_out, wp_out, vecs_ref,
    wq_ref, wo_ref, wf_ref, wp_ref, xo_ref, xs_ref, xr_ref, co_ref, cs_ref, cr_ref, x_ref, cot_ref, small_ref, sm_ref,
    jn_ref, ks_ref, vs_ref, att_ref, ext_ref, hid_ref, n2_ref, act_ref, der_ref, acc_ref, obf_ref,
    wsend, wrecv, wload, wsave, xsend, xrecv, csem, ssem, lsem, osem, jsem, asem,
):
    rep, shard = place()
    rows, width = x_ref.shape
    nb = rows // BQ
    npair = width // 128
    nf = act_out.shape[0]
    across = (rep, 1 - shard)
    peers = [(rep ^ (1 << d), shard) for d in range(4)]
    core = rep & 1
    plan = Plan(lens_ref, shard, rows)
    bounds, slot = plan.bounds(), plan.away()

    parts = []
    for src, dst, nrows, ncols in ((wq_in, wq_ref, 1, 3), (wo_in, wo_ref, 1, 1), (wf_in, wf_ref, 1, 2), (wp_in, wp_ref, 2, 1)):
        size, cols = src.shape[0] // nrows, src.shape[1] // ncols
        for n in range(nrows * ncols):
            parts.append((src, dst, n // ncols * size, size, n % ncols * cols, cols, WAYS[len(parts)]))
    nparts = len(parts)
    early = 4

    def chain(n, step):
        src, dst, row, size, col, cols, way = parts[n]
        half, unit = src.shape[0], size >> len(way)
        index = sum(((rep >> d) & 1) << i for i, d in enumerate(way))
        count = 1 if step == 0 else 1 << (step - 1)
        first = row + ((index & ~(count - 1)) * unit if step <= len(way) else 0)
        here = pl.ds(pl.multiple_of(first, 16), count * unit)
        side = pl.ds(pl.multiple_of(col + core * (cols // 2), 128), cols // 2)
        sems = (wsend.at[n, step], wrecv.at[n, step])
        if step == 0:
            into = pl.ds(pl.multiple_of(shard * half + first, 16), unit)
            return remote(src.at[here, side], dst.at[into, side], *sems, across)
        into = pl.ds(pl.multiple_of((1 - shard) * half + first, 16), count * unit)
        return remote(dst.at[into, side], dst.at[into, side], *sems, peers[(way + (0,))[step - 1]])

    def hops(n):
        return len(parts[n][-1]) + 2

    def act(n, step):
        if step:
            chain(n, step - 1).wait_recv()
        if step < hops(n):
            chain(n, step).start()

    def expected(n):
        _src, _dst, _row, size, _col, cols, way = parts[n]
        mb = size * cols * 1e-6
        out = [(0, mb / LINK_RATE / (1 << len(way)), 1.5)]
        for i, d in enumerate(way):
            out.append((link_of(d)[0], mb / LINK_RATE * link_of(d)[1] / (1 << (len(way) - i)), 1.5))
        return out + [("core", mb / CORE_RATE, 1.0)]

    points, now = [], 21.0
    for i in range(nb):
        for name, long in [(("b", i), 2.0)] + [(("h", i, h), 0.5 + 0.55 * i) for h in range(npair)]:
            now += long
            points.append((name, now))
    first_ones = {n: expected(n) for n in range(early)}
    late_ones = {n: expected(n) for n in range(early, nparts)}
    _none, opening = timetable([("start", 3.0)], first_ones, {n: "start" for n in first_ones}, {})
    opening = sorted(_none["start"], key=lambda e: e[1]) + opening
    busy = {0: 3.0 + sum(c[0][1] for c in first_ones.values()) + 2 * BQ * width * 2e-6 / LINK_RATE}
    agenda, closing = timetable([("start", 20.0)] + points, late_ones, {n: "start" for n in late_ones}, busy)

    whole = [(wq_in, wq_ref, wq_out), (wo_in, wo_ref, wo_out), (wf_in, wf_ref, wf_out), (wp_in, wp_ref, wp_out)]

    def half_rows(src, which):
        return pl.ds(pl.multiple_of(which * src.shape[0], 16), src.shape[0])

    def own_load(n):
        src, dst, _ = whole[n]
        return pltpu.make_async_copy(src, dst.at[half_rows(src, shard), :], wload.at[n])

    def other_save(n):
        src, dst, save = whole[n]
        return pltpu.make_async_copy(dst.at[half_rows(src, 1 - shard), :], save, wsave.at[n])

    x_load = pltpu.make_async_copy(xin_ref, xo_ref, lsem.at[0])
    c_load = pltpu.make_async_copy(cin_ref, co_ref, lsem.at[1])
    x_load.start()
    for n in range(4):
        own_load(n).start()
    c_load.start()
    hw = width // 2
    for n, ref in enumerate((g1_in, b1_in, qb_in, vb_in, ob_in, g2_in, b2_in, pb_in)):
        small_ref[n, :] = ref[...].astype(F32)
    for n in range(nf):
        small_ref[8 + n, :] = fb_in[n * hw : (n + 1) * hw].astype(F32)
    greet([across] + peers)
    small = remote(small_ref, sm_ref.at[shard], ssem.at[0], ssem.at[1], across)
    small.start()
    for n in range(early):
        act(n, 0)

    tail = plan.s0 + plan.s1
    theirs = jnp.where(plan.stays, rows, tail)
    split = jnp.where(plan.stays, rows, plan.s0)
    whole_one = jnp.where(plan.stays & (plan.slot == 1), 1, 0)

    def pack_sent(dst_ref, src_ref, i):
        n = (i + 1) * BQ
        total = None
        for k in range(2):
            part = dot(moved_pick(jnp.where(slot == k, tail, rows), i), src_ref[k, 0:n, :])
            total = part if total is None else total + part
        dst_ref[i * BQ : n, :] = total.astype(BF)

    def pack_own(dst_ref, src_ref, i):
        n = (i + 1) * BQ
        r = slice(i * BQ, n)
        row = i * BQ + lax.broadcasted_iota(jnp.int32, (BQ, width), 0)
        base = jnp.where(whole_one == 1, src_ref[1, r, :].astype(F32), src_ref[0, r, :].astype(F32))
        dst_ref[r, :] = jnp.where(row >= split, dot(moved_pick(split, i), src_ref[1, 0:n, :]), base).astype(BF)

    def merged(own_ref, got_ref, i):
        r = rows_of(i, BQ)
        row = i * BQ + lax.broadcasted_iota(jnp.int32, (BQ, width), 0)
        return jnp.where(row >= theirs, got_ref[r, :].astype(F32), own_ref[r, :].astype(F32)).astype(BF)

    def x_chunk(i):
        r = pl.ds(i * BQ, BQ)
        return remote(xs_ref.at[r, :], xr_ref.at[r, :], xsend.at[i], xrecv.at[i], across)

    c_copy = remote(cs_ref, cr_ref, csem.at[0], csem.at[1], across)
    x_load.wait()
    pack_sent(xs_ref, xo_ref, 0)
    x_chunk(0).start()
    for i in range(1, nb):
        pack_sent(xs_ref, xo_ref, i)
        if i == 2:
            for n, step in agenda["start"]:
                act(n, step)
        x_chunk(i).start()
    sm_ref[shard] = small_ref[...]
    small.wait()
    for n in range(8):
        for which in range(2):
            vecs_ref[n : n + 1, which * hw : (which + 1) * hw] = sm_ref[which, n : n + 1, :]
    for n in range(nf):
        for part in range(2):
            which, row = (2 * n + part) // nf, 8 + (2 * n + part) % nf
            vecs_ref[8 + n : 9 + n, part * hw : (part + 1) * hw] = sm_ref[which, row : row + 1, :]
    vecs_ref[8 + nf : 16, :] = jnp.zeros((8 - nf, width), F32)
    c_load.wait()

    for i in range(nb):
        pack_sent(cs_ref, co_ref, i)
        pack_own(x_ref, xo_ref, i)

    c_copy.start()
    for n, step in opening:
        if step:
            act(n, step)
    own_load(0).wait()
    own_load(1).wait()
    other_save(0).start()
    other_save(1).start()
    def at_point(name):
        for n, step in agenda[name]:
            act(n, step)

    gain, shift = vecs_ref[G1 : G1 + 1, :], vecs_ref[B1 : B1 + 1, :]
    lq = lane_half((BQ, 128))
    tri = lax.broadcasted_iota(jnp.int32, (BQ, BQ), 1) <= lax.broadcasted_iota(jnp.int32, (BQ, BQ), 0)
    def joined_save(i, b):
        r = pl.ds(i * BQ, BQ)
        return pltpu.make_async_copy(jn_ref.at[r, pl.ds(b * width, width)], joined_out.at[b, r, :], jsem.at[i, b])

    for i in range(nb):
        x_chunk(i).wait_recv()
        n = (i + 1) * BQ
        r = slice(i * BQ, n)
        xb = merged(x_ref, xr_ref, i)
        x_ref[r, :] = xb
        unit, _inv = norm_stats(xb.astype(F32))
        n1 = (unit * gain + shift).astype(BF)
        for b, row in ((0, QB), (1, None), (2, VB)):
            value = dot(n1, wq_ref[:, b * width : (b + 1) * width])
            if row is not None:
                value = value + vecs_ref[row : row + 1, :]
            jn_ref[r, b * width : (b + 1) * width] = value.astype(BF)
        for b in range(3):
            joined_save(i, b).start()
        at_point(("b", i))
        ohf = own_segment(bounds, i * BQ, BQ)
        oh = ohf.astype(BF)
        neg = other_segment(bounds, i * BQ, BQ).astype(BF)

        @pl.loop(0, npair)
        def _(h):
            k2 = jn_ref[r, pl.ds(pl.multiple_of(width + h * 128, 128), 128)]
            v2 = jn_ref[r, pl.ds(pl.multiple_of(2 * width + h * 128, 128), 128)]
            one = jnp.ones_like(v2)
            ks_ref[h, 0, r, :] = jnp.where(lq, k2, neg)
            ks_ref[h, 1, r, :] = jnp.where(lq, neg, k2)
            vs_ref[h, 0, r, :] = jnp.where(lq, v2, one)
            vs_ref[h, 1, r, :] = jnp.where(lq, one, v2)

        @pl.loop(0, npair)
        def _(h):
            cq = pl.ds(pl.multiple_of(h * 128, 128), 128)
            q2 = jn_ref[r, cq]
            qs = [jnp.where(lq, q2, oh), jnp.where(lq, oh, q2)]
            outs, exts = [], []
            for e in range(2):
                sd = jnp.where(tri, dot_nt(qs[e], ks_ref[h, e, r, :]), NEG)
                peak = jnp.max(sd, axis=1, keepdims=True)
                if i:
                    so = dot_nt(qs[e], ks_ref[h, e, 0 : n - BQ, :])
                    peak = jnp.maximum(peak, jnp.max(so, axis=1, keepdims=True))
                    po = jnp.exp2((so - peak) * EXPC).astype(BF)
                pd = jnp.exp2((sd - peak) * EXPC).astype(BF)
                acc = dot(pd, vs_ref[h, e, r, :])
                if i:
                    acc = acc + dot(po, vs_ref[h, e, 0 : n - BQ, :])
                outs.append(acc)
                tot = acc[:, HD : HD + 1] if e == 0 else acc[:, 0:1]
                exts.append(extra(ohf, -(peak + jnp.log(tot) * (1.0 / SCALE)), 3))
            num = jnp.where(lq, outs[0], outs[1])
            den = pltpu.roll(jnp.where(lq, outs[1], outs[0]), HD, 1)
            att_ref[r, cq] = (num / den).astype(BF)
            ext_ref[r, cq] = jnp.where(lq, exts[1], exts[0]).astype(BF)
            for hh in range(npair):
                if agenda[("h", i, hh)]:

                    @pl.when(h == hh)
                    def _():
                        at_point(("h", i, hh))

    x_save = pltpu.make_async_copy(x_ref, x_out, osem.at[0])
    att_save = pltpu.make_async_copy(att_ref, att_out, osem.at[1])
    ext_save = pltpu.make_async_copy(ext_ref, ext_out, osem.at[2])
    for copy in (x_save, att_save, ext_save):
        copy.start()

    gain2, shift2 = vecs_ref[G2 : G2 + 1, :], vecs_ref[B2 : B2 + 1, :]

    @pl.loop(0, nb)
    def _(i):
        r = rows_of(i, BQ)
        hid = x_ref[r, :].astype(F32) + (dot(att_ref[r, :], wo_ref[...]) + vecs_ref[OB : OB + 1, :])
        hid_ref[r, :] = hid
        unit, _inv = norm_stats(hid)
        n2_ref[r, :] = (unit * gain2 + shift2).astype(BF)
        acc_ref[r, :] = hid + vecs_ref[PB : PB + 1, :]

    hid_save = pltpu.make_async_copy(hid_ref, hid_out, osem.at[3])
    n2_save = pltpu.make_async_copy(n2_ref, n2_out, osem.at[4])
    hid_save.start()
    n2_save.start()

    def gelu_save(n):
        return (
            pltpu.make_async_copy(act_ref.at[n % 2], act_out.at[n], asem.at[0, n]),
            pltpu.make_async_copy(der_ref.at[n % 2], der_out.at[n], asem.at[1, n]),
        )

    for n, step in closing:
        act(n, step)
    own_load(2).wait()
    own_load(3).wait()
    other_save(2).start()
    other_save(3).start()
    for n in range(nf):
        if n >= 2:
            for copy in gelu_save(n - 2):
                copy.wait()
        c = slice(n * width, (n + 1) * width)

        @pl.loop(0, nb)
        def _(i):
            r = rows_of(i, BQ)
            act, der = gelu_both(dot(n2_ref[r, :], wf_ref[:, c]) + vecs_ref[FB + n : FB + n + 1, :])
            act = act.astype(BF)
            act_ref[n % 2, r, :] = act
            der_ref[n % 2, r, :] = der.astype(BF)
            total = acc_ref[r, :] + dot(act, wp_ref[c, :])
            if n < nf - 1:
                acc_ref[r, :] = total
            else:
                obf_ref[r, :] = total.astype(BF)

        for copy in gelu_save(n):
            copy.start()
    out_save = pltpu.make_async_copy(obf_ref, out_out, osem.at[5])
    out_save.start()

    for i in range(nb):
        pack_own(cot_ref, co_ref, i)

    c_copy.wait_recv()

    @pl.loop(0, nb)
    def _(i):
        cot_ref[rows_of(i, BQ), :] = merged(cot_ref, cr_ref, i)

    cot_save = pltpu.make_async_copy(cot_ref, cot_out, osem.at[6])
    cot_save.start()
    for n in range(nparts):
        for step in range(hops(n)):
            chain(n, step).wait_send()
    for i in range(nb):
        x_chunk(i).wait_send()
        for b in range(3):
            joined_save(i, b).wait()
    c_copy.wait_send()
    for n in range(4):
        other_save(n).wait()
    for n in range(max(0, nf - 2), nf):
        for copy in gelu_save(n):
            copy.wait()
    for copy in (x_save, att_save, ext_save, hid_save, n2_save, out_save, cot_save):
        copy.wait()


WAYS = [(2, 1), (1, 2), (2, 1), (1, 2), (3, 2, 1), (3, 1, 2), (3, 2, 1), (3, 1, 2)]


def front(lens, xin, cin, small, wq, wo, wf, wp):
    slots, rows, width = xin.shape
    ff = wf.shape[1]
    nf = ff // width
    nb = rows // BQ
    s = jax.ShapeDtypeStruct
    v = pltpu.VMEM
    act = s((rows, width), BF)
    nparts = len(WAYS)
    return pl.pallas_call(
        front_body,
        name="front",
        out_shape=(
            act, s((3, rows, width), BF), act, act, s((rows, width), F32), act, s((nf, rows, width), BF), s((nf, rows, width), BF),
            act, act, s(wq.shape, BF), s(wo.shape, BF), s(wf.shape, BF), s(wp.shape, BF), s((16, width), F32),
        ),
        in_specs=[SMEM] + anyspecs(2) + vspecs(9) + anyspecs(4),
        out_specs=tuple(anyspecs(14) + vspecs(1)),
        scratch_shapes=[
            v((width, 3 * width), BF), v((width, width), BF), v((width, ff), BF), v((ff, width), BF),
            v((slots, rows, width), BF), v((rows, width), BF), v((rows, width), BF),
            v((slots, rows, width), BF), v((rows, width), BF), v((rows, width), BF),
            v((rows, width), BF), v((rows, width), BF), v((16, width // 2), F32), v((2, 16, width // 2), F32),
            v((rows, 3 * width), BF), v((width // 128, 2, rows, 128), BF), v((width // 128, 2, rows, 128), BF),
            v((rows, width), BF), v((rows, width), BF), v((rows, width), F32), v((rows, width), BF),
            v((2, rows, width), BF), v((2, rows, width), BF), v((rows, width), F32), v((rows, width), BF),
            DMA((nparts, 5)), DMA((nparts, 5)), DMA((4,)), DMA((4,)), DMA((nb,)), DMA((nb,)), DMA((2,)), DMA((2,)), DMA((2,)),
            DMA((7,)), DMA((nb, 3)), DMA((2, nf)),
        ],
        compiler_params=params(collective_id=0, has_side_effects=True),
        cost_estimate=cost(40e9, 60e6, 12e6),
    )(lens, xin, cin, *small, wq, wo, wf, wp)


def back_body(
    bits, lens_ref, vecs_ref, x_in, joined_in, att_in, ext_in, hid_in, n2_in, act_in, der_in, out_in, cot_in,
    wq_own, wo_own, wf_own, wp_own, wq_oth, wo_oth, wf_oth, wp_oth,
    res_out, dx_out, dxr_out, outr_out, sums_ref,
    wf_ref, wp_ref, wo_ref, wq_ref, cot_ref, n2_ref, act_ref, der_ref, gpre_ref, acc_ref, hid_ref, att_ref,
    gm_ref, r0_ref, rb_ref, res_ref, sm_ref, smb_ref, smr_ref,
    wsem, lsem, asem, hsem, ssem, rsem, msem, mrem, osem, dsem, drem, vsem, fsem,
):
    rep, shard = place()
    core = rep & 1
    rows, width = cot_ref.shape
    hw = width // 2
    nb = rows // BQ
    nf = act_in.shape[0]
    npair = width // 128
    m = bits - 1
    sibling, across = (rep ^ 1, shard), (rep, 1 - shard)
    peers = {0: across}
    for t in range(1, bits):
        peers[t] = (rep ^ (1 << t), shard)
    plan = Plan(lens_ref, shard, rows)
    bounds = plan.bounds()

    def weight_loads(own, oth, dst, into):
        half = own.shape[0]
        for n, (src, which) in enumerate(((own, shard), (oth, 1 - shard))):
            yield n, src, dst.at[pl.ds(pl.multiple_of(into + which * half, 16), half), :]

    def fc_loads(j):
        for n, src, dst in weight_loads(wf_own, wf_oth, wf_ref, j * width):
            for part in range(2):
                here = pl.ds((part * nf + j) * hw, hw)
                yield pltpu.make_async_copy(src.at[:, here], dst.at[:, pl.ds(part * hw, hw)], wsem.at[0, n, part, j])

    def proj_loads(j):
        for n, (src, which) in enumerate(((wp_own, shard), (wp_oth, 1 - shard))):
            into = pl.ds(pl.multiple_of(j * width + which * hw, 16), hw)
            yield pltpu.make_async_copy(src.at[pl.ds(j * hw, hw), :], wp_ref.at[into, :], wsem.at[1, n, 0, j])

    def gelu_loads(j):
        for k, (src, dst) in enumerate(((act_in, act_ref), (der_in, der_ref))):
            for part in range(2):
                block = part * (nf // 2) + j // 2
                here = pl.ds((j % 2) * hw, hw)
                yield pltpu.make_async_copy(src.at[block, :, here], dst.at[j % 2, :, pl.ds(part * hw, hw)], asem.at[k, part, j])

    def plain(n, src, dst):
        return pltpu.make_async_copy(src, dst, lsem.at[n])

    cot_load, n2_load, att_load = plain(0, cot_in, cot_ref), plain(1, n2_in, n2_ref), plain(2, att_in, att_ref)
    wo_loads = [pltpu.make_async_copy(s_, d_, wsem.at[2, n, 0, 0]) for n, s_, d_ in weight_loads(wo_own, wo_oth, wo_ref, 0)]
    wq_loads = [pltpu.make_async_copy(s_, d_, wsem.at[2, n, 0, 1]) for n, s_, d_ in weight_loads(wq_own, wq_oth, wq_ref, 0)]
    x_load, ext_load = plain(3, x_in, act_ref.at[0]), plain(4, ext_in, der_ref.at[0])
    joined_loads = [plain(5 + b, joined_in.at[b], wf_ref.at[pl.ds(b * rows, rows), :]) for b in range(3)]

    def hid_load(i):
        return pltpu.make_async_copy(hid_in.at[pl.ds(i * BQ, BQ), :], hid_ref.at[i % 2], hsem.at[i])

    cot_load.start()
    for j in range(2):
        for copy in list(proj_loads(j)) + list(gelu_loads(j)) + list(fc_loads(j)):
            copy.start()
        if j == 0:
            n2_load.start()
    greet([sibling, across] + [peers[t] for t in range(1, bits)])

    per = gm_ref.shape[3] // PIECE
    count = 3 * per
    last = 3 + 2 * m
    rest = tuple(range(3, bits))
    orders = [PATHS[k] + rest + ((0,) if 0 not in PATHS[k] else ()) for k in range(count)]

    def source(k, away):
        a, at = k // per, pl.ds((k % per) * PIECE, PIECE)
        return gm_ref.at[away, a, :, at, :] if a < 2 else gm_ref.at[1, away, :, at, :]

    def held(k, i):
        half, first, size = None, 0, PIECE
        for d in orders[k][:i]:
            if d == 0:
                half = shard
            else:
                size //= 2
                first = first + ((rep >> d) & 1) * size
        return half, first, size

    def at_rows(first, size):
        return pl.ds(pl.multiple_of(first, 16), size)

    def landing(k, i):
        d = orders[k][i]
        half, _first, size = held(k, i + 1)
        before = sum(PIECE >> (n + 1) for n in range(len([e for e in orders[k][:i] if e])))
        if d == 0:
            return rb_ref.at[k, 0, pl.ds(before, size), :]
        at = pl.ds(before, size)
        return rb_ref.at[k, :, at, :] if half is None else rb_ref.at[k, 1, at, :]

    def leaving(k, i):
        d = orders[k][i]
        half, first, size = held(k, i)
        own = source(k, 0)
        if d == 0:
            return own.at[1 - shard, at_rows(first, size), :]
        size //= 2
        at = at_rows(first + (1 - ((rep >> d) & 1)) * size, size)
        return own.at[:, at, :] if half is None else own.at[half, at, :]

    def copy(k, step):
        sems = (ssem.at[step, k], rsem.at[step, k])
        if step == 0:
            return remote(source(k, 1), r0_ref.at[k], *sems, sibling)
        if step <= m + 1:
            return remote(leaving(k, step - 1), landing(k, step - 1), *sems, peers[orders[k][step - 1]])
        if step <= 2 * m + 1:
            back = [d for d in orders[k] if d]
            t = m - (step - m - 2)
            size = PIECE >> t
            first = 0
            for n in range(t):
                first = first + ((rep >> back[n]) & 1) * (PIECE >> (n + 1))
            here = res_ref.at[k, at_rows(first, size), :]
            return remote(here, here, *sems, peers[back[t - 1]])
        return remote(res_ref.at[k], res_out.at[core, k], *sems, sibling)

    def keep(k):
        return pltpu.make_async_copy(res_ref.at[k], res_out.at[core, k], fsem.at[k])

    def add(dst, first, other, base, size, out=None):
        chunk = min(size, 64)

        @pl.loop(0, size // chunk)
        def _(i):
            at = pl.ds(pl.multiple_of(first + i * chunk, 16), chunk)
            total = dst[at, :].astype(F32) + other[pl.ds(pl.multiple_of(base + i * chunk, 16), chunk), :].astype(F32)
            (dst if out is None else out)[at, :] = total.astype(BF)

    def act_step(k, step):
        if step:
            copy(k, step - 1).wait_recv()
        own = source(k, 0)
        if step == 1:
            for h in range(2):
                add(own.at[h], 0, r0_ref.at[k, h], 0, PIECE)
        elif 2 <= step <= m + 2:
            i = step - 2
            half, first, size = held(k, i + 1)
            land = landing(k, i)
            if half is None:
                for h in range(2):
                    add(own.at[h], first, land.at[h], 0, size)
            else:
                add(own.at[half], first, land, 0, size, res_ref.at[k] if i == m else None)
        if step < last:
            copy(k, step).start()
        if step == last - 1:
            keep(k).start()

    def small_copy(step):
        src = sm_ref if step == 0 else smb_ref.at[step - 1]
        return remote(src, smr_ref.at[step], msem.at[step], mrem.at[step], small_peers[step])

    def small_step(step):
        if step:
            small_copy(step - 1).wait_recv()
            before = sm_ref[...] if step == 1 else smb_ref[step - 2]
            total = before + smr_ref[step - 1]
            if step == 2 + m:
                sums_ref[...] = total
            else:
                smb_ref[step - 1] = total
        if step < 2 + m:
            small_copy(step).start()

    def dx_chunk(i):
        at = pl.ds(i * BQ, BQ)
        return remote(dxb_ref.at[at, :], dxr_out.at[at, :], dsem.at[i], drem.at[i], across)

    def dx_step(i):
        if i:
            dx_chunk(i - 1).wait_send()
        if i < nb:
            dx_chunk(i).start()

    def act(c, step):
        if c == "small":
            small_step(step)
        elif c == "dx":
            dx_step(step)
        else:
            act_step(c, step)

    small_peers = [sibling, across] + [peers[t] for t in range(1, bits)]
    xb_ref, eb_ref, n1_ref, dxb_ref = act_ref.at[0], der_ref.at[0], der_ref.at[1], act_ref.at[1]

    points, now = [], 5.0
    for name, long in (
        [(("ff", j, n), 4.1) for j in range(nf) for n in range(2)]
        + [(("hid", i), 1.6) for i in range(nb)]
        + [("go", 2.0)]
        + [p for t in range(THIRDS) for p in [(("at", t, p, i), 0.72 * (i + 1)) for p in range(npair // THIRDS) for i in range(nb)] + [(("gw", t), 2.0)]]
        + [(("dx", i), 2.0) for i in range(nb)]
    ):
        now += long
        points.append((name, now))
    chains, ready = {}, {}
    half_mb = 2 * PIECE * hw / 1e6
    for k in range(count):
        steps, size = [("core", 2 * half_mb / CORE_RATE, 1.0)], 2 * half_mb
        for d in orders[k]:
            size /= 2
            steps.append((link_of(d)[0], size / LINK_RATE * link_of(d)[1], 1.5))
        size = half_mb / (1 << m)
        for d in reversed([d for d in orders[k] if d]):
            steps.append((link_of(d)[0], size / LINK_RATE * link_of(d)[1], 1.5))
            size *= 2
        chains[k] = steps + [("core", half_mb / CORE_RATE, 1.0)]
        ready[k] = ("ff", 1 + k % per, 1) if k < 2 * per else ("gw", k - 2 * per)
    small_us = 24 * width * 4e-6 / LINK_RATE
    chains["small"] = [("core", 0.5, 1.0), (0, small_us, 1.5)] + [(link_of(d)[0], small_us * link_of(d)[1], 1.5) for d in range(1, bits)]
    chains["dx"] = [(0, BQ * width * 2e-6 / LINK_RATE, 0.0)] * nb
    ready["small"], ready["dx"] = ("dx", nb - 1), ("dx", 0)
    agenda, tail = timetable(points, chains, ready, {0: 5.0 + rows * width * 2e-6 / LINK_RATE})

    def at_point(name):
        for c, step in agenda[name]:
            act(c, step)

    gbase = 16
    sm_ref[...] = jnp.zeros_like(sm_ref)

    @pl.loop(0, nb)
    def _(i):
        acc_ref[rows_of(i, BQ), :] = jnp.zeros((BQ, width), F32)

    out_copy = remote(out_in, outr_out, osem.at[0], osem.at[1], across)
    out_copy.start()
    cot_load.wait()
    n2_load.wait()
    for j in range(nf):
        for c in list(proj_loads(j)) + list(gelu_loads(j)) + list(fc_loads(j)):
            c.wait()
        if j + 2 < nf:
            for c in list(proj_loads(j + 2)) + list(fc_loads(j + 2)):
                c.start()
        here = slice(j * width, (j + 1) * width)

        @pl.loop(0, nb)
        def _(i):
            r = rows_of(i, BQ)
            gact = dot_nt(cot_ref[r, :], wp_ref[here, :])
            gpre = (gact * der_ref[j % 2, r, :].astype(F32)).astype(BF)
            gpre_ref[r, :] = gpre
            sm_ref[gbase + j : gbase + j + 1, :] += jnp.sum(gpre.astype(F32), axis=0, keepdims=True)
            acc_ref[r, :] += dot_nt(gpre, wf_ref[here, :])

        at_point(("ff", j, 0))
        for h in range(2):
            gp = dot_tn(act_ref[j % 2, :, h * hw : (h + 1) * hw], cot_ref[...]).astype(BF)
            gf = dot_tn(n2_ref[:, h * hw : (h + 1) * hw], gpre_ref[...]).astype(BF)
            for c in range(2):
                gm_ref[c ^ core, 1, h, j * hw : (j + 1) * hw, :] = gp[:, c * hw : (c + 1) * hw]
                gm_ref[c ^ core, 0, h, j * hw : (j + 1) * hw, :] = gf[:, c * hw : (c + 1) * hw]
        if j + 2 < nf:
            for c in gelu_loads(j + 2):
                c.start()
        elif j + 2 == nf:
            for c in [x_load, ext_load, att_load] + wo_loads + wq_loads:
                c.start()
            hid_load(0).start()
            hid_load(1).start()
        at_point(("ff", j, 1))

    for c in joined_loads:
        c.start()
    for c in [att_load] + wo_loads:
        c.wait()
    gain2 = vecs_ref[G2 : G2 + 1, :]
    gatt_ref = cot_ref
    for i in range(nb):
        r = slice(i * BQ, (i + 1) * BQ)
        hid_load(i).wait()
        unit, inv = norm_stats(hid_ref[i % 2])
        gn2 = acc_ref[r, :]
        gy = cot_ref[r, :].astype(F32)
        ghid = gy + norm_back(gn2, unit, inv, gain2)
        if i + 2 < nb:
            hid_load(i + 2).start()
        acc_ref[r, :] = ghid
        low = ghid.astype(BF)
        gpre_ref[r, :] = low
        gatt_ref[r, :] = dot_nt(low, wo_ref[...]).astype(BF)
        sm_ref[0:1, :] += jnp.sum(gn2 * unit, axis=0, keepdims=True)
        sm_ref[1:2, :] += jnp.sum(gn2, axis=0, keepdims=True)
        sm_ref[2:3, :] += jnp.sum(gy, axis=0, keepdims=True)
        sm_ref[3:4, :] += jnp.sum(low.astype(F32), axis=0, keepdims=True)
        at_point(("hid", i))
    x_load.wait()
    gain1, shift1 = vecs_ref[G1 : G1 + 1, :], vecs_ref[B1 : B1 + 1, :]

    @pl.loop(0, nb)
    def _(i):
        r = rows_of(i, BQ)
        unit, _inv = norm_stats(xb_ref[r, :].astype(F32))
        n1_ref[r, :] = (unit * gain1 + shift1).astype(BF)

    for k in range(2 * per):
        copy(k, 0).wait_send()
    for h in range(2):
        go = dot_tn(att_ref[:, h * hw : (h + 1) * hw], gpre_ref[...]).astype(BF)
        for c in range(2):
            gm_ref[1, c ^ core, h, 0:hw, :] = go[:, c * hw : (c + 1) * hw]
    at_point("go")
    for c in joined_loads + [ext_load]:
        c.wait()

    lq = lane_half((BQ, 128))
    tri = lax.broadcasted_iota(jnp.int32, (BQ, BQ), 0) <= lax.broadcasted_iota(jnp.int32, (BQ, BQ), 1)
    left = lane_half((rows, 128))
    ones = lax.broadcasted_iota(jnp.int32, (rows, 128), 1) % HD
    ones = (ones >= 3) & (ones < 6)
    tcols = width // THIRDS
    here_at = lambda t, p, i: agenda[("at", t, p, i)]

    def head_pair(t, p):
        h = t * (npair // THIRDS) + p
        col = pl.ds(pl.multiple_of(h * 128, 128), 128)
        k2 = wf_ref[rows : 2 * rows, col]
        v2 = wf_ref[2 * rows : 3 * rows, col]
        zero = jnp.zeros_like(k2)
        kx = jnp.where(ones, 1.0, other_segment(bounds, 0, rows)).astype(BF)
        vx = jnp.where(ones, 1.0, 0.0).astype(BF)
        ks = [jnp.where(left, k2, kx), jnp.where(left, kx, k2)]
        vs = [jnp.where(left, v2, vx), jnp.where(left, vx, v2)]
        km = [jnp.where(left, k2, zero), jnp.where(left, zero, k2)]
        hid_ref[...] = jnp.zeros_like(hid_ref)
        for i in range(nb):
            r = slice(i * BQ, (i + 1) * BQ)
            q2 = wf_ref[r, col]
            g2 = gatt_ref[r, col]
            ext = eb_ref[r, col]
            zq = jnp.zeros_like(q2)
            prod = g2.astype(F32) * att_ref[r, col].astype(F32)
            d0 = jnp.sum(jnp.where(lq, prod, 0.0), axis=1, keepdims=True)
            d1 = jnp.sum(jnp.where(lq, 0.0, prod), axis=1, keepdims=True)
            zf = jnp.zeros((BQ, 128), F32)
            qs = [jnp.where(lq, q2, ext), jnp.where(lq, ext, q2)]
            gs = [jnp.where(lq, g2, extra(zf, -d0, 3).astype(BF)), jnp.where(lq, extra(zf, -d1, 3).astype(BF), g2)]
            qm = [jnp.where(lq, q2, zq), jnp.where(lq, zq, q2)]
            gm = [jnp.where(lq, g2, zq), jnp.where(lq, zq, g2)]
            dq = None
            for u in range(i + 1):
                b = slice(u * BQ, (u + 1) * BQ)
                dk = dv = None
                for e in range(2):
                    st = dot_nt(ks[e][b], qs[e])
                    if u == i:
                        st = jnp.where(tri, st, NEG)
                    pt = jnp.exp2(st * EXPC)
                    dst = (pt * dot_nt(vs[e][b], gs[e])).astype(BF)
                    one, two, three = dot(pt.astype(BF), gm[e]), dot(dst, qm[e]), dot_tn(dst, km[e][b])
                    dv = one if dv is None else dv + one
                    dk = two if dk is None else dk + two
                    dq = three if dq is None else dq + three
                hid_ref[1, :, u * 128 : (u + 1) * 128] += dv
                hid_ref[0, :, u * 128 : (u + 1) * 128] += dk
            wp_ref[r, col] = (dq * SCALE).astype(BF)
            for tt in range(THIRDS):
                for pp in range(npair // THIRDS):
                    if here_at(tt, pp, i):

                        @pl.when((t == tt) & (p == pp))
                        def _():
                            for c, step in here_at(tt, pp, i):
                                act(c, step)

        for u in range(nb):
            wp_ref[rows + u * BQ : rows + (u + 1) * BQ, col] = (hid_ref[0, :, u * 128 : (u + 1) * 128] * SCALE).astype(BF)
            wp_ref[2 * rows + u * BQ : 2 * rows + (u + 1) * BQ, col] = hid_ref[1, :, u * 128 : (u + 1) * 128].astype(BF)

    @pl.loop(0, THIRDS)
    def _(t):
        @pl.loop(0, npair // THIRDS)
        def _(p):
            head_pair(t, p)

        cols = pl.ds(pl.multiple_of(t * tcols, 128), tcols)
        into = pl.ds(pl.multiple_of(hw + t * hw, 128), hw)
        cut = hw - tcols
        for h in range(2):
            n1h = n1_ref[:, h * hw : (h + 1) * hw]
            gq, gk, gv = [dot_tn(n1h, wp_ref[b * rows : (b + 1) * rows, cols]).astype(BF) for b in range(3)]
            gm_ref[1, core, h, into, 0:tcols] = gq
            gm_ref[1, core, h, into, tcols:hw] = gk[:, 0:cut]
            gm_ref[1, 1 - core, h, into, 0:cut] = gk[:, cut:tcols]
            gm_ref[1, 1 - core, h, into, cut:hw] = gv
        for b in (0, 2):
            sm_ref[8 + b : 9 + b, cols] = jnp.sum(wp_ref[b * rows : (b + 1) * rows, cols].astype(F32), axis=0, keepdims=True)
        for tt in range(THIRDS):
            if agenda[("gw", tt)]:

                @pl.when(t == tt)
                def _():
                    at_point(("gw", tt))

    for c in wq_loads:
        c.wait()

    for i in range(nb):
        r = slice(i * BQ, (i + 1) * BQ)
        gn1 = dot_nt(wp_ref[0:rows][r], wq_ref[:, 0:width])
        for b in (1, 2):
            gn1 = gn1 + dot_nt(wp_ref[b * rows + i * BQ : b * rows + (i + 1) * BQ, :], wq_ref[:, b * width : (b + 1) * width])
        unit, inv = norm_stats(xb_ref[r, :].astype(F32))
        dxb_ref[r, :] = (acc_ref[r, :] + norm_back(gn1, unit, inv, gain1)).astype(BF)
        sm_ref[11:12, :] += jnp.sum(gn1 * unit, axis=0, keepdims=True)
        sm_ref[12:13, :] += jnp.sum(gn1, axis=0, keepdims=True)
        at_point(("dx", i))
    dx_save = plain(8, dxb_ref, dx_out)
    dx_save.start()

    for c, step in tail:
        act(c, step)
    for k in range(count):
        for step in range(last):
            if step or k >= 2 * per:
                copy(k, step).wait_send()
        keep(k).wait()
    for step in range(2 + m):
        small_copy(step).wait_send()
    out_copy.wait()
    for i in range(nb):
        dx_chunk(i).wait_recv()
    dx_save.wait()


THIRDS = 3
CORE_RATE, LINK_RATE = 0.15, 0.045
PATHS = [(1, 0, 2), (1, 0, 2), (1, 0, 2), (2, 1), (0, 1, 2), (1, 2), (0, 1, 2), (0, 1, 2), (0, 1, 2)]


def back(bits, lens, vecs, saved, own, oth):
    x, joined, att, ext, hid, n2, act, der, out, cot = saved
    rows, width = x.shape
    nf = act.shape[0]
    nb = rows // BQ
    hw = width // 2
    m = bits - 1
    count = 3 * (nf * hw // PIECE)
    s = jax.ShapeDtypeStruct
    v = pltpu.VMEM
    sums = (24, width)
    return pl.pallas_call(
        functools.partial(back_body, bits),
        name="back",
        out_shape=(s((2, count, PIECE, hw), BF), s((rows, width), BF), s((rows, width), BF), s((rows, width), BF), s(sums, F32)),
        in_specs=[SMEM] + vspecs(1) + anyspecs(18),
        out_specs=tuple(anyspecs(4) + vspecs(1)),
        scratch_shapes=[
            v((nf * width, width), BF), v((nf * width, width), BF), v((width, width), BF), v((width, 3 * width), BF),
            v((rows, width), BF), v((rows, width), BF), v((2, rows, width), BF), v((2, rows, width), BF), v((rows, width), BF),
            v((rows, width), F32), v((2, BQ, width), F32), v((rows, width), BF),
            v((2, 2, 2, nf * hw, hw), BF), v((count, 2, PIECE, hw), BF), v((count, 2, PIECE, hw), BF), v((count, PIECE, hw), BF),
            v(sums, F32), v((m + 1,) + sums, F32), v((m + 2,) + sums, F32),
            DMA((3, 2, 2, nf)), DMA((9,)), DMA((2, 2, nf)), DMA((nb,)), DMA((3 + 2 * m, count)), DMA((3 + 2 * m, count)),
            DMA((m + 2,)), DMA((m + 2,)), DMA((2,)), DMA((nb,)), DMA((nb,)), DMA((1,)), DMA((count,)),
        ],
        compiler_params=params(collective_id=1, has_side_effects=True),
        cost_estimate=cost(60e9, 60e6, 8e6),
    )(lens, vecs, *saved, *own, *oth)


def finish_body(
    lens_ref, deal_ref, sums_ref, res_in, dx_in, dxr_in, out_in, outr_in, y_out, d_out, *rest
):
    outs, scratch = rest[:13], rest[13:]
    (o_g1, o_b1, o_qkv, o_qb, o_vb, o_wo, o_ob, o_g2, o_b2, o_fc, o_fb, o_proj, o_pb) = outs
    res_ref, src_ref, y_ref, qkv_ref, wo_ref, fc_ref, proj_ref, lsem, ssem = scratch
    shard = lax.axis_index("shard")
    rows, width = src_ref.shape[1:]
    hw = width // 2
    nb = rows // BQ
    slots = y_ref.shape[1]
    nf = fc_ref.shape[1] // width
    plan = Plan(lens_ref, shard, rows)
    loads = [pltpu.make_async_copy(a, src_ref.at[n], lsem.at[n]) for n, a in enumerate((out_in, outr_in, dx_in, dxr_in))]
    per = res_in.shape[1] // 3
    pieces = [pltpu.make_async_copy(res_in.at[:, pl.ds(per * a, per)], res_ref.at[:, pl.ds(per * a, per)], lsem.at[4 + a]) for a in range(3)]
    for copy in loads + pieces:
        copy.start()
    own = pl.ds(pl.multiple_of(shard * hw, 128), hw)
    for ref, row in ((o_g1, 11), (o_b1, 12), (o_qb, 8), (o_vb, 10), (o_ob, 3), (o_g2, 0), (o_b2, 1), (o_pb, 2)):
        ref[...] = sums_ref[row, own]
    for j in range(nf):
        o_fb[j * hw : (j + 1) * hw] = sums_ref[16 + j, own]

    def save(n, src, dst):
        return pltpu.make_async_copy(src, dst, ssem.at[n])

    saves = []
    for g in range(2):
        loads[2 * g].wait()
        loads[2 * g + 1].wait()
        for j in range(slots):
            q = slots * shard + j
            if g == 0:
                q = sum(jnp.where(q == n, deal_ref[0, n], 0) for n in range(2 * slots))
            side, offset, size = plan.where(q)

            @pl.loop(0, nb)
            def _(i):
                low, pick = window_pick(rows, i * BQ + offset, BQ)
                row = i * BQ + lax.broadcasted_iota(jnp.int32, pick.shape, 0)
                pick = jnp.where(pick & (row < size), 1.0, 0.0).astype(BF)
                y_ref[g, j, rows_of(i, BQ), :] = dot(pick, src_ref[2 * g + side, pl.ds(low, WINDOW), :]).astype(BF)

            saves.append(save(2 * g + j, y_ref.at[g, j], (y_out, d_out)[g].at[j]))
            saves[-1].start()
    block = lambda c, a, n, r, size: res_ref[c, a * per + (n * hw + r) // PIECE, (n * hw + r) % PIECE : (n * hw + r) % PIECE + size, :]
    for a, (dst, out) in enumerate(((fc_ref, o_fc), (proj_ref, o_proj), (qkv_ref, o_qkv))):
        pieces[a].wait()
        for n in range(nf):
            for c in range(2):
                for r in range(0, hw, 128):
                    value = block(c, a, n, r, 128).astype(F32)
                    at = slice(r, r + 128)
                    if a == 0:
                        fc_ref[at, (c * nf + n) * hw : (c * nf + n + 1) * hw] = value
                    elif a == 1:
                        proj_ref[n * hw + r : n * hw + r + 128, c * hw : (c + 1) * hw] = value
                    elif n == 0:
                        wo_ref[at, c * hw : (c + 1) * hw] = value
                    else:
                        tcols = width // THIRDS
                        cut, lead = hw - tcols, (n - 1) * tcols
                        if c == 0:
                            qkv_ref[at, lead : lead + tcols] = value[:, 0:tcols]
                            qkv_ref[at, width + lead : width + lead + cut] = value[:, tcols:hw]
                        else:
                            qkv_ref[at, width + lead + cut : width + lead + tcols] = value[:, 0:cut]
                            qkv_ref[at, 2 * width + lead : 2 * width + lead + tcols] = value[:, cut:hw]
        saves.append(save(4 + a, dst, out))
        saves[-1].start()
    saves.append(save(7, wo_ref, o_wo))
    saves[-1].start()
    for copy in saves:
        copy.wait()


def finish(lens, deal, sums, res, dx, dxr, out, outr, slots):
    rows, width = dx.shape
    hw = width // 2
    nf = res.shape[1] * PIECE // 3 // hw
    s = jax.ShapeDtypeStruct
    v = pltpu.VMEM
    vec, act = s((hw,), F32), s((slots, rows, width), BF)
    wide = lambda a, b: s((a, b), F32)
    vs, an = vspecs(1), anyspecs(1)
    return pl.pallas_call(
        finish_body,
        name="finish",
        out_shape=(act, act, vec, vec, wide(hw, 3 * width), vec, vec, wide(hw, width), vec, vec, vec, wide(hw, nf * width),
                   s((nf * hw,), F32), wide(nf * hw, width), vec),
        in_specs=[SMEM, SMEM] + vs + anyspecs(5),
        out_specs=tuple(an * 2 + vs * 2 + an + vs * 2 + an + vs * 3 + an + vs + an + vs),
        scratch_shapes=[
            v(res.shape, BF), v((4, rows, width), BF), v((2, slots, rows, width), BF),
            v((hw, 3 * width), F32), v((hw, width), F32), v((hw, nf * width), F32), v((nf * hw, width), F32), DMA((7,)), DMA((8,)),
        ],
        compiler_params=params(),
        cost_estimate=cost(8e9, 34e6),
    )(lens, deal, sums, res, dx, dxr, out, outr)


def local(bits, layer_in, cotangent, lengths, dealing, g1, b1, wqkv, qb, vb, wout, ob, g2, b2, wfc, bfc, wproj, pb):
    slots, rows, width = layer_in.shape
    own = (wqkv, wout, wfc, wproj)
    got = front(lengths, layer_in, cotangent, (g1, b1, qb, vb, ob, g2, b2, pb, bfc), *own)
    saved, oth, vecs = got[:10], got[10:14], got[14]
    res, dx, dxr, outr, sums = back(bits, lengths, vecs, saved, own, oth)
    return finish(lengths, dealing, sums, res, dx, dxr, saved[8], outr, slots)


def solution(mesh):
    both, one = P(("rep", "shard"), None, None), P("shard")
    mat = P("shard", None)
    in_specs = (both, both, P("rep", None), P("rep", None), one, one, mat, one, one, mat, one, one, one, mat, one, mat, one)
    out_specs = (both, both, one, one, mat, one, one, mat, one, one, one, mat, one, mat, one)
    bits = mesh.shape["rep"].bit_length() - 1
    return jax.shard_map(functools.partial(local, bits), mesh=mesh, in_specs=in_specs, out_specs=out_specs, check_vma=False)
```

```python
import functools

import jax
import jax.numpy as jnp
from jax import lax
from jax.experimental import pallas as pl
from jax.experimental.pallas import tpu as pltpu
from jax.sharding import PartitionSpec as P

HD = 64
BQ = 256
EPS = 1e-05
BF = jnp.bfloat16
F32 = jnp.float32
NEG = -1e30
LOG2E = 1.4426950408889634
SCALE = HD**-0.5
EXPC = SCALE * LOG2E
VLIM = 66_900_000
GELU_A = 0.7978845608028654
GELU_B = 0.044715
MESH = pl.DeviceIdType.MESH
PIECE = 512
WINDOW = 384
G1, B1, QB, VB, OB, G2, B2, PB, FB = range(9)


def dot(a, b):
    return jnp.dot(a, b, preferred_element_type=F32)


def dot_tn(a, b):
    return lax.dot_general(a, b, (((0,), (0,)), ((), ())), preferred_element_type=F32)


def dot_nt(a, b):
    return lax.dot_general(a, b, (((1,), (1,)), ((), ())), preferred_element_type=F32)


def norm_stats(v):
    mean = jnp.mean(v, axis=-1, keepdims=True)
    cen = v - mean
    inv = lax.rsqrt(jnp.mean(cen * cen, axis=-1, keepdims=True) + EPS)
    return cen * inv, inv


def norm_back(grad, unit, inv, gain):
    e = grad * gain
    m1 = jnp.mean(e, axis=-1, keepdims=True)
    m2 = jnp.mean(e * unit, axis=-1, keepdims=True)
    return inv * (e - m1 - unit * m2)


def rows_of(i, size):
    return pl.ds(pl.multiple_of(i * size, size), size)


def span(first, size):
    return pl.ds(first if isinstance(first, int) else pl.multiple_of(first, 128), size)


def lane_half(shape):
    return lax.broadcasted_iota(jnp.int32, shape, 1) < HD


def extra(base, v, first):
    hi = v.astype(BF).astype(F32)
    mid = (v - hi).astype(BF).astype(F32)
    lane = lax.broadcasted_iota(jnp.int32, base.shape, 1) % HD
    out = jnp.where(lane == first, hi, base)
    out = jnp.where(lane == first + 1, mid, out)
    return jnp.where(lane == first + 2, v - hi - mid, out)


def vspecs(n):
    return [pl.BlockSpec(memory_space=pltpu.VMEM)] * n


def anyspecs(n):
    return [pl.BlockSpec(memory_space=pl.ANY)] * n


SMEM = pl.BlockSpec(memory_space=pltpu.SMEM)
DMA = pltpu.SemaphoreType.DMA


def params(**kw):
    return pltpu.CompilerParams(vmem_limit_bytes=VLIM, **kw)


def cost(flops, moved, trans=0):
    return pl.CostEstimate(flops=int(flops), bytes_accessed=int(moved), transcendentals=int(trans))


class Plan:
    def __init__(self, lens_ref, shard, rows):
        group = lens_ref.shape[1]
        half = group // 2
        self.half, self.shard, self.rows = half, shard, rows
        self.lens = [lens_ref[0, q] for q in range(group)]
        long = jnp.int32(0)
        for q in range(1, group):
            long = jnp.where(self.lens[q] == rows, q, long)
        self.long = long
        self.home = lax.div(long, jnp.int32(half))
        self.stays = shard == self.home
        self.slot = long & 1
        self.first = half * (1 - self.home)
        self.s0, self.s1 = self.size(self.first), self.size(self.first + 1)
        self.moved = self.size(long ^ 1)

    def size(self, q):
        out = self.lens[0]
        for n in range(1, len(self.lens)):
            out = jnp.where(q == n, self.lens[n], out)
        return out

    def away(self):
        return jnp.where(self.stays, 1 - self.slot, 0)

    def bounds(self):
        return jnp.where(self.stays, self.rows, self.s0), jnp.where(self.stays, self.rows, self.s0 + self.s1)

    def where(self, q):
        start = jnp.where(q == self.first, 0, jnp.where(q == self.first + 1, self.s0, self.s0 + self.s1))
        start = jnp.where(q == self.long, 0, start)
        side = jnp.where(q == self.long, self.home, 1 - self.home) ^ self.shard
        return side, start, self.size(q)


def window_pick(total, first, count):
    low = jnp.clip((first >> 7) << 7, 0, total - WINDOW)
    want = first - low + lax.broadcasted_iota(jnp.int32, (count, WINDOW), 0)
    return pl.multiple_of(low, 128), want == lax.broadcasted_iota(jnp.int32, (count, WINDOW), 1)


def moved_pick(start, i, upto):
    want = i * BQ - start + lax.broadcasted_iota(jnp.int32, (BQ, upto), 0)
    return jnp.where(want == lax.broadcasted_iota(jnp.int32, (BQ, upto), 1), 1.0, 0.0).astype(BF)


def lane_and_segment(bounds, first, rows):
    row = first + lax.broadcasted_iota(jnp.int32, (rows, 128), 0)
    seg = (row >= bounds[0]).astype(jnp.int32) + (row >= bounds[1]).astype(jnp.int32)
    return lax.broadcasted_iota(jnp.int32, (rows, 128), 1) % HD, seg


def own_segment(bounds, first, rows):
    lane, seg = lane_and_segment(bounds, first, rows)
    return jnp.where(lane == seg, 1.0, 0.0)


def other_segment(bounds, first, rows):
    lane, seg = lane_and_segment(bounds, first, rows)
    return jnp.where((lane < 3) & (lane != seg), NEG, 0.0)


def gelu_both(v):
    v2 = v * v
    t = jnp.tanh(v * (GELU_A + (GELU_A * GELU_B) * v2))
    half = 0.5 + 0.5 * t
    return v * half, half + (0.5 * v) * (1.0 - t * t) * (GELU_A + (3.0 * GELU_A * GELU_B) * v2)


def place():
    return lax.axis_index("rep"), lax.axis_index("shard")


def greet(partners):
    barrier = pltpu.get_barrier_semaphore()
    for partner in partners:
        pl.semaphore_signal(barrier, inc=1, device_id=partner, device_id_type=MESH)
    pl.semaphore_wait(barrier, len(partners))


def remote(src, dst, ssem, rsem, to):
    return pltpu.make_async_remote_copy(
        src_ref=src, dst_ref=dst, send_sem=ssem, recv_sem=rsem, device_id=to, device_id_type=MESH
    )


def link_of(d):
    return ((d + 2) // 2 if d else 0), (2 if d > 2 and d % 2 else 1)


def timetable(points, chains, ready, busy):
    free, at, step = dict(busy), {}, {c: 0 for c in chains}
    plan, tail = {name: [] for name, _ in points}, []

    def take(c, now, dest):
        dest.append((c, step[c]))
        if step[c] < len(chains[c]):
            link, long, lag = chains[c][step[c]]
            free[link] = max(now, free.get(link, 0.0)) + long
            at[c] = free[link] + lag
        step[c] += 1

    left = lambda: [c for c in chains if c in at and step[c] <= len(chains[c])]
    for name, now in points:
        for c in chains:
            if ready[c] == name:
                at[c] = now
        while True:
            due = [c for c in left() if at[c] <= now]
            if not due:
                break
            take(min(due, key=lambda c: at[c]), now, plan[name])
    now = points[-1][1]
    while left():
        c = min(left(), key=lambda c: at[c])
        now = max(now, at[c])
        take(c, now, tail)
    return plan, tail


def front_body(
    lens_ref, xin_ref, cin_ref, g1_in, b1_in, qb_in, vb_in, ob_in, g2_in, b2_in, pb_in, fb_in, wq_in, wo_in, wf_in, wp_in,
    x_out, joined_out, att_out, ext_out, hid_out, n2_out, act_out, der_out, out_out, cot_out, wq_out, wo_out, wf_out, wp_out, vecs_ref,
    wq_ref, wo_ref, wf_ref, wp_ref, xo_ref, xs_ref, xr_ref, co_ref, cs_ref, cr_ref, x_ref, cot_ref, small_ref, sm_ref,
    jn_ref, ks_ref, vs_ref, att_ref, ext_ref, hid_ref, n2_ref, act_ref, der_ref, acc_ref, obf_ref,
    wsend, wrecv, wload, wsave, xsend, xrecv, csem, ssem, lsem, osem, jsem, asem,
):
    rep, shard = place()
    rows, width = x_ref.shape
    nb = rows // BQ
    npair = width // 128
    nf = act_out.shape[0]
    across = (rep, 1 - shard)
    peers = [(rep ^ (1 << d), shard) for d in range(4)]
    core = rep & 1
    plan = Plan(lens_ref, shard, rows)
    bounds, slot = plan.bounds(), plan.away()

    parts = []
    for src, dst, nrows, ncols in ((wq_in, wq_ref, 1, 3), (wo_in, wo_ref, 1, 1), (wf_in, wf_ref, 1, 2), (wp_in, wp_ref, 2, 1)):
        size, cols = src.shape[0] // nrows, src.shape[1] // ncols
        for n in range(nrows * ncols):
            parts.append((src, dst, n // ncols * size, size, n % ncols * cols, cols, WAYS[len(parts)]))
    nparts = len(parts)
    early = 4

    def chain(n, step):
        src, dst, row, size, col, cols, way = parts[n]
        half, unit = src.shape[0], size >> len(way)
        index = sum(((rep >> d) & 1) << i for i, d in enumerate(way))
        count = 1 if step == 0 else 1 << (step - 1)
        first = row + ((index & ~(count - 1)) * unit if step <= len(way) else 0)
        here = pl.ds(pl.multiple_of(first, 16), count * unit)
        side = pl.ds(pl.multiple_of(col + core * (cols // 2), 128), cols // 2)
        sems = (wsend.at[n, step], wrecv.at[n, step])
        if step == 0:
            into = pl.ds(pl.multiple_of(shard * half + first, 16), unit)
            return remote(src.at[here, side], dst.at[into, side], *sems, across)
        into = pl.ds(pl.multiple_of((1 - shard) * half + first, 16), count * unit)
        return remote(dst.at[into, side], dst.at[into, side], *sems, peers[(way + (0,))[step - 1]])

    def hops(n):
        return len(parts[n][-1]) + 2

    def act(n, step):
        if step:
            chain(n, step - 1).wait_recv()
        if step < hops(n):
            chain(n, step).start()

    def expected(n):
        _src, _dst, _row, size, _col, cols, way = parts[n]
        mb = size * cols * 1e-6
        out = [(0, mb / LINK_RATE / (1 << len(way)), 1.5)]
        for i, d in enumerate(way):
            out.append((link_of(d)[0], mb / LINK_RATE * link_of(d)[1] / (1 << (len(way) - i)), 1.5))
        return out + [("core", mb / CORE_RATE, 1.0)]

    points, now = [], 21.0
    for i in range(nb):
        for name, long in [(("b", i), 2.0)] + [(("h", i, h), 0.5 + 0.55 * i) for h in range(npair)]:
            now += long
            points.append((name, now))
    first_ones = {n: expected(n) for n in range(early)}
    late_ones = {n: expected(n) for n in range(early, nparts)}
    starts = [("start", 3.0)] + [(("sx", i), 5.0 + 1.8 * i) for i in range(nb)] + [(("pk", i), 13.5 + 2.7 * i) for i in range(nb)]
    opening, opened = timetable(starts, first_ones, {n: "start" for n in first_ones}, {})
    busy = {0: 3.0 + sum(c[0][1] for c in first_ones.values()) + 2 * BQ * width * 2e-6 / LINK_RATE}
    agenda, closing = timetable([("start", 20.0)] + points, late_ones, {n: "start" for n in late_ones}, busy)

    whole = [(wq_in, wq_ref, wq_out), (wo_in, wo_ref, wo_out), (wf_in, wf_ref, wf_out), (wp_in, wp_ref, wp_out)]

    def half_rows(src, which):
        return pl.ds(pl.multiple_of(which * src.shape[0], 16), src.shape[0])

    def own_load(n):
        src, dst, _ = whole[n]
        return pltpu.make_async_copy(src, dst.at[half_rows(src, shard), :], wload.at[n])

    def other_save(n):
        src, dst, save = whole[n]
        return pltpu.make_async_copy(dst.at[half_rows(src, 1 - shard), :], save, wsave.at[n])

    x_load = pltpu.make_async_copy(xin_ref, xo_ref, lsem.at[0])
    c_load = pltpu.make_async_copy(cin_ref, co_ref, lsem.at[1])
    x_load.start()
    for n in range(4):
        own_load(n).start()
    c_load.start()
    hw = width // 2
    for n, ref in enumerate((g1_in, b1_in, qb_in, vb_in, ob_in, g2_in, b2_in, pb_in)):
        small_ref[n, :] = ref[...].astype(F32)
    for n in range(nf):
        small_ref[8 + n, :] = fb_in[n * hw : (n + 1) * hw].astype(F32)
    greet([across] + peers)
    small = remote(small_ref, sm_ref.at[shard], ssem.at[0], ssem.at[1], across)
    small.start()
    for n, step in opening["start"]:
        act(n, step)

    tail = plan.s0 + plan.s1
    theirs = jnp.where(plan.stays, rows, tail)
    split = jnp.where(plan.stays, rows, plan.s0)
    whole_one = jnp.where(plan.stays & (plan.slot == 1), 1, 0)

    def pack_sent(dst_ref, src_ref, i, upto):
        total = None
        for k in range(2):
            part = dot(moved_pick(jnp.where(slot == k, tail, rows), i, upto), src_ref[k, 0:upto, :])
            total = part if total is None else total + part
        dst_ref[rows_of(i, BQ), :] = total.astype(BF)

    def pack_own(dst_ref, src_ref, i):
        r = rows_of(i, BQ)
        row = i * BQ + lax.broadcasted_iota(jnp.int32, (BQ, width), 0)
        base = jnp.where(whole_one == 1, src_ref[1, r, :].astype(F32), src_ref[0, r, :].astype(F32))
        dst_ref[r, :] = jnp.where(row >= split, dot(moved_pick(split, i, rows), src_ref[1]), base).astype(BF)

    def merged(own_ref, got_ref, i):
        r = rows_of(i, BQ)
        row = i * BQ + lax.broadcasted_iota(jnp.int32, (BQ, width), 0)
        return jnp.where(row >= theirs, got_ref[r, :].astype(F32), own_ref[r, :].astype(F32)).astype(BF)

    def x_chunk(i):
        r = rows_of(i, BQ)
        return remote(xs_ref.at[r, :], xr_ref.at[r, :], xsend.at[i], xrecv.at[i], across)

    c_copy = remote(cs_ref, cr_ref, csem.at[0], csem.at[1], across)
    x_load.wait()

    def opened_at(i, name):
        for ii in range(nb):
            if opening[(name, ii)]:

                @pl.when(i == ii)
                def _():
                    for n, step in opening[(name, ii)]:
                        act(n, step)

    pack_sent(xs_ref, xo_ref, 0, BQ)
    x_chunk(0).start()
    for n, step in opening[("sx", 0)]:
        act(n, step)

    @pl.loop(1, nb)
    def _(i):
        pack_sent(xs_ref, xo_ref, i, rows)

        @pl.when(i == 2)
        def _():
            for n, step in agenda["start"]:
                act(n, step)

        x_chunk(i).start()
        opened_at(i, "sx")

    sm_ref[shard] = small_ref[...]
    small.wait()
    for n in range(8):
        for which in range(2):
            vecs_ref[n : n + 1, which * hw : (which + 1) * hw] = sm_ref[which, n : n + 1, :]
    for n in range(nf):
        for part in range(2):
            which, row = (2 * n + part) // nf, 8 + (2 * n + part) % nf
            vecs_ref[8 + n : 9 + n, part * hw : (part + 1) * hw] = sm_ref[which, row : row + 1, :]
    vecs_ref[8 + nf : 16, :] = jnp.zeros((8 - nf, width), F32)
    c_load.wait()

    @pl.loop(0, nb)
    def _(i):
        pack_own(x_ref, xo_ref, i)
        pack_sent(cs_ref, co_ref, i, rows)
        opened_at(i, "pk")

    c_copy.start()
    for n, step in opened:
        act(n, step)
    own_load(0).wait()
    own_load(1).wait()
    other_save(0).start()
    other_save(1).start()
    def at_point(name):
        for n, step in agenda[name]:
            act(n, step)

    gain, shift = vecs_ref[G1 : G1 + 1, :], vecs_ref[B1 : B1 + 1, :]
    lq = lane_half((BQ, 128))
    tri = lax.broadcasted_iota(jnp.int32, (BQ, BQ), 1) <= lax.broadcasted_iota(jnp.int32, (BQ, BQ), 0)
    def joined_save(i, b):
        r = pl.ds(i * BQ, BQ)
        return pltpu.make_async_copy(jn_ref.at[r, pl.ds(b * width, width)], joined_out.at[b, r, :], jsem.at[i, b])

    for i in range(nb):
        x_chunk(i).wait_recv()
        n = (i + 1) * BQ
        r = slice(i * BQ, n)
        xb = merged(x_ref, xr_ref, i)
        x_ref[r, :] = xb
        unit, _inv = norm_stats(xb.astype(F32))
        n1 = (unit * gain + shift).astype(BF)
        for b, row in ((0, QB), (1, None), (2, VB)):
            value = dot(n1, wq_ref[:, b * width : (b + 1) * width])
            if row is not None:
                value = value + vecs_ref[row : row + 1, :]
            jn_ref[r, b * width : (b + 1) * width] = value.astype(BF)
        for b in range(3):
            joined_save(i, b).start()
        at_point(("b", i))
        ohf = own_segment(bounds, i * BQ, BQ)
        oh = ohf.astype(BF)
        neg = other_segment(bounds, i * BQ, BQ).astype(BF)

        @pl.loop(0, npair)
        def _(h):
            k2 = jn_ref[r, pl.ds(pl.multiple_of(width + h * 128, 128), 128)]
            v2 = jn_ref[r, pl.ds(pl.multiple_of(2 * width + h * 128, 128), 128)]
            one = jnp.ones_like(v2)
            ks_ref[h, 0, r, :] = jnp.where(lq, k2, neg)
            ks_ref[h, 1, r, :] = jnp.where(lq, neg, k2)
            vs_ref[h, 0, r, :] = jnp.where(lq, v2, one)
            vs_ref[h, 1, r, :] = jnp.where(lq, one, v2)

        @pl.loop(0, npair)
        def _(h):
            cq = pl.ds(pl.multiple_of(h * 128, 128), 128)
            q2 = jn_ref[r, cq]
            qs = [jnp.where(lq, q2, oh), jnp.where(lq, oh, q2)]
            outs, exts = [], []
            for e in range(2):
                sd = jnp.where(tri, dot_nt(qs[e], ks_ref[h, e, r, :]), NEG)
                peak = jnp.max(sd, axis=1, keepdims=True)
                if i:
                    so = dot_nt(qs[e], ks_ref[h, e, 0 : n - BQ, :])
                    peak = jnp.maximum(peak, jnp.max(so, axis=1, keepdims=True))
                    po = jnp.exp2((so - peak) * EXPC).astype(BF)
                pd = jnp.exp2((sd - peak) * EXPC).astype(BF)
                acc = dot(pd, vs_ref[h, e, r, :])
                if i:
                    acc = acc + dot(po, vs_ref[h, e, 0 : n - BQ, :])
                outs.append(acc)
                tot = acc[:, HD : HD + 1] if e == 0 else acc[:, 0:1]
                exts.append(extra(ohf, -(peak + jnp.log(tot) * (1.0 / SCALE)), 3))
            num = jnp.where(lq, outs[0], outs[1])
            den = pltpu.roll(jnp.where(lq, outs[1], outs[0]), HD, 1)
            att_ref[r, cq] = (num / den).astype(BF)
            ext_ref[r, cq] = jnp.where(lq, exts[1], exts[0]).astype(BF)
            for hh in range(npair):
                if agenda[("h", i, hh)]:

                    @pl.when(h == hh)
                    def _():
                        at_point(("h", i, hh))

    x_save = pltpu.make_async_copy(x_ref, x_out, osem.at[0])
    att_save = pltpu.make_async_copy(att_ref, att_out, osem.at[1])
    ext_save = pltpu.make_async_copy(ext_ref, ext_out, osem.at[2])
    for copy in (x_save, att_save, ext_save):
        copy.start()

    gain2, shift2 = vecs_ref[G2 : G2 + 1, :], vecs_ref[B2 : B2 + 1, :]

    @pl.loop(0, nb)
    def _(i):
        r = rows_of(i, BQ)
        hid = x_ref[r, :].astype(F32) + (dot(att_ref[r, :], wo_ref[...]) + vecs_ref[OB : OB + 1, :])
        hid_ref[r, :] = hid
        unit, _inv = norm_stats(hid)
        n2_ref[r, :] = (unit * gain2 + shift2).astype(BF)
        acc_ref[r, :] = hid + vecs_ref[PB : PB + 1, :]

    hid_save = pltpu.make_async_copy(hid_ref, hid_out, osem.at[3])
    n2_save = pltpu.make_async_copy(n2_ref, n2_out, osem.at[4])
    hid_save.start()
    n2_save.start()

    def gelu_save(n):
        return (
            pltpu.make_async_copy(act_ref.at[n & 1], act_out.at[n], asem.at[0, n]),
            pltpu.make_async_copy(der_ref.at[n & 1], der_out.at[n], asem.at[1, n]),
        )

    for n, step in closing:
        act(n, step)
    own_load(2).wait()
    own_load(3).wait()
    other_save(2).start()
    other_save(3).start()

    @pl.loop(0, nf)
    def _(n):
        @pl.when(n >= 2)
        def _():
            for copy in gelu_save(n - 2):
                copy.wait()

        c = span(n * width, width)

        @pl.loop(0, nb)
        def _(i):
            r = rows_of(i, BQ)
            act, der = gelu_both(dot(n2_ref[r, :], wf_ref[:, c]) + vecs_ref[pl.ds(FB + n, 1), :])
            act = act.astype(BF)
            act_ref[n & 1, r, :] = act
            der_ref[n & 1, r, :] = der.astype(BF)
            acc_ref[r, :] += dot(act, wp_ref[c, :])

        for copy in gelu_save(n):
            copy.start()

    @pl.loop(0, nb)
    def _(i):
        r = rows_of(i, BQ)
        obf_ref[r, :] = acc_ref[r, :].astype(BF)

    out_save = pltpu.make_async_copy(obf_ref, out_out, osem.at[5])
    out_save.start()

    @pl.loop(0, nb)
    def _(i):
        pack_own(cot_ref, co_ref, i)

    c_copy.wait_recv()

    @pl.loop(0, nb)
    def _(i):
        cot_ref[rows_of(i, BQ), :] = merged(cot_ref, cr_ref, i)

    cot_save = pltpu.make_async_copy(cot_ref, cot_out, osem.at[6])
    cot_save.start()
    for n in range(nparts):
        for step in range(hops(n)):
            chain(n, step).wait_send()
    for i in range(nb):
        x_chunk(i).wait_send()
        for b in range(3):
            joined_save(i, b).wait()
    c_copy.wait_send()
    for n in range(4):
        other_save(n).wait()
    for n in range(max(0, nf - 2), nf):
        for copy in gelu_save(n):
            copy.wait()
    for copy in (x_save, att_save, ext_save, hid_save, n2_save, out_save, cot_save):
        copy.wait()


WAYS = [(2, 1), (1, 2), (2, 1), (1, 2), (3, 2, 1), (3, 1, 2), (3, 2, 1), (3, 1, 2)]


def front(lens, xin, cin, small, wq, wo, wf, wp):
    slots, rows, width = xin.shape
    ff = wf.shape[1]
    nf = ff // width
    nb = rows // BQ
    s = jax.ShapeDtypeStruct
    v = pltpu.VMEM
    act = s((rows, width), BF)
    nparts = len(WAYS)
    return pl.pallas_call(
        front_body,
        name="front",
        out_shape=(
            act, s((3, rows, width), BF), act, act, s((rows, width), F32), act, s((nf, rows, width), BF), s((nf, rows, width), BF),
            act, act, s(wq.shape, BF), s(wo.shape, BF), s(wf.shape, BF), s(wp.shape, BF), s((16, width), F32),
        ),
        in_specs=[SMEM] + anyspecs(2) + vspecs(9) + anyspecs(4),
        out_specs=tuple(anyspecs(14) + vspecs(1)),
        scratch_shapes=[
            v((width, 3 * width), BF), v((width, width), BF), v((width, ff), BF), v((ff, width), BF),
            v((slots, rows, width), BF), v((rows, width), BF), v((rows, width), BF),
            v((slots, rows, width), BF), v((rows, width), BF), v((rows, width), BF),
            v((rows, width), BF), v((rows, width), BF), v((16, width // 2), F32), v((2, 16, width // 2), F32),
            v((rows, 3 * width), BF), v((width // 128, 2, rows, 128), BF), v((width // 128, 2, rows, 128), BF),
            v((rows, width), BF), v((rows, width), BF), v((rows, width), F32), v((rows, width), BF),
            v((2, rows, width), BF), v((2, rows, width), BF), v((rows, width), F32), v((rows, width), BF),
            DMA((nparts, 5)), DMA((nparts, 5)), DMA((4,)), DMA((4,)), DMA((nb,)), DMA((nb,)), DMA((2,)), DMA((2,)), DMA((2,)),
            DMA((7,)), DMA((nb, 3)), DMA((2, nf)),
        ],
        compiler_params=params(collective_id=0, has_side_effects=True),
        cost_estimate=cost(40e9, 60e6, 12e6),
    )(lens, xin, cin, *small, wq, wo, wf, wp)


def back_body(
    bits, lens_ref, vecs_ref, x_in, joined_in, att_in, ext_in, hid_in, n2_in, act_in, der_in, out_in, cot_in,
    wq_own, wo_own, wf_own, wp_own, wq_oth, wo_oth, wf_oth, wp_oth,
    res_out, dx_out, dxr_out, outr_out, sums_ref,
    wf_ref, wp_ref, wo_ref, wq_ref, cot_ref, n2_ref, act_ref, der_ref, gpre_ref, acc_ref, hid_ref, att_ref,
    gm_ref, r0_ref, rb_ref, res_ref, sm_ref, smb_ref, smr_ref,
    wsem, lsem, asem, hsem, ssem, rsem, msem, mrem, osem, dsem, drem, vsem, fsem,
):
    rep, shard = place()
    core = rep & 1
    rows, width = cot_ref.shape
    hw = width // 2
    nb = rows // BQ
    nf = act_in.shape[0]
    npair = width // 128
    m = bits - 1
    sibling, across = (rep ^ 1, shard), (rep, 1 - shard)
    peers = {0: across}
    for t in range(1, bits):
        peers[t] = (rep ^ (1 << t), shard)
    plan = Plan(lens_ref, shard, rows)
    bounds = plan.bounds()

    def weight_loads(own, oth, dst, into):
        half = own.shape[0]
        for n, (src, which) in enumerate(((own, shard), (oth, 1 - shard))):
            yield n, src, dst.at[pl.ds(pl.multiple_of(into + which * half, 16), half), :]

    def fc_loads(j):
        for n, src, dst in weight_loads(wf_own, wf_oth, wf_ref, j * width):
            for part in range(2):
                here = span((part * nf + j) * hw, hw)
                yield pltpu.make_async_copy(src.at[:, here], dst.at[:, pl.ds(part * hw, hw)], wsem.at[0, n, part, j])

    def proj_loads(j):
        for n, (src, which) in enumerate(((wp_own, shard), (wp_oth, 1 - shard))):
            into = pl.ds(pl.multiple_of(j * width + which * hw, 16), hw)
            yield pltpu.make_async_copy(src.at[span(j * hw, hw), :], wp_ref.at[into, :], wsem.at[1, n, 0, j])

    def gelu_loads(k, j):
        src, dst = ((act_in, act_ref), (der_in, der_ref))[k]
        for part in range(2):
            block = part * (nf // 2) + (j >> 1)
            here = span((j & 1) * hw, hw)
            yield pltpu.make_async_copy(src.at[block, :, here], dst.at[j & 1, :, pl.ds(part * hw, hw)], asem.at[k, part, j])

    def plain(n, src, dst):
        return pltpu.make_async_copy(src, dst, lsem.at[n])

    cot_load, n2_load, att_load = plain(0, cot_in, cot_ref), plain(1, n2_in, n2_ref), plain(2, att_in, att_ref)
    wo_loads = [pltpu.make_async_copy(s_, d_, wsem.at[2, n, 0, 0]) for n, s_, d_ in weight_loads(wo_own, wo_oth, wo_ref, 0)]
    wq_loads = [pltpu.make_async_copy(s_, d_, wsem.at[2, n, 0, 1]) for n, s_, d_ in weight_loads(wq_own, wq_oth, wq_ref, 0)]
    x_load, ext_load = plain(3, x_in, act_ref.at[0]), plain(4, ext_in, der_ref.at[0])
    joined_loads = [plain(5 + b, joined_in.at[b], wf_ref.at[pl.ds(b * rows, rows), :]) for b in range(3)]

    def hid_load(i):
        return pltpu.make_async_copy(hid_in.at[pl.ds(i * BQ, BQ), :], hid_ref.at[i % 2], hsem.at[i])

    cot_load.start()
    for j in range(2):
        for copy in list(gelu_loads(0, j)) + list(proj_loads(j)) + list(gelu_loads(1, j)) + list(fc_loads(j)):
            copy.start()
        if j == 0:
            n2_load.start()
    greet([sibling, across] + [peers[t] for t in range(1, bits)])

    per = gm_ref.shape[3] // PIECE
    pieces = pieces_of(per, hw)
    count = len(pieces)
    last = 3 + 2 * m
    orders = [PATHS[k] + tuple(range(4, bits)) for k in range(count)]

    def source(k, away):
        n, c = pieces[k]
        a, at = n // per, pl.ds((n % per) * PIECE, PIECE)
        return gm_ref.at[away, a, :, at, c] if a < 2 else gm_ref.at[1, away, :, at, c]

    def place_of(ref, k):
        n, c = pieces[k]
        return ref.at[n, :, :, c]

    def result_of(ref, k):
        n, c = pieces[k]
        return ref.at[n, :, c]

    def held(k, i):
        half, first, size = None, 0, PIECE
        for d in orders[k][:i]:
            if d == 0:
                half = shard
            else:
                size //= 2
                first = first + ((rep >> d) & 1) * size
        return half, first, size

    def at_rows(first, size):
        return pl.ds(pl.multiple_of(first, 16), size)

    def landing(k, i):
        d = orders[k][i]
        half, _first, size = held(k, i + 1)
        before = sum(PIECE >> (n + 1) for n in range(len([e for e in orders[k][:i] if e])))
        if d == 0:
            return place_of(rb_ref, k).at[0, pl.ds(before, size), :]
        at = pl.ds(before, size)
        return place_of(rb_ref, k).at[:, at, :] if half is None else place_of(rb_ref, k).at[1, at, :]

    def leaving(k, i):
        d = orders[k][i]
        half, first, size = held(k, i)
        own = source(k, 0)
        if d == 0:
            return own.at[1 - shard, at_rows(first, size), :]
        size //= 2
        at = at_rows(first + (1 - ((rep >> d) & 1)) * size, size)
        return own.at[:, at, :] if half is None else own.at[half, at, :]

    def copy(k, step):
        sems = (ssem.at[step, k], rsem.at[step, k])
        if step == 0:
            return remote(source(k, 1), place_of(r0_ref, k), *sems, sibling)
        if step <= m + 1:
            return remote(leaving(k, step - 1), landing(k, step - 1), *sems, peers[orders[k][step - 1]])
        if step <= 2 * m + 1:
            back = [d for d in orders[k] if d]
            t = m - (step - m - 2)
            size = PIECE >> t
            first = 0
            for n in range(t):
                first = first + ((rep >> back[n]) & 1) * (PIECE >> (n + 1))
            here = result_of(res_ref, k).at[at_rows(first, size), :]
            return remote(here, here, *sems, peers[back[t - 1]])
        return remote(result_of(res_ref, k), result_of(res_out.at[core], k), *sems, sibling)

    def keep(k):
        return pltpu.make_async_copy(result_of(res_ref, k), result_of(res_out.at[core], k), fsem.at[k])

    def add(dst, first, other, base, size, out=None):
        chunk = min(size, 64)

        @pl.loop(0, size // chunk)
        def _(i):
            at = pl.ds(pl.multiple_of(first + i * chunk, 16), chunk)
            total = dst[at, :].astype(F32) + other[pl.ds(pl.multiple_of(base + i * chunk, 16), chunk), :].astype(F32)
            (dst if out is None else out)[at, :] = total.astype(BF)

    def act_step(k, step):
        if step:
            copy(k, step - 1).wait_recv()
        own = source(k, 0)
        if step == 1:
            for h in range(2):
                add(own.at[h], 0, place_of(r0_ref, k).at[h], 0, PIECE)
        elif 2 <= step <= m + 2:
            i = step - 2
            half, first, size = held(k, i + 1)
            land = landing(k, i)
            if half is None:
                for h in range(2):
                    add(own.at[h], first, land.at[h], 0, size)
            else:
                add(own.at[half], first, land, 0, size, result_of(res_ref, k) if i == m else None)
        if step < last:
            copy(k, step).start()
        if step == last - 1:
            keep(k).start()

    def small_copy(step):
        src = sm_ref if step == 0 else smb_ref.at[step - 1]
        return remote(src, smr_ref.at[step], msem.at[step], mrem.at[step], small_peers[step])

    def small_step(step):
        if step:
            small_copy(step - 1).wait_recv()
            before = sm_ref[...] if step == 1 else smb_ref[step - 2]
            total = before + smr_ref[step - 1]
            if step == 2 + m:
                sums_ref[...] = total
            else:
                smb_ref[step - 1] = total
        if step < 2 + m:
            small_copy(step).start()

    def dx_chunk(i):
        at = pl.ds(i * BQ, BQ)
        return remote(dxb_ref.at[at, :], dxr_out.at[at, :], dsem.at[i], drem.at[i], across)

    def dx_step(i):
        if i:
            dx_chunk(i - 1).wait_send()
        if i < nb:
            dx_chunk(i).start()

    def out_chunk(i):
        at = pl.ds(i * BQ, BQ)
        return remote(out_in.at[at, :], outr_out.at[at, :], osem.at[0, i], osem.at[1, i], across)

    def out_step(i):
        if i:
            out_chunk(i - 1).wait_send()
        if i < nb:
            out_chunk(i).start()

    def act(c, step):
        if c == "out":
            out_step(step)
        elif c == "small":
            small_step(step)
        elif c == "dx":
            dx_step(step)
        else:
            act_step(c, step)

    small_peers = [sibling, across] + [peers[t] for t in range(1, bits)]
    xb_ref, eb_ref, n1_ref, dxb_ref = act_ref.at[0], der_ref.at[0], der_ref.at[1], act_ref.at[1]

    points, now = [], 5.0
    for name, long in (
        [(("gp", j), 1.9) for j in range(nf)]
        + [(("ff", j, n), (4.1, 2.2)[n]) for j in range(nf) for n in range(2)]
        + [(("hid", i), 1.6) for i in range(nb)]
        + [("go", 2.0)]
        + [p for t in range(THIRDS) for p in [(("at", t, p, i), 0.72 * (i + 1)) for p in range(npair // THIRDS) for i in range(nb)] + [(("gw", t), 2.0)]]
        + [(("dx", i), 2.0) for i in range(nb)]
    ):
        now += long
        points.append((name, now))
    chains, ready = {}, {}
    for k, (n, c) in enumerate(pieces):
        half_mb = 2 * PIECE * (c.stop - c.start) / 1e6
        steps, size = [("core", 2 * half_mb / CORE_RATE, 1.0)], 2 * half_mb
        for d in orders[k]:
            size /= 2
            steps.append((link_of(d)[0], size / LINK_RATE * link_of(d)[1], 1.5))
        size = half_mb / (1 << m)
        for d in reversed([d for d in orders[k] if d]):
            steps.append((link_of(d)[0], size / LINK_RATE * link_of(d)[1], 1.5))
            size *= 2
        chains[k] = steps + [("core", half_mb / CORE_RATE, 1.0)]
        ready[k] = ("ff", 1 + n, 1) if n < per else ("gp", 1 + n - per) if n < 2 * per else ("gw", n - 2 * per)
    small_us = 24 * width * 4e-6 / LINK_RATE
    chains["small"] = [("core", 0.5, 1.0), (0, small_us, 1.5)] + [(link_of(d)[0], small_us * link_of(d)[1], 1.5) for d in range(1, bits)]
    chains["dx"] = [(0, BQ * width * 2e-6 / LINK_RATE, 0.0)] * nb
    chains["out"] = chains["dx"]
    ready["small"], ready["dx"], ready["out"] = ("dx", nb - 1), ("dx", 0), OUT_AT
    agenda, tail = timetable(points, chains, ready, {})

    def at_point(name):
        for c, step in agenda[name]:
            act(c, step)

    gbase = 16
    sm_ref[...] = jnp.zeros_like(sm_ref)

    @pl.loop(0, nb)
    def _(i):
        acc_ref[rows_of(i, BQ), :] = jnp.zeros((BQ, width), F32)

    def at_step(j, name):
        for jj in range(nf):
            if agenda[name(jj)]:

                @pl.when(j == jj)
                def _():
                    at_point(name(jj))

    cot_load.wait()

    @pl.loop(0, nf)
    def _(j):
        for c in gelu_loads(0, j):
            c.wait()
        into = span(j * hw, hw)
        for h in range(2):
            gp = dot_tn(act_ref[j & 1, :, h * hw : (h + 1) * hw], cot_ref[...]).astype(BF)
            for c in range(2):
                gm_ref[c ^ core, 1, h, into, :] = gp[:, c * hw : (c + 1) * hw]

        @pl.when(j < nf - 2)
        def _():
            for c in gelu_loads(0, j + 2):
                c.start()

        at_step(j, lambda jj: ("gp", jj))

    n2_load.wait()

    @pl.loop(0, nf)
    def _(j):
        for c in list(proj_loads(j)) + list(gelu_loads(1, j)) + list(fc_loads(j)):
            c.wait()

        @pl.when(j < nf - 2)
        def _():
            for c in list(proj_loads(j + 2)) + list(fc_loads(j + 2)):
                c.start()

        here, into, bias = span(j * width, width), span(j * hw, hw), pl.ds(gbase + j, 1)

        @pl.loop(0, nb)
        def _(i):
            r = rows_of(i, BQ)
            gact = dot_nt(cot_ref[r, :], wp_ref[here, :])
            gpre = (gact * der_ref[j & 1, r, :].astype(F32)).astype(BF)
            gpre_ref[r, :] = gpre
            sm_ref[bias, :] += jnp.sum(gpre.astype(F32), axis=0, keepdims=True)
            acc_ref[r, :] += dot_nt(gpre, wf_ref[here, :])

        at_step(j, lambda jj: ("ff", jj, 0))
        for h in range(2):
            gf = dot_tn(n2_ref[:, h * hw : (h + 1) * hw], gpre_ref[...]).astype(BF)
            for c in range(2):
                gm_ref[c ^ core, 0, h, into, :] = gf[:, c * hw : (c + 1) * hw]

        @pl.when(j < nf - 2)
        def _():
            for c in gelu_loads(1, j + 2):
                c.start()

        @pl.when(j == nf - 2)
        def _():
            for c in [x_load, ext_load, att_load] + wo_loads + wq_loads:
                c.start()
            hid_load(0).start()
            hid_load(1).start()

        at_step(j, lambda jj: ("ff", jj, 1))

    for c in joined_loads:
        c.start()
    for c in [att_load] + wo_loads:
        c.wait()
    gain2 = vecs_ref[G2 : G2 + 1, :]
    gatt_ref = cot_ref
    for i in range(nb):
        r = slice(i * BQ, (i + 1) * BQ)
        hid_load(i).wait()
        unit, inv = norm_stats(hid_ref[i % 2])
        gn2 = acc_ref[r, :]
        gy = cot_ref[r, :].astype(F32)
        ghid = gy + norm_back(gn2, unit, inv, gain2)
        if i + 2 < nb:
            hid_load(i + 2).start()
        acc_ref[r, :] = ghid
        low = ghid.astype(BF)
        gpre_ref[r, :] = low
        gatt_ref[r, :] = dot_nt(low, wo_ref[...]).astype(BF)
        sm_ref[0:1, :] += jnp.sum(gn2 * unit, axis=0, keepdims=True)
        sm_ref[1:2, :] += jnp.sum(gn2, axis=0, keepdims=True)
        sm_ref[2:3, :] += jnp.sum(gy, axis=0, keepdims=True)
        sm_ref[3:4, :] += jnp.sum(low.astype(F32), axis=0, keepdims=True)
        at_point(("hid", i))
    x_load.wait()
    gain1, shift1 = vecs_ref[G1 : G1 + 1, :], vecs_ref[B1 : B1 + 1, :]

    @pl.loop(0, nb)
    def _(i):
        r = rows_of(i, BQ)
        unit, _inv = norm_stats(xb_ref[r, :].astype(F32))
        n1_ref[r, :] = (unit * gain1 + shift1).astype(BF)

    aways = [k for k, (n, _) in enumerate(pieces) if n < 2 * per]
    for k in aways:
        copy(k, 0).wait_send()
    for h in range(2):
        go = dot_tn(att_ref[:, h * hw : (h + 1) * hw], gpre_ref[...]).astype(BF)
        for c in range(2):
            gm_ref[1, c ^ core, h, 0:hw, :] = go[:, c * hw : (c + 1) * hw]
    at_point("go")
    for c in joined_loads + [ext_load]:
        c.wait()

    lq = lane_half((BQ, 128))
    tri = lax.broadcasted_iota(jnp.int32, (BQ, BQ), 0) <= lax.broadcasted_iota(jnp.int32, (BQ, BQ), 1)
    left = lane_half((rows, 128))
    ones = lax.broadcasted_iota(jnp.int32, (rows, 128), 1) % HD
    ones = (ones >= 3) & (ones < 6)
    tcols = width // THIRDS
    here_at = lambda t, p, i: agenda[("at", t, p, i)]

    def head_pair(t, p):
        h = t * (npair // THIRDS) + p
        col = pl.ds(pl.multiple_of(h * 128, 128), 128)
        k2 = wf_ref[rows : 2 * rows, col]
        v2 = wf_ref[2 * rows : 3 * rows, col]
        zero = jnp.zeros_like(k2)
        kx = jnp.where(ones, 1.0, other_segment(bounds, 0, rows)).astype(BF)
        vx = jnp.where(ones, 1.0, 0.0).astype(BF)
        ks = [jnp.where(left, k2, kx), jnp.where(left, kx, k2)]
        vs = [jnp.where(left, v2, vx), jnp.where(left, vx, v2)]
        km = [jnp.where(left, k2, zero), jnp.where(left, zero, k2)]
        hid_ref[...] = jnp.zeros_like(hid_ref)
        for i in range(nb):
            r = slice(i * BQ, (i + 1) * BQ)
            q2 = wf_ref[r, col]
            g2 = gatt_ref[r, col]
            ext = eb_ref[r, col]
            zq = jnp.zeros_like(q2)
            prod = g2.astype(F32) * att_ref[r, col].astype(F32)
            d0 = jnp.sum(jnp.where(lq, prod, 0.0), axis=1, keepdims=True)
            d1 = jnp.sum(jnp.where(lq, 0.0, prod), axis=1, keepdims=True)
            zf = jnp.zeros((BQ, 128), F32)
            qs = [jnp.where(lq, q2, ext), jnp.where(lq, ext, q2)]
            gs = [jnp.where(lq, g2, extra(zf, -d0, 3).astype(BF)), jnp.where(lq, extra(zf, -d1, 3).astype(BF), g2)]
            qm = [jnp.where(lq, q2, zq), jnp.where(lq, zq, q2)]
            gm = [jnp.where(lq, g2, zq), jnp.where(lq, zq, g2)]
            dq = None
            for u in range(i + 1):
                b = slice(u * BQ, (u + 1) * BQ)
                dk = dv = None
                for e in range(2):
                    st = dot_nt(ks[e][b], qs[e])
                    if u == i:
                        st = jnp.where(tri, st, NEG)
                    pt = jnp.exp2(st * EXPC)
                    dst = (pt * dot_nt(vs[e][b], gs[e])).astype(BF)
                    one, two, three = dot(pt.astype(BF), gm[e]), dot(dst, qm[e]), dot_tn(dst, km[e][b])
                    dv = one if dv is None else dv + one
                    dk = two if dk is None else dk + two
                    dq = three if dq is None else dq + three
                hid_ref[1, :, u * 128 : (u + 1) * 128] += dv
                hid_ref[0, :, u * 128 : (u + 1) * 128] += dk
            wp_ref[r, col] = (dq * SCALE).astype(BF)
            for tt in range(THIRDS):
                for pp in range(npair // THIRDS):
                    if here_at(tt, pp, i):

                        @pl.when((t == tt) & (p == pp))
                        def _():
                            for c, step in here_at(tt, pp, i):
                                act(c, step)

        for u in range(nb):
            wp_ref[rows + u * BQ : rows + (u + 1) * BQ, col] = (hid_ref[0, :, u * 128 : (u + 1) * 128] * SCALE).astype(BF)
            wp_ref[2 * rows + u * BQ : 2 * rows + (u + 1) * BQ, col] = hid_ref[1, :, u * 128 : (u + 1) * 128].astype(BF)

    @pl.loop(0, THIRDS)
    def _(t):
        @pl.loop(0, npair // THIRDS)
        def _(p):
            head_pair(t, p)

        cols = pl.ds(pl.multiple_of(t * tcols, 128), tcols)
        into = pl.ds(pl.multiple_of(hw + t * hw, 128), hw)
        cut = hw - tcols
        for h in range(2):
            n1h = n1_ref[:, h * hw : (h + 1) * hw]
            gq, gk, gv = [dot_tn(n1h, wp_ref[b * rows : (b + 1) * rows, cols]).astype(BF) for b in range(3)]
            gm_ref[1, core, h, into, 0:tcols] = gq
            gm_ref[1, core, h, into, tcols:hw] = gk[:, 0:cut]
            gm_ref[1, 1 - core, h, into, 0:cut] = gk[:, cut:tcols]
            gm_ref[1, 1 - core, h, into, cut:hw] = gv
        for b in (0, 2):
            sm_ref[8 + b : 9 + b, cols] = jnp.sum(wp_ref[b * rows : (b + 1) * rows, cols].astype(F32), axis=0, keepdims=True)
        for tt in range(THIRDS):
            if agenda[("gw", tt)]:

                @pl.when(t == tt)
                def _():
                    at_point(("gw", tt))

    for c in wq_loads:
        c.wait()

    for i in range(nb):
        r = slice(i * BQ, (i + 1) * BQ)
        gn1 = dot_nt(wp_ref[0:rows][r], wq_ref[:, 0:width])
        for b in (1, 2):
            gn1 = gn1 + dot_nt(wp_ref[b * rows + i * BQ : b * rows + (i + 1) * BQ, :], wq_ref[:, b * width : (b + 1) * width])
        unit, inv = norm_stats(xb_ref[r, :].astype(F32))
        dxb_ref[r, :] = (acc_ref[r, :] + norm_back(gn1, unit, inv, gain1)).astype(BF)
        sm_ref[11:12, :] += jnp.sum(gn1 * unit, axis=0, keepdims=True)
        sm_ref[12:13, :] += jnp.sum(gn1, axis=0, keepdims=True)
        at_point(("dx", i))
    dx_save = plain(8, dxb_ref, dx_out)
    dx_save.start()

    for c, step in tail:
        act(c, step)
    for k in range(count):
        for step in range(last):
            if step or k not in aways:
                copy(k, step).wait_send()
        keep(k).wait()
    for step in range(2 + m):
        small_copy(step).wait_send()
    for i in range(nb):
        out_chunk(i).wait_recv()
        dx_chunk(i).wait_recv()
    dx_save.wait()


THIRDS = 3
CORE_RATE, LINK_RATE = 0.15, 0.045
OUT_AT = ("gp", 0)
PATHS = [(2, 1, 0, 3), (1, 0, 3, 2), (1, 0, 2, 3), (1, 2, 0, 3), (0, 1, 2, 3), (1, 2, 0, 3), (1, 0, 2, 3), (0, 1, 2, 3), (2, 1, 0, 3), (1, 2, 3, 0), (0, 1, 2, 3)]


def pieces_of(per, columns):
    out = [(n, slice(0, columns)) for n in range(3 * per - 1)]
    return out + [(3 * per - 1, slice(c, c + 128)) for c in range(0, columns, 128)]


def back(bits, lens, vecs, saved, own, oth):
    x, joined, att, ext, hid, n2, act, der, out, cot = saved
    rows, width = x.shape
    nf = act.shape[0]
    nb = rows // BQ
    hw = width // 2
    m = bits - 1
    per = nf * hw // PIECE
    wholes, count = 3 * per, len(pieces_of(per, hw))
    s = jax.ShapeDtypeStruct
    v = pltpu.VMEM
    sums = (24, width)
    return pl.pallas_call(
        functools.partial(back_body, bits),
        name="back",
        out_shape=(s((2, wholes, PIECE, hw), BF), s((rows, width), BF), s((rows, width), BF), s((rows, width), BF), s(sums, F32)),
        in_specs=[SMEM] + vspecs(1) + anyspecs(18),
        out_specs=tuple(anyspecs(4) + vspecs(1)),
        scratch_shapes=[
            v((nf * width, width), BF), v((nf * width, width), BF), v((width, width), BF), v((width, 3 * width), BF),
            v((rows, width), BF), v((rows, width), BF), v((2, rows, width), BF), v((2, rows, width), BF), v((rows, width), BF),
            v((rows, width), F32), v((2, BQ, width), F32), v((rows, width), BF),
            v((2, 2, 2, nf * hw, hw), BF), v((wholes, 2, PIECE, hw), BF), v((wholes, 2, PIECE, hw), BF), v((wholes, PIECE, hw), BF),
            v(sums, F32), v((m + 1,) + sums, F32), v((m + 2,) + sums, F32),
            DMA((3, 2, 2, nf)), DMA((9,)), DMA((2, 2, nf)), DMA((nb,)), DMA((3 + 2 * m, count)), DMA((3 + 2 * m, count)),
            DMA((m + 2,)), DMA((m + 2,)), DMA((2, nb)), DMA((nb,)), DMA((nb,)), DMA((1,)), DMA((count,)),
        ],
        compiler_params=params(collective_id=1, has_side_effects=True),
        cost_estimate=cost(60e9, 60e6, 8e6),
    )(lens, vecs, *saved, *own, *oth)


def finish_body(
    lens_ref, deal_ref, sums_ref, res_in, dx_in, dxr_in, out_in, outr_in, y_out, d_out, *rest
):
    outs, scratch = rest[:13], rest[13:]
    (o_g1, o_b1, o_qkv, o_qb, o_vb, o_wo, o_ob, o_g2, o_b2, o_fc, o_fb, o_proj, o_pb) = outs
    res_ref, src_ref, y_ref, qkv_ref, wo_ref, fc_ref, proj_ref, lsem, ssem = scratch
    shard = lax.axis_index("shard")
    rows, width = src_ref.shape[1:]
    hw = width // 2
    nb = rows // BQ
    slots = y_ref.shape[1]
    nf = fc_ref.shape[1] // width
    plan = Plan(lens_ref, shard, rows)
    loads = [pltpu.make_async_copy(a, src_ref.at[n], lsem.at[n]) for n, a in enumerate((out_in, outr_in, dx_in, dxr_in))]
    per = res_in.shape[1] // 3
    pieces = [pltpu.make_async_copy(res_in.at[:, pl.ds(per * a, per)], res_ref.at[:, pl.ds(per * a, per)], lsem.at[4 + a]) for a in range(3)]
    for copy in loads + pieces:
        copy.start()
    own = pl.ds(pl.multiple_of(shard * hw, 128), hw)
    for ref, row in ((o_g1, 11), (o_b1, 12), (o_qb, 8), (o_vb, 10), (o_ob, 3), (o_g2, 0), (o_b2, 1), (o_pb, 2)):
        ref[...] = sums_ref[row, own]
    for j in range(nf):
        o_fb[j * hw : (j + 1) * hw] = sums_ref[16 + j, own]

    def save(n, src, dst):
        return pltpu.make_async_copy(src, dst, ssem.at[n])

    saves = []
    for g in range(2):
        loads[2 * g].wait()
        loads[2 * g + 1].wait()
        for j in range(slots):
            q = slots * shard + j
            if g == 0:
                q = sum(jnp.where(q == n, deal_ref[0, n], 0) for n in range(2 * slots))
            side, offset, size = plan.where(q)

            @pl.loop(0, nb)
            def _(i):
                low, pick = window_pick(rows, i * BQ + offset, BQ)
                row = i * BQ + lax.broadcasted_iota(jnp.int32, pick.shape, 0)
                pick = jnp.where(pick & (row < size), 1.0, 0.0).astype(BF)
                y_ref[g, j, rows_of(i, BQ), :] = dot(pick, src_ref[2 * g + side, pl.ds(low, WINDOW), :]).astype(BF)

            saves.append(save(2 * g + j, y_ref.at[g, j], (y_out, d_out)[g].at[j]))
            saves[-1].start()
    block = lambda c, a, n, r, size: res_ref[c, a * per + (n * hw + r) // PIECE, (n * hw + r) % PIECE : (n * hw + r) % PIECE + size, :]
    for a, (dst, out) in enumerate(((fc_ref, o_fc), (proj_ref, o_proj), (qkv_ref, o_qkv))):
        pieces[a].wait()
        for n in range(nf):
            for c in range(2):
                for r in range(0, hw, 128):
                    value = block(c, a, n, r, 128).astype(F32)
                    at = slice(r, r + 128)
                    if a == 0:
                        fc_ref[at, (c * nf + n) * hw : (c * nf + n + 1) * hw] = value
                    elif a == 1:
                        proj_ref[n * hw + r : n * hw + r + 128, c * hw : (c + 1) * hw] = value
                    elif n == 0:
                        wo_ref[at, c * hw : (c + 1) * hw] = value
                    else:
                        tcols = width // THIRDS
                        cut, lead = hw - tcols, (n - 1) * tcols
                        if c == 0:
                            qkv_ref[at, lead : lead + tcols] = value[:, 0:tcols]
                            qkv_ref[at, width + lead : width + lead + cut] = value[:, tcols:hw]
                        else:
                            qkv_ref[at, width + lead + cut : width + lead + tcols] = value[:, 0:cut]
                            qkv_ref[at, 2 * width + lead : 2 * width + lead + tcols] = value[:, cut:hw]
        saves.append(save(4 + a, dst, out))
        saves[-1].start()
    saves.append(save(7, wo_ref, o_wo))
    saves[-1].start()
    for copy in saves:
        copy.wait()


def finish(lens, deal, sums, res, dx, dxr, out, outr, slots):
    rows, width = dx.shape
    hw = width // 2
    nf = res.shape[1] * PIECE // 3 // hw
    s = jax.ShapeDtypeStruct
    v = pltpu.VMEM
    vec, act = s((hw,), F32), s((slots, rows, width), BF)
    wide = lambda a, b: s((a, b), F32)
    vs, an = vspecs(1), anyspecs(1)
    return pl.pallas_call(
        finish_body,
        name="finish",
        out_shape=(act, act, vec, vec, wide(hw, 3 * width), vec, vec, wide(hw, width), vec, vec, vec, wide(hw, nf * width),
                   s((nf * hw,), F32), wide(nf * hw, width), vec),
        in_specs=[SMEM, SMEM] + vs + anyspecs(5),
        out_specs=tuple(an * 2 + vs * 2 + an + vs * 2 + an + vs * 3 + an + vs + an + vs),
        scratch_shapes=[
            v(res.shape, BF), v((4, rows, width), BF), v((2, slots, rows, width), BF),
            v((hw, 3 * width), F32), v((hw, width), F32), v((hw, nf * width), F32), v((nf * hw, width), F32), DMA((7,)), DMA((8,)),
        ],
        compiler_params=params(),
        cost_estimate=cost(8e9, 34e6),
    )(lens, deal, sums, res, dx, dxr, out, outr)


def local(bits, layer_in, cotangent, lengths, dealing, g1, b1, wqkv, qb, vb, wout, ob, g2, b2, wfc, bfc, wproj, pb):
    slots, rows, width = layer_in.shape
    own = (wqkv, wout, wfc, wproj)
    got = front(lengths, layer_in, cotangent, (g1, b1, qb, vb, ob, g2, b2, pb, bfc), *own)
    saved, oth, vecs = got[:10], got[10:14], got[14]
    res, dx, dxr, outr, sums = back(bits, lengths, vecs, saved, own, oth)
    return finish(lengths, dealing, sums, res, dx, dxr, saved[8], outr, slots)


def solution(mesh):
    both, one = P(("rep", "shard"), None, None), P("shard")
    mat = P("shard", None)
    in_specs = (both, both, P("rep", None), P("rep", None), one, one, mat, one, one, mat, one, one, one, mat, one, mat, one)
    out_specs = (both, both, one, one, mat, one, one, mat, one, one, one, mat, one, mat, one)
    bits = mesh.shape["rep"].bit_length() - 1
    return jax.shard_map(functools.partial(local, bits), mesh=mesh, in_specs=in_specs, out_specs=out_specs, check_vma=False)
```

```python
import functools

import jax
import jax.numpy as jnp
from jax import lax
from jax.experimental import pallas as pl
from jax.experimental.pallas import tpu as pltpu
from jax.sharding import PartitionSpec as P

HD = 64
BQ = 256
EPS = 1e-05
BF = jnp.bfloat16
F32 = jnp.float32
NEG = -1e30
LOG2E = 1.4426950408889634
SCALE = HD**-0.5
EXPC = SCALE * LOG2E
VLIM = 66_900_000
GELU_A = 0.7978845608028654
GELU_B = 0.044715
MESH = pl.DeviceIdType.MESH
PIECE = 512
WINDOW = 384
G1, B1, QB, VB, OB, G2, B2, PB, FB = range(9)
JB = 12


def dot(a, b):
    return jnp.dot(a, b, preferred_element_type=F32)


def dot_tn(a, b):
    return lax.dot_general(a, b, (((0,), (0,)), ((), ())), preferred_element_type=F32)


def dot_nt(a, b):
    return lax.dot_general(a, b, (((1,), (1,)), ((), ())), preferred_element_type=F32)


def norm_stats(v):
    mean = jnp.mean(v, axis=-1, keepdims=True)
    cen = v - mean
    inv = lax.rsqrt(jnp.mean(cen * cen, axis=-1, keepdims=True) + EPS)
    return cen * inv, inv


def norm_back(grad, unit, inv, gain):
    e = grad * gain
    m1 = jnp.mean(e, axis=-1, keepdims=True)
    m2 = jnp.mean(e * unit, axis=-1, keepdims=True)
    return inv * (e - m1 - unit * m2)


def rows_of(i, size):
    return pl.ds(pl.multiple_of(i * size, size), size)


def span(first, size):
    return pl.ds(first if isinstance(first, int) else pl.multiple_of(first, 128), size)


def lane_half(shape):
    return lax.broadcasted_iota(jnp.int32, shape, 1) < HD


def extra(base, v, first):
    hi = v.astype(BF).astype(F32)
    mid = (v - hi).astype(BF).astype(F32)
    lane = lax.broadcasted_iota(jnp.int32, base.shape, 1) % HD
    out = jnp.where(lane == first, hi, base)
    out = jnp.where(lane == first + 1, mid, out)
    return jnp.where(lane == first + 2, v - hi - mid, out)


def vspecs(n):
    return [pl.BlockSpec(memory_space=pltpu.VMEM)] * n


def anyspecs(n):
    return [pl.BlockSpec(memory_space=pl.ANY)] * n


SMEM = pl.BlockSpec(memory_space=pltpu.SMEM)
DMA = pltpu.SemaphoreType.DMA


def params(**kw):
    return pltpu.CompilerParams(vmem_limit_bytes=VLIM, **kw)


def cost(flops, moved, trans=0):
    return pl.CostEstimate(flops=int(flops), bytes_accessed=int(moved), transcendentals=int(trans))


class Plan:
    def __init__(self, lens_ref, shard, rows):
        group = lens_ref.shape[1]
        half = group // 2
        self.half, self.shard, self.rows = half, shard, rows
        self.lens = [lens_ref[0, q] for q in range(group)]
        long = jnp.int32(0)
        for q in range(1, group):
            long = jnp.where(self.lens[q] == rows, q, long)
        self.long = long
        self.home = lax.div(long, jnp.int32(half))
        self.stays = shard == self.home
        self.slot = long & 1
        self.first = half * (1 - self.home)
        self.s0, self.s1 = self.size(self.first), self.size(self.first + 1)
        self.moved = self.size(long ^ 1)

    def size(self, q):
        out = self.lens[0]
        for n in range(1, len(self.lens)):
            out = jnp.where(q == n, self.lens[n], out)
        return out

    def away(self):
        return jnp.where(self.stays, 1 - self.slot, 0)

    def bounds(self):
        return jnp.where(self.stays, self.rows, self.s0), jnp.where(self.stays, self.rows, self.s0 + self.s1)

    def where(self, q):
        start = jnp.where(q == self.first, 0, jnp.where(q == self.first + 1, self.s0, self.s0 + self.s1))
        start = jnp.where(q == self.long, 0, start)
        side = jnp.where(q == self.long, self.home, 1 - self.home) ^ self.shard
        return side, start, self.size(q)


def window_pick(total, first, count):
    low = jnp.clip((first >> 7) << 7, 0, total - WINDOW)
    want = first - low + lax.broadcasted_iota(jnp.int32, (count, WINDOW), 0)
    return pl.multiple_of(low, 128), want == lax.broadcasted_iota(jnp.int32, (count, WINDOW), 1)


def moved_pick(start, i, upto):
    want = i * BQ - start + lax.broadcasted_iota(jnp.int32, (BQ, upto), 0)
    return jnp.where(want == lax.broadcasted_iota(jnp.int32, (BQ, upto), 1), 1.0, 0.0).astype(BF)


def lane_and_segment(bounds, first, rows):
    row = first + lax.broadcasted_iota(jnp.int32, (rows, 128), 0)
    seg = (row >= bounds[0]).astype(jnp.int32) + (row >= bounds[1]).astype(jnp.int32)
    return lax.broadcasted_iota(jnp.int32, (rows, 128), 1) % HD, seg


def own_segment(bounds, first, rows):
    lane, seg = lane_and_segment(bounds, first, rows)
    return jnp.where(lane == seg, 1.0, 0.0)


def other_segment(bounds, first, rows):
    lane, seg = lane_and_segment(bounds, first, rows)
    return jnp.where((lane < 3) & (lane != seg), NEG, 0.0)


def gelu_both(v):
    v2 = v * v
    t = jnp.tanh(v * (GELU_A + (GELU_A * GELU_B) * v2))
    half = 0.5 + 0.5 * t
    return v * half, half + (0.5 * v) * (1.0 - t * t) * (GELU_A + (3.0 * GELU_A * GELU_B) * v2)


def place():
    return lax.axis_index("rep"), lax.axis_index("shard")


def greet(partners):
    barrier = pltpu.get_barrier_semaphore()
    for partner in partners:
        pl.semaphore_signal(barrier, inc=1, device_id=partner, device_id_type=MESH)
    pl.semaphore_wait(barrier, len(partners))


def remote(src, dst, ssem, rsem, to):
    return pltpu.make_async_remote_copy(
        src_ref=src, dst_ref=dst, send_sem=ssem, recv_sem=rsem, device_id=to, device_id_type=MESH
    )


def link_of(d):
    return ((d + 2) // 2 if d else 0), (2 if d > 2 and d % 2 else 1)


def timetable(points, chains, ready, busy):
    free, at, step = dict(busy), {}, {c: 0 for c in chains}
    plan, tail = {name: [] for name, _ in points}, []

    def take(c, now, dest):
        dest.append((c, step[c]))
        if step[c] < len(chains[c]):
            link, long, lag = chains[c][step[c]]
            free[link] = max(now, free.get(link, 0.0)) + long
            at[c] = free[link] + lag
        step[c] += 1

    left = lambda: [c for c in chains if c in at and step[c] <= len(chains[c])]
    for name, now in points:
        for c in chains:
            if ready[c] == name:
                at[c] = now
        while True:
            due = [c for c in left() if at[c] <= now]
            if not due:
                break
            take(min(due, key=lambda c: at[c]), now, plan[name])
    now = points[-1][1]
    while left():
        c = min(left(), key=lambda c: at[c])
        now = max(now, at[c])
        take(c, now, tail)
    return plan, tail


def front_body(
    lens_ref, xin_ref, cin_ref, g1_in, b1_in, qb_in, vb_in, ob_in, g2_in, b2_in, pb_in, fb_in, wq_in, wo_in, wf_in, wp_in,
    x_out, joined_out, att_out, ext_out, hid_out, n2_out, act_out, der_out, out_out, cot_out, wq_out, wo_out, wf_out, wp_out, vecs_ref,
    wq_ref, wo_ref, wf_ref, wp_ref, xo_ref, xs_ref, xr_ref, co_ref, cs_ref, cr_ref, x_ref, cot_ref, small_ref, sm_ref,
    jn_ref, ks_ref, vs_ref, att_ref, ext_ref, hid_ref, n2_ref, act_ref, der_ref, acc_ref, obf_ref,
    wsend, wrecv, wload, wsave, xsend, xrecv, csem, ssem, lsem, osem, jsem, asem,
):
    rep, shard = place()
    rows, width = x_ref.shape
    nb = rows // BQ
    npair = width // 128
    nf = act_out.shape[0]
    across = (rep, 1 - shard)
    peers = [(rep ^ (1 << d), shard) for d in range(4)]
    core = rep & 1
    plan = Plan(lens_ref, shard, rows)
    bounds, slot = plan.bounds(), plan.away()

    parts = []
    for src, dst, nrows, ncols in ((wq_in, wq_ref, 1, 3), (wo_in, wo_ref, 1, 1), (wf_in, wf_ref, 1, 2), (wp_in, wp_ref, 2, 1)):
        size, cols = src.shape[0] // nrows, src.shape[1] // ncols
        for n in range(nrows * ncols):
            parts.append((src, dst, n // ncols * size, size, n % ncols * cols, cols, WAYS[len(parts)]))
    nparts = len(parts)
    early = 4

    def chain(n, step):
        src, dst, row, size, col, cols, way = parts[n]
        half, unit = src.shape[0], size >> len(way)
        index = sum(((rep >> d) & 1) << i for i, d in enumerate(way))
        count = 1 if step == 0 else 1 << (step - 1)
        first = row + ((index & ~(count - 1)) * unit if step <= len(way) else 0)
        here = pl.ds(pl.multiple_of(first, 16), count * unit)
        side = pl.ds(pl.multiple_of(col + core * (cols // 2), 128), cols // 2)
        sems = (wsend.at[n, step], wrecv.at[n, step])
        if step == 0:
            into = pl.ds(pl.multiple_of(shard * half + first, 16), unit)
            return remote(src.at[here, side], dst.at[into, side], *sems, across)
        into = pl.ds(pl.multiple_of((1 - shard) * half + first, 16), count * unit)
        return remote(dst.at[into, side], dst.at[into, side], *sems, peers[(way + (0,))[step - 1]])

    def hops(n):
        return len(parts[n][-1]) + 2

    def act(n, step):
        if step:
            chain(n, step - 1).wait_recv()
        if step < hops(n):
            chain(n, step).start()

    def expected(n):
        _src, _dst, _row, size, _col, cols, way = parts[n]
        mb = size * cols * 1e-6
        out = [(0, mb / LINK_RATE / (1 << len(way)), 1.5)]
        for i, d in enumerate(way):
            out.append((link_of(d)[0], mb / LINK_RATE * link_of(d)[1] / (1 << (len(way) - i)), 1.5))
        return out + [("core", mb / CORE_RATE, 1.0)]

    points, now = [], 21.0
    for i in range(nb):
        for name, long in [(("b", i), 2.0)] + [(("h", i, h), 0.5 + 0.55 * i) for h in range(npair)]:
            now += long
            points.append((name, now))
    first_ones = {n: expected(n) for n in range(early)}
    late_ones = {n: expected(n) for n in range(early, nparts)}
    starts = [("start", 3.0)] + [(("sx", i), 5.0 + 1.8 * i) for i in range(nb)] + [(("pk", i), 13.5 + 2.7 * i) for i in range(nb)]
    opening, opened = timetable(starts, first_ones, {n: "start" for n in first_ones}, {})
    busy = {0: 3.0 + sum(c[0][1] for c in first_ones.values()) + 2 * BQ * width * 2e-6 / LINK_RATE}
    agenda, closing = timetable([("start", 20.0)] + points, late_ones, {n: "start" for n in late_ones}, busy)

    whole = [(wq_in, wq_ref, wq_out), (wo_in, wo_ref, wo_out), (wf_in, wf_ref, wf_out), (wp_in, wp_ref, wp_out)]

    def half_rows(src, which):
        return pl.ds(pl.multiple_of(which * src.shape[0], 16), src.shape[0])

    def own_load(n):
        src, dst, _ = whole[n]
        return pltpu.make_async_copy(src, dst.at[half_rows(src, shard), :], wload.at[n])

    def other_save(n):
        src, dst, save = whole[n]
        return pltpu.make_async_copy(dst.at[half_rows(src, 1 - shard), :], save, wsave.at[n])

    x_load = pltpu.make_async_copy(xin_ref, xo_ref, lsem.at[0])
    c_load = pltpu.make_async_copy(cin_ref, co_ref, lsem.at[1])
    x_load.start()
    for n in range(4):
        own_load(n).start()
    c_load.start()
    hw = width // 2
    for n, ref in enumerate((g1_in, b1_in, qb_in, vb_in, ob_in, g2_in, b2_in, pb_in)):
        small_ref[n, :] = ref[...].astype(F32)
    for n in range(nf):
        small_ref[8 + n, :] = fb_in[n * hw : (n + 1) * hw].astype(F32)
    greet([across] + peers)
    small = remote(small_ref, sm_ref.at[shard], ssem.at[0], ssem.at[1], across)
    small.start()
    for n, step in opening["start"]:
        act(n, step)

    tail = plan.s0 + plan.s1
    theirs = jnp.where(plan.stays, rows, tail)
    split = jnp.where(plan.stays, rows, plan.s0)
    whole_one = jnp.where(plan.stays & (plan.slot == 1), 1, 0)

    def pack_sent(dst_ref, src_ref, i, upto):
        total = None
        for k in range(2):
            part = dot(moved_pick(jnp.where(slot == k, tail, rows), i, upto), src_ref[k, 0:upto, :])
            total = part if total is None else total + part
        dst_ref[rows_of(i, BQ), :] = total.astype(BF)

    def pack_own(dst_ref, src_ref, i):
        r = rows_of(i, BQ)
        row = i * BQ + lax.broadcasted_iota(jnp.int32, (BQ, width), 0)
        base = jnp.where(whole_one == 1, src_ref[1, r, :].astype(F32), src_ref[0, r, :].astype(F32))
        dst_ref[r, :] = jnp.where(row >= split, dot(moved_pick(split, i, rows), src_ref[1]), base).astype(BF)

    def merged(own_ref, got_ref, i):
        r = rows_of(i, BQ)
        row = i * BQ + lax.broadcasted_iota(jnp.int32, (BQ, width), 0)
        return jnp.where(row >= theirs, got_ref[r, :].astype(F32), own_ref[r, :].astype(F32)).astype(BF)

    def x_chunk(i):
        r = rows_of(i, BQ)
        return remote(xs_ref.at[r, :], xr_ref.at[r, :], xsend.at[i], xrecv.at[i], across)

    c_copy = remote(cs_ref, cr_ref, csem.at[0], csem.at[1], across)
    x_load.wait()

    def opened_at(i, name):
        for ii in range(nb):
            if opening[(name, ii)]:

                @pl.when(i == ii)
                def _():
                    for n, step in opening[(name, ii)]:
                        act(n, step)

    pack_sent(xs_ref, xo_ref, 0, BQ)
    x_chunk(0).start()
    for n, step in opening[("sx", 0)]:
        act(n, step)

    @pl.loop(1, nb)
    def _(i):
        pack_sent(xs_ref, xo_ref, i, rows)

        @pl.when(i == 2)
        def _():
            for n, step in agenda["start"]:
                act(n, step)

        x_chunk(i).start()
        opened_at(i, "sx")

    sm_ref[shard] = small_ref[...]
    small.wait()
    for n in range(8):
        for which in range(2):
            vecs_ref[n : n + 1, which * hw : (which + 1) * hw] = sm_ref[which, n : n + 1, :]
    for n in range(nf):
        for part in range(2):
            which, row = (2 * n + part) // nf, 8 + (2 * n + part) % nf
            vecs_ref[8 + n : 9 + n, part * hw : (part + 1) * hw] = sm_ref[which, row : row + 1, :]
    vecs_ref[8 + nf : 16, :] = jnp.zeros((8 - nf, width), F32)
    vecs_ref[JB : JB + 1, :] = vecs_ref[QB : QB + 1, :]
    vecs_ref[JB + 2 : JB + 3, :] = vecs_ref[VB : VB + 1, :]
    c_load.wait()

    @pl.loop(0, nb)
    def _(i):
        pack_own(x_ref, xo_ref, i)
        pack_sent(cs_ref, co_ref, i, rows)
        opened_at(i, "pk")

    c_copy.start()
    for n, step in opened:
        act(n, step)
    own_load(0).wait()
    own_load(1).wait()
    other_save(0).start()
    other_save(1).start()
    def at_point(name):
        for n, step in agenda[name]:
            act(n, step)

    gain, shift = vecs_ref[G1 : G1 + 1, :], vecs_ref[B1 : B1 + 1, :]
    lq = lane_half((BQ, 128))
    tri = lax.broadcasted_iota(jnp.int32, (BQ, BQ), 1) <= lax.broadcasted_iota(jnp.int32, (BQ, BQ), 0)
    def joined_save(i, b):
        r = pl.ds(i * BQ, BQ)
        return pltpu.make_async_copy(jn_ref.at[r, pl.ds(b * width, width)], joined_out.at[b, r, :], jsem.at[i, b])

    for i in range(nb):
        x_chunk(i).wait_recv()
        n = (i + 1) * BQ
        r = slice(i * BQ, n)
        xb = merged(x_ref, xr_ref, i)
        x_ref[r, :] = xb
        unit, _inv = norm_stats(xb.astype(F32))
        n1 = (unit * gain + shift).astype(BF)

        @pl.loop(0, 3)
        def _(b):
            c = span(b * width, width)
            jn_ref[r, c] = (dot(n1, wq_ref[:, c]) + vecs_ref[pl.ds(JB + b, 1), :]).astype(BF)

        for b in range(3):
            joined_save(i, b).start()
        at_point(("b", i))
        ohf = own_segment(bounds, i * BQ, BQ)
        oh = ohf.astype(BF)
        neg = other_segment(bounds, i * BQ, BQ).astype(BF)

        @pl.loop(0, npair)
        def _(h):
            k2 = jn_ref[r, pl.ds(pl.multiple_of(width + h * 128, 128), 128)]
            v2 = jn_ref[r, pl.ds(pl.multiple_of(2 * width + h * 128, 128), 128)]
            one = jnp.ones_like(v2)
            ks_ref[h, 0, r, :] = jnp.where(lq, k2, neg)
            ks_ref[h, 1, r, :] = jnp.where(lq, neg, k2)
            vs_ref[h, 0, r, :] = jnp.where(lq, v2, one)
            vs_ref[h, 1, r, :] = jnp.where(lq, one, v2)

        @pl.loop(0, npair)
        def _(h):
            cq = pl.ds(pl.multiple_of(h * 128, 128), 128)
            q2 = jn_ref[r, cq]
            qs = [jnp.where(lq, q2, oh), jnp.where(lq, oh, q2)]
            outs, exts = [], []
            for e in range(2):
                sd = jnp.where(tri, dot_nt(qs[e], ks_ref[h, e, r, :]), NEG)
                peak = jnp.max(sd, axis=1, keepdims=True)
                if i:
                    so = dot_nt(qs[e], ks_ref[h, e, 0 : n - BQ, :])
                    peak = jnp.maximum(peak, jnp.max(so, axis=1, keepdims=True))
                    po = jnp.exp2((so - peak) * EXPC).astype(BF)
                pd = jnp.exp2((sd - peak) * EXPC).astype(BF)
                acc = dot(pd, vs_ref[h, e, r, :])
                if i:
                    acc = acc + dot(po, vs_ref[h, e, 0 : n - BQ, :])
                outs.append(acc)
                tot = acc[:, HD : HD + 1] if e == 0 else acc[:, 0:1]
                exts.append(extra(ohf, -(peak + jnp.log(tot) * (1.0 / SCALE)), 3))
            num = jnp.where(lq, outs[0], outs[1])
            den = pltpu.roll(jnp.where(lq, outs[1], outs[0]), HD, 1)
            att_ref[r, cq] = (num / den).astype(BF)
            ext_ref[r, cq] = jnp.where(lq, exts[1], exts[0]).astype(BF)
            for hh in range(npair):
                if agenda[("h", i, hh)]:

                    @pl.when(h == hh)
                    def _():
                        at_point(("h", i, hh))

    x_save = pltpu.make_async_copy(x_ref, x_out, osem.at[0])
    att_save = pltpu.make_async_copy(att_ref, att_out, osem.at[1])
    ext_save = pltpu.make_async_copy(ext_ref, ext_out, osem.at[2])
    for copy in (x_save, att_save, ext_save):
        copy.start()

    gain2, shift2 = vecs_ref[G2 : G2 + 1, :], vecs_ref[B2 : B2 + 1, :]

    @pl.loop(0, nb)
    def _(i):
        r = rows_of(i, BQ)
        hid = x_ref[r, :].astype(F32) + (dot(att_ref[r, :], wo_ref[...]) + vecs_ref[OB : OB + 1, :])
        hid_ref[r, :] = hid
        unit, _inv = norm_stats(hid)
        n2_ref[r, :] = (unit * gain2 + shift2).astype(BF)
        acc_ref[r, :] = hid + vecs_ref[PB : PB + 1, :]

    hid_save = pltpu.make_async_copy(hid_ref, hid_out, osem.at[3])
    n2_save = pltpu.make_async_copy(n2_ref, n2_out, osem.at[4])
    hid_save.start()
    n2_save.start()

    def gelu_save(n):
        return (
            pltpu.make_async_copy(act_ref.at[n & 1], act_out.at[n], asem.at[0, n]),
            pltpu.make_async_copy(der_ref.at[n & 1], der_out.at[n], asem.at[1, n]),
        )

    for n, step in closing:
        act(n, step)
    own_load(2).wait()
    own_load(3).wait()
    other_save(2).start()
    other_save(3).start()

    @pl.loop(0, nf)
    def _(n):
        @pl.when(n >= 2)
        def _():
            for copy in gelu_save(n - 2):
                copy.wait()

        c = span(n * width, width)

        @pl.loop(0, nb)
        def _(i):
            r = rows_of(i, BQ)
            act, der = gelu_both(dot(n2_ref[r, :], wf_ref[:, c]) + vecs_ref[pl.ds(FB + n, 1), :])
            act = act.astype(BF)
            act_ref[n & 1, r, :] = act
            der_ref[n & 1, r, :] = der.astype(BF)
            acc_ref[r, :] += dot(act, wp_ref[c, :])

        for copy in gelu_save(n):
            copy.start()

    @pl.loop(0, nb)
    def _(i):
        r = rows_of(i, BQ)
        obf_ref[r, :] = acc_ref[r, :].astype(BF)

    out_save = pltpu.make_async_copy(obf_ref, out_out, osem.at[5])
    out_save.start()

    @pl.loop(0, nb)
    def _(i):
        pack_own(cot_ref, co_ref, i)

    c_copy.wait_recv()

    @pl.loop(0, nb)
    def _(i):
        cot_ref[rows_of(i, BQ), :] = merged(cot_ref, cr_ref, i)

    cot_save = pltpu.make_async_copy(cot_ref, cot_out, osem.at[6])
    cot_save.start()
    for n in range(nparts):
        for step in range(hops(n)):
            chain(n, step).wait_send()
    for i in range(nb):
        x_chunk(i).wait_send()
        for b in range(3):
            joined_save(i, b).wait()
    c_copy.wait_send()
    for n in range(4):
        other_save(n).wait()
    for n in range(max(0, nf - 2), nf):
        for copy in gelu_save(n):
            copy.wait()
    for copy in (x_save, att_save, ext_save, hid_save, n2_save, out_save, cot_save):
        copy.wait()


WAYS = [(2, 1), (1, 2), (2, 1), (1, 2), (3, 2, 1), (3, 1, 2), (3, 2, 1), (3, 1, 2)]


def front(lens, xin, cin, small, wq, wo, wf, wp):
    slots, rows, width = xin.shape
    ff = wf.shape[1]
    nf = ff // width
    nb = rows // BQ
    s = jax.ShapeDtypeStruct
    v = pltpu.VMEM
    act = s((rows, width), BF)
    nparts = len(WAYS)
    return pl.pallas_call(
        front_body,
        name="front",
        out_shape=(
            act, s((3, rows, width), BF), act, act, s((rows, width), F32), act, s((nf, rows, width), BF), s((nf, rows, width), BF),
            act, act, s(wq.shape, BF), s(wo.shape, BF), s(wf.shape, BF), s(wp.shape, BF), s((16, width), F32),
        ),
        in_specs=[SMEM] + anyspecs(2) + vspecs(9) + anyspecs(4),
        out_specs=tuple(anyspecs(14) + vspecs(1)),
        scratch_shapes=[
            v((width, 3 * width), BF), v((width, width), BF), v((width, ff), BF), v((ff, width), BF),
            v((slots, rows, width), BF), v((rows, width), BF), v((rows, width), BF),
            v((slots, rows, width), BF), v((rows, width), BF), v((rows, width), BF),
            v((rows, width), BF), v((rows, width), BF), v((16, width // 2), F32), v((2, 16, width // 2), F32),
            v((rows, 3 * width), BF), v((width // 128, 2, rows, 128), BF), v((width // 128, 2, rows, 128), BF),
            v((rows, width), BF), v((rows, width), BF), v((rows, width), F32), v((rows, width), BF),
            v((2, rows, width), BF), v((2, rows, width), BF), v((rows, width), F32), v((rows, width), BF),
            DMA((nparts, 5)), DMA((nparts, 5)), DMA((4,)), DMA((4,)), DMA((nb,)), DMA((nb,)), DMA((2,)), DMA((2,)), DMA((2,)),
            DMA((7,)), DMA((nb, 3)), DMA((2, nf)),
        ],
        compiler_params=params(collective_id=0, has_side_effects=True),
        cost_estimate=cost(40e9, 60e6, 12e6),
    )(lens, xin, cin, *small, wq, wo, wf, wp)


def back_body(
    bits, lens_ref, vecs_ref, x_in, joined_in, att_in, ext_in, hid_in, n2_in, act_in, der_in, out_in, cot_in,
    wq_own, wo_own, wf_own, wp_own, wq_oth, wo_oth, wf_oth, wp_oth,
    res_out, dx_out, dxr_out, outr_out, sums_ref,
    wf_ref, wp_ref, wo_ref, wq_ref, cot_ref, n2_ref, act_ref, der_ref, gpre_ref, acc_ref, hid_ref, att_ref,
    gm_ref, r0_ref, rb_ref, res_ref, sm_ref, smb_ref, smr_ref,
    wsem, lsem, asem, hsem, ssem, rsem, msem, mrem, osem, dsem, drem, vsem, fsem,
):
    rep, shard = place()
    core = rep & 1
    rows, width = cot_ref.shape
    hw = width // 2
    nb = rows // BQ
    nf = act_in.shape[0]
    npair = width // 128
    m = bits - 1
    sibling, across = (rep ^ 1, shard), (rep, 1 - shard)
    peers = {0: across}
    for t in range(1, bits):
        peers[t] = (rep ^ (1 << t), shard)
    plan = Plan(lens_ref, shard, rows)
    bounds = plan.bounds()

    def weight_loads(own, oth, dst, into):
        half = own.shape[0]
        for n, (src, which) in enumerate(((own, shard), (oth, 1 - shard))):
            yield n, src, dst.at[pl.ds(pl.multiple_of(into + which * half, 16), half), :]

    def fc_loads(j):
        for n, src, dst in weight_loads(wf_own, wf_oth, wf_ref, j * width):
            for part in range(2):
                here = span((part * nf + j) * hw, hw)
                yield pltpu.make_async_copy(src.at[:, here], dst.at[:, pl.ds(part * hw, hw)], wsem.at[0, n, part, j])

    def proj_loads(j):
        for n, (src, which) in enumerate(((wp_own, shard), (wp_oth, 1 - shard))):
            into = pl.ds(pl.multiple_of(j * width + which * hw, 16), hw)
            yield pltpu.make_async_copy(src.at[span(j * hw, hw), :], wp_ref.at[into, :], wsem.at[1, n, 0, j])

    def gelu_loads(k, j):
        src, dst = ((act_in, act_ref), (der_in, der_ref))[k]
        for part in range(2):
            block = part * (nf // 2) + (j >> 1)
            here = span((j & 1) * hw, hw)
            yield pltpu.make_async_copy(src.at[block, :, here], dst.at[j & 1, :, pl.ds(part * hw, hw)], asem.at[k, part, j])

    def plain(n, src, dst):
        return pltpu.make_async_copy(src, dst, lsem.at[n])

    cot_load, n2_load, att_load = plain(0, cot_in, cot_ref), plain(1, n2_in, n2_ref), plain(2, att_in, att_ref)
    wo_loads = [pltpu.make_async_copy(s_, d_, wsem.at[2, n, 0, 0]) for n, s_, d_ in weight_loads(wo_own, wo_oth, wo_ref, 0)]
    wq_loads = [pltpu.make_async_copy(s_, d_, wsem.at[2, n, 0, 1]) for n, s_, d_ in weight_loads(wq_own, wq_oth, wq_ref, 0)]
    x_load, ext_load = plain(3, x_in, act_ref.at[0]), plain(4, ext_in, der_ref.at[0])
    joined_loads = [plain(5 + b, joined_in.at[b], wf_ref.at[pl.ds(b * rows, rows), :]) for b in range(3)]

    def hid_load(i):
        return pltpu.make_async_copy(hid_in.at[span(i * BQ, BQ), :], hid_ref.at[i & 1], hsem.at[i])

    cot_load.start()
    for j in range(2):
        for copy in list(gelu_loads(0, j)) + list(proj_loads(j)) + list(gelu_loads(1, j)) + list(fc_loads(j)):
            copy.start()
        if j == 0:
            n2_load.start()
    greet([sibling, across] + [peers[t] for t in range(1, bits)])

    per = gm_ref.shape[3] // PIECE
    pieces = pieces_of(per, hw)
    count = len(pieces)
    last = 3 + 2 * m
    orders = [PATHS[k] + tuple(range(4, bits)) for k in range(count)]

    def source(k, away):
        n, c = pieces[k]
        a, at = n // per, pl.ds((n % per) * PIECE, PIECE)
        return gm_ref.at[away, a, :, at, c] if a < 2 else gm_ref.at[1, away, :, at, c]

    def place_of(ref, k):
        n, c = pieces[k]
        return ref.at[n, :, :, c]

    def result_of(ref, k):
        n, c = pieces[k]
        return ref.at[n, :, c]

    def held(k, i):
        half, first, size = None, 0, PIECE
        for d in orders[k][:i]:
            if d == 0:
                half = shard
            else:
                size //= 2
                first = first + ((rep >> d) & 1) * size
        return half, first, size

    def at_rows(first, size):
        return pl.ds(pl.multiple_of(first, 16), size)

    def landing(k, i):
        d = orders[k][i]
        half, _first, size = held(k, i + 1)
        before = sum(PIECE >> (n + 1) for n in range(len([e for e in orders[k][:i] if e])))
        if d == 0:
            return place_of(rb_ref, k).at[0, pl.ds(before, size), :]
        at = pl.ds(before, size)
        return place_of(rb_ref, k).at[:, at, :] if half is None else place_of(rb_ref, k).at[1, at, :]

    def leaving(k, i):
        d = orders[k][i]
        half, first, size = held(k, i)
        own = source(k, 0)
        if d == 0:
            return own.at[1 - shard, at_rows(first, size), :]
        size //= 2
        at = at_rows(first + (1 - ((rep >> d) & 1)) * size, size)
        return own.at[:, at, :] if half is None else own.at[half, at, :]

    def copy(k, step):
        sems = (ssem.at[step, k], rsem.at[step, k])
        if step == 0:
            return remote(source(k, 1), place_of(r0_ref, k), *sems, sibling)
        if step <= m + 1:
            return remote(leaving(k, step - 1), landing(k, step - 1), *sems, peers[orders[k][step - 1]])
        if step <= 2 * m + 1:
            back = [d for d in orders[k] if d]
            t = m - (step - m - 2)
            size = PIECE >> t
            first = 0
            for n in range(t):
                first = first + ((rep >> back[n]) & 1) * (PIECE >> (n + 1))
            here = result_of(res_ref, k).at[at_rows(first, size), :]
            return remote(here, here, *sems, peers[back[t - 1]])
        return remote(result_of(res_ref, k), result_of(res_out.at[core], k), *sems, sibling)

    def keep(k):
        return pltpu.make_async_copy(result_of(res_ref, k), result_of(res_out.at[core], k), fsem.at[k])

    def add(dst, first, other, base, size, out=None):
        chunk = min(size, 64)

        @pl.loop(0, size // chunk)
        def _(i):
            at = pl.ds(pl.multiple_of(first + i * chunk, 16), chunk)
            total = dst[at, :].astype(F32) + other[pl.ds(pl.multiple_of(base + i * chunk, 16), chunk), :].astype(F32)
            (dst if out is None else out)[at, :] = total.astype(BF)

    def act_step(k, step):
        if step:
            copy(k, step - 1).wait_recv()
        own = source(k, 0)
        if step == 1:
            for h in range(2):
                add(own.at[h], 0, place_of(r0_ref, k).at[h], 0, PIECE)
        elif 2 <= step <= m + 2:
            i = step - 2
            half, first, size = held(k, i + 1)
            land = landing(k, i)
            if half is None:
                for h in range(2):
                    add(own.at[h], first, land.at[h], 0, size)
            else:
                add(own.at[half], first, land, 0, size, result_of(res_ref, k) if i == m else None)
        if step < last:
            copy(k, step).start()
        if step == last - 1:
            keep(k).start()

    def small_copy(step):
        src = sm_ref if step == 0 else smb_ref.at[step - 1]
        return remote(src, smr_ref.at[step], msem.at[step], mrem.at[step], small_peers[step])

    def small_step(step):
        if step:
            small_copy(step - 1).wait_recv()
            before = sm_ref[...] if step == 1 else smb_ref[step - 2]
            total = before + smr_ref[step - 1]
            if step == 2 + m:
                sums_ref[...] = total
            else:
                smb_ref[step - 1] = total
        if step < 2 + m:
            small_copy(step).start()

    def dx_chunk(i):
        at = pl.ds(i * BQ, BQ)
        return remote(dxb_ref.at[at, :], dxr_out.at[at, :], dsem.at[i], drem.at[i], across)

    def dx_step(i):
        if i:
            dx_chunk(i - 1).wait_send()
        if i < nb:
            dx_chunk(i).start()

    def out_chunk(i):
        at = pl.ds(i * BQ, BQ)
        return remote(out_in.at[at, :], outr_out.at[at, :], osem.at[0, i], osem.at[1, i], across)

    def out_step(i):
        if i:
            out_chunk(i - 1).wait_send()
        if i < nb:
            out_chunk(i).start()

    def act(c, step):
        if c == "out":
            out_step(step)
        elif c == "small":
            small_step(step)
        elif c == "dx":
            dx_step(step)
        else:
            act_step(c, step)

    small_peers = [sibling, across] + [peers[t] for t in range(1, bits)]
    xb_ref, eb_ref, n1_ref, dxb_ref = act_ref.at[0], der_ref.at[0], der_ref.at[1], act_ref.at[1]

    points, now = [], 5.0
    for name, long in (
        [(("gp", j), 1.9) for j in range(nf)]
        + [(("ff", j, n), (4.1, 2.2)[n]) for j in range(nf) for n in range(2)]
        + [(("hid", i), 1.6) for i in range(nb)]
        + [("go", 2.0)]
        + [p for t in range(THIRDS) for p in [(("at", t, p, i), 0.72 * (i + 1)) for p in range(npair // THIRDS) for i in range(nb)] + [(("gw", t), 2.0)]]
        + [(("dx", i), 2.0) for i in range(nb)]
    ):
        now += long
        points.append((name, now))
    chains, ready = {}, {}
    for k, (n, c) in enumerate(pieces):
        half_mb = 2 * PIECE * (c.stop - c.start) / 1e6
        steps, size = [("core", 2 * half_mb / CORE_RATE, 1.0)], 2 * half_mb
        for d in orders[k]:
            size /= 2
            steps.append((link_of(d)[0], size / LINK_RATE * link_of(d)[1], 1.5))
        size = half_mb / (1 << m)
        for d in reversed([d for d in orders[k] if d]):
            steps.append((link_of(d)[0], size / LINK_RATE * link_of(d)[1], 1.5))
            size *= 2
        chains[k] = steps + [("core", half_mb / CORE_RATE, 1.0)]
        ready[k] = ("ff", 1 + n, 1) if n < per else ("gp", 1 + n - per) if n < 2 * per else ("gw", n - 2 * per)
    small_us = 24 * width * 4e-6 / LINK_RATE
    chains["small"] = [("core", 0.5, 1.0), (0, small_us, 1.5)] + [(link_of(d)[0], small_us * link_of(d)[1], 1.5) for d in range(1, bits)]
    chains["dx"] = [(0, BQ * width * 2e-6 / LINK_RATE, 0.0)] * nb
    chains["out"] = chains["dx"]
    ready["small"], ready["dx"], ready["out"] = ("dx", nb - 1), ("dx", 0), OUT_AT
    agenda, tail = timetable(points, chains, ready, {})

    def at_point(name):
        for c, step in agenda[name]:
            act(c, step)

    gbase = 16
    sm_ref[...] = jnp.zeros_like(sm_ref)

    @pl.loop(0, nb)
    def _(i):
        acc_ref[rows_of(i, BQ), :] = jnp.zeros((BQ, width), F32)

    def at_step(j, name):
        for jj in range(nf):
            if agenda[name(jj)]:

                @pl.when(j == jj)
                def _():
                    at_point(name(jj))

    cot_load.wait()

    @pl.loop(0, nf)
    def _(j):
        for c in gelu_loads(0, j):
            c.wait()
        into = span(j * hw, hw)
        for h in range(2):
            gp = dot_tn(act_ref[j & 1, :, h * hw : (h + 1) * hw], cot_ref[...]).astype(BF)
            for c in range(2):
                gm_ref[c ^ core, 1, h, into, :] = gp[:, c * hw : (c + 1) * hw]

        @pl.when(j < nf - 2)
        def _():
            for c in gelu_loads(0, j + 2):
                c.start()

        at_step(j, lambda jj: ("gp", jj))

    n2_load.wait()

    @pl.loop(0, nf)
    def _(j):
        for c in list(proj_loads(j)) + list(gelu_loads(1, j)) + list(fc_loads(j)):
            c.wait()

        @pl.when(j < nf - 2)
        def _():
            for c in list(proj_loads(j + 2)) + list(fc_loads(j + 2)):
                c.start()

        here, into, bias = span(j * width, width), span(j * hw, hw), pl.ds(gbase + j, 1)

        @pl.loop(0, nb)
        def _(i):
            r = rows_of(i, BQ)
            gact = dot_nt(cot_ref[r, :], wp_ref[here, :])
            gpre = (gact * der_ref[j & 1, r, :].astype(F32)).astype(BF)
            gpre_ref[r, :] = gpre
            sm_ref[bias, :] += jnp.sum(gpre.astype(F32), axis=0, keepdims=True)
            acc_ref[r, :] += dot_nt(gpre, wf_ref[here, :])

        at_step(j, lambda jj: ("ff", jj, 0))
        for h in range(2):
            gf = dot_tn(n2_ref[:, h * hw : (h + 1) * hw], gpre_ref[...]).astype(BF)
            for c in range(2):
                gm_ref[c ^ core, 0, h, into, :] = gf[:, c * hw : (c + 1) * hw]

        @pl.when(j < nf - 2)
        def _():
            for c in gelu_loads(1, j + 2):
                c.start()

        @pl.when(j == nf - 2)
        def _():
            for c in [x_load, ext_load, att_load] + wo_loads + wq_loads:
                c.start()
            hid_load(0).start()
            hid_load(1).start()

        at_step(j, lambda jj: ("ff", jj, 1))

    for c in joined_loads:
        c.start()
    for c in [att_load] + wo_loads:
        c.wait()
    gain2 = vecs_ref[G2 : G2 + 1, :]
    gatt_ref = cot_ref

    def at_block(i, name):
        for ii in range(nb):
            if agenda[(name, ii)]:

                @pl.when(i == ii)
                def _():
                    at_point((name, ii))

    @pl.loop(0, nb)
    def _(i):
        r = rows_of(i, BQ)
        hid_load(i).wait()
        unit, inv = norm_stats(hid_ref[i & 1])
        gn2 = acc_ref[r, :]
        gy = cot_ref[r, :].astype(F32)
        ghid = gy + norm_back(gn2, unit, inv, gain2)

        @pl.when(i < nb - 2)
        def _():
            hid_load(i + 2).start()

        acc_ref[r, :] = ghid
        low = ghid.astype(BF)
        gpre_ref[r, :] = low
        gatt_ref[r, :] = dot_nt(low, wo_ref[...]).astype(BF)
        sm_ref[0:1, :] += jnp.sum(gn2 * unit, axis=0, keepdims=True)
        sm_ref[1:2, :] += jnp.sum(gn2, axis=0, keepdims=True)
        sm_ref[2:3, :] += jnp.sum(gy, axis=0, keepdims=True)
        sm_ref[3:4, :] += jnp.sum(low.astype(F32), axis=0, keepdims=True)
        at_block(i, "hid")

    x_load.wait()
    gain1, shift1 = vecs_ref[G1 : G1 + 1, :], vecs_ref[B1 : B1 + 1, :]

    @pl.loop(0, nb)
    def _(i):
        r = rows_of(i, BQ)
        unit, _inv = norm_stats(xb_ref[r, :].astype(F32))
        n1_ref[r, :] = (unit * gain1 + shift1).astype(BF)

    aways = [k for k, (n, _) in enumerate(pieces) if n < 2 * per]
    for k in aways:
        copy(k, 0).wait_send()
    for h in range(2):
        go = dot_tn(att_ref[:, h * hw : (h + 1) * hw], gpre_ref[...]).astype(BF)
        for c in range(2):
            gm_ref[1, c ^ core, h, 0:hw, :] = go[:, c * hw : (c + 1) * hw]
    at_point("go")
    for c in joined_loads + [ext_load]:
        c.wait()

    lq = lane_half((BQ, 128))
    tri = lax.broadcasted_iota(jnp.int32, (BQ, BQ), 0) <= lax.broadcasted_iota(jnp.int32, (BQ, BQ), 1)
    left = lane_half((rows, 128))
    ones = lax.broadcasted_iota(jnp.int32, (rows, 128), 1) % HD
    ones = (ones >= 3) & (ones < 6)
    tcols = width // THIRDS
    here_at = lambda t, p, i: agenda[("at", t, p, i)]

    def head_pair(t, p):
        h = t * (npair // THIRDS) + p
        col = pl.ds(pl.multiple_of(h * 128, 128), 128)
        k2 = wf_ref[rows : 2 * rows, col]
        v2 = wf_ref[2 * rows : 3 * rows, col]
        zero = jnp.zeros_like(k2)
        kx = jnp.where(ones, 1.0, other_segment(bounds, 0, rows)).astype(BF)
        vx = jnp.where(ones, 1.0, 0.0).astype(BF)
        ks = [jnp.where(left, k2, kx), jnp.where(left, kx, k2)]
        vs = [jnp.where(left, v2, vx), jnp.where(left, vx, v2)]
        km = [jnp.where(left, k2, zero), jnp.where(left, zero, k2)]
        hid_ref[...] = jnp.zeros_like(hid_ref)
        for i in range(nb):
            r = slice(i * BQ, (i + 1) * BQ)
            q2 = wf_ref[r, col]
            g2 = gatt_ref[r, col]
            ext = eb_ref[r, col]
            zq = jnp.zeros_like(q2)
            prod = g2.astype(F32) * att_ref[r, col].astype(F32)
            d0 = jnp.sum(jnp.where(lq, prod, 0.0), axis=1, keepdims=True)
            d1 = jnp.sum(jnp.where(lq, 0.0, prod), axis=1, keepdims=True)
            zf = jnp.zeros((BQ, 128), F32)
            qs = [jnp.where(lq, q2, ext), jnp.where(lq, ext, q2)]
            gs = [jnp.where(lq, g2, extra(zf, -d0, 3).astype(BF)), jnp.where(lq, extra(zf, -d1, 3).astype(BF), g2)]
            qm = [jnp.where(lq, q2, zq), jnp.where(lq, zq, q2)]
            gm = [jnp.where(lq, g2, zq), jnp.where(lq, zq, g2)]
            dq = None
            for u in range(i + 1):
                b = slice(u * BQ, (u + 1) * BQ)
                dk = dv = None
                for e in range(2):
                    st = dot_nt(ks[e][b], qs[e])
                    if u == i:
                        st = jnp.where(tri, st, NEG)
                    pt = jnp.exp2(st * EXPC)
                    dst = (pt * dot_nt(vs[e][b], gs[e])).astype(BF)
                    one, two, three = dot(pt.astype(BF), gm[e]), dot(dst, qm[e]), dot_tn(dst, km[e][b])
                    dv = one if dv is None else dv + one
                    dk = two if dk is None else dk + two
                    dq = three if dq is None else dq + three
                hid_ref[1, :, u * 128 : (u + 1) * 128] += dv
                hid_ref[0, :, u * 128 : (u + 1) * 128] += dk
            wp_ref[r, col] = (dq * SCALE).astype(BF)
            for tt in range(THIRDS):
                for pp in range(npair // THIRDS):
                    if here_at(tt, pp, i):

                        @pl.when((t == tt) & (p == pp))
                        def _():
                            for c, step in here_at(tt, pp, i):
                                act(c, step)

        for u in range(nb):
            wp_ref[rows + u * BQ : rows + (u + 1) * BQ, col] = (hid_ref[0, :, u * 128 : (u + 1) * 128] * SCALE).astype(BF)
            wp_ref[2 * rows + u * BQ : 2 * rows + (u + 1) * BQ, col] = hid_ref[1, :, u * 128 : (u + 1) * 128].astype(BF)

    @pl.loop(0, THIRDS)
    def _(t):
        @pl.loop(0, npair // THIRDS)
        def _(p):
            head_pair(t, p)

        cols = pl.ds(pl.multiple_of(t * tcols, 128), tcols)
        into = pl.ds(pl.multiple_of(hw + t * hw, 128), hw)
        cut = hw - tcols
        for h in range(2):
            n1h = n1_ref[:, h * hw : (h + 1) * hw]
            gq, gk, gv = [dot_tn(n1h, wp_ref[b * rows : (b + 1) * rows, cols]).astype(BF) for b in range(3)]
            gm_ref[1, core, h, into, 0:tcols] = gq
            gm_ref[1, core, h, into, tcols:hw] = gk[:, 0:cut]
            gm_ref[1, 1 - core, h, into, 0:cut] = gk[:, cut:tcols]
            gm_ref[1, 1 - core, h, into, cut:hw] = gv
        for b in (0, 2):
            sm_ref[8 + b : 9 + b, cols] = jnp.sum(wp_ref[b * rows : (b + 1) * rows, cols].astype(F32), axis=0, keepdims=True)
        for tt in range(THIRDS):
            if agenda[("gw", tt)]:

                @pl.when(t == tt)
                def _():
                    at_point(("gw", tt))

    for c in wq_loads:
        c.wait()

    @pl.loop(0, nb)
    def _(i):
        r = rows_of(i, BQ)
        gn1 = dot_nt(wp_ref[r, :], wq_ref[:, 0:width])
        for b in (1, 2):
            gn1 = gn1 + dot_nt(wp_ref[span(b * rows + i * BQ, BQ), :], wq_ref[:, b * width : (b + 1) * width])
        unit, inv = norm_stats(xb_ref[r, :].astype(F32))
        dxb_ref[r, :] = (acc_ref[r, :] + norm_back(gn1, unit, inv, gain1)).astype(BF)
        sm_ref[11:12, :] += jnp.sum(gn1 * unit, axis=0, keepdims=True)
        sm_ref[12:13, :] += jnp.sum(gn1, axis=0, keepdims=True)
        at_block(i, "dx")

    dx_save = plain(8, dxb_ref, dx_out)
    dx_save.start()

    for c, step in tail:
        act(c, step)
    for k in range(count):
        for step in range(last):
            if step or k not in aways:
                copy(k, step).wait_send()
        keep(k).wait()
    for step in range(2 + m):
        small_copy(step).wait_send()
    for i in range(nb):
        out_chunk(i).wait_recv()
        dx_chunk(i).wait_recv()
    dx_save.wait()


THIRDS = 3
CORE_RATE, LINK_RATE = 0.15, 0.045
OUT_AT = ("gp", 0)
PATHS = [(2, 1, 0, 3), (1, 0, 3, 2), (1, 0, 2, 3), (1, 2, 0, 3), (0, 1, 2, 3), (1, 2, 0, 3), (1, 0, 2, 3), (0, 1, 2, 3), (2, 1, 0, 3), (1, 2, 3, 0), (0, 1, 2, 3)]


def pieces_of(per, columns):
    out = [(n, slice(0, columns)) for n in range(3 * per - 1)]
    return out + [(3 * per - 1, slice(c, c + 128)) for c in range(0, columns, 128)]


def back(bits, lens, vecs, saved, own, oth):
    x, joined, att, ext, hid, n2, act, der, out, cot = saved
    rows, width = x.shape
    nf = act.shape[0]
    nb = rows // BQ
    hw = width // 2
    m = bits - 1
    per = nf * hw // PIECE
    wholes, count = 3 * per, len(pieces_of(per, hw))
    s = jax.ShapeDtypeStruct
    v = pltpu.VMEM
    sums = (24, width)
    return pl.pallas_call(
        functools.partial(back_body, bits),
        name="back",
        out_shape=(s((2, wholes, PIECE, hw), BF), s((rows, width), BF), s((rows, width), BF), s((rows, width), BF), s(sums, F32)),
        in_specs=[SMEM] + vspecs(1) + anyspecs(18),
        out_specs=tuple(anyspecs(4) + vspecs(1)),
        scratch_shapes=[
            v((nf * width, width), BF), v((nf * width, width), BF), v((width, width), BF), v((width, 3 * width), BF),
            v((rows, width), BF), v((rows, width), BF), v((2, rows, width), BF), v((2, rows, width), BF), v((rows, width), BF),
            v((rows, width), F32), v((2, BQ, width), F32), v((rows, width), BF),
            v((2, 2, 2, nf * hw, hw), BF), v((wholes, 2, PIECE, hw), BF), v((wholes, 2, PIECE, hw), BF), v((wholes, PIECE, hw), BF),
            v(sums, F32), v((m + 1,) + sums, F32), v((m + 2,) + sums, F32),
            DMA((3, 2, 2, nf)), DMA((9,)), DMA((2, 2, nf)), DMA((nb,)), DMA((3 + 2 * m, count)), DMA((3 + 2 * m, count)),
            DMA((m + 2,)), DMA((m + 2,)), DMA((2, nb)), DMA((nb,)), DMA((nb,)), DMA((1,)), DMA((count,)),
        ],
        compiler_params=params(collective_id=1, has_side_effects=True),
        cost_estimate=cost(60e9, 60e6, 8e6),
    )(lens, vecs, *saved, *own, *oth)


def finish_body(
    lens_ref, deal_ref, sums_ref, res_in, dx_in, dxr_in, out_in, outr_in, y_out, d_out, *rest
):
    outs, scratch = rest[:13], rest[13:]
    (o_g1, o_b1, o_qkv, o_qb, o_vb, o_wo, o_ob, o_g2, o_b2, o_fc, o_fb, o_proj, o_pb) = outs
    res_ref, src_ref, y_ref, qkv_ref, wo_ref, fc_ref, proj_ref, lsem, ssem = scratch
    shard = lax.axis_index("shard")
    rows, width = src_ref.shape[1:]
    hw = width // 2
    nb = rows // BQ
    slots = y_ref.shape[1]
    nf = fc_ref.shape[1] // width
    plan = Plan(lens_ref, shard, rows)
    loads = [pltpu.make_async_copy(a, src_ref.at[n], lsem.at[n]) for n, a in enumerate((out_in, outr_in, dx_in, dxr_in))]
    per = res_in.shape[1] // 3
    pieces = [pltpu.make_async_copy(res_in.at[:, pl.ds(per * a, per)], res_ref.at[:, pl.ds(per * a, per)], lsem.at[4 + a]) for a in range(3)]
    for copy in loads + pieces:
        copy.start()
    own = pl.ds(pl.multiple_of(shard * hw, 128), hw)
    for ref, row in ((o_g1, 11), (o_b1, 12), (o_qb, 8), (o_vb, 10), (o_ob, 3), (o_g2, 0), (o_b2, 1), (o_pb, 2)):
        ref[...] = sums_ref[row, own]
    for j in range(nf):
        o_fb[j * hw : (j + 1) * hw] = sums_ref[16 + j, own]

    def save(n, src, dst):
        return pltpu.make_async_copy(src, dst, ssem.at[n])

    saves = []
    for g in range(2):
        loads[2 * g].wait()
        loads[2 * g + 1].wait()
        for j in range(slots):
            q = slots * shard + j
            if g == 0:
                q = sum(jnp.where(q == n, deal_ref[0, n], 0) for n in range(2 * slots))
            side, offset, size = plan.where(q)

            @pl.loop(0, nb)
            def _(i):
                low, pick = window_pick(rows, i * BQ + offset, BQ)
                row = i * BQ + lax.broadcasted_iota(jnp.int32, pick.shape, 0)
                pick = jnp.where(pick & (row < size), 1.0, 0.0).astype(BF)
                y_ref[g, j, rows_of(i, BQ), :] = dot(pick, src_ref[2 * g + side, pl.ds(low, WINDOW), :]).astype(BF)

            saves.append(save(2 * g + j, y_ref.at[g, j], (y_out, d_out)[g].at[j]))
            saves[-1].start()
    block = lambda c, a, n, r, size: res_ref[c, a * per + (n * hw + r) // PIECE, (n * hw + r) % PIECE : (n * hw + r) % PIECE + size, :]
    for a, (dst, out) in enumerate(((fc_ref, o_fc), (proj_ref, o_proj), (qkv_ref, o_qkv))):
        pieces[a].wait()
        for n in range(nf):
            for c in range(2):
                for r in range(0, hw, 128):
                    value = block(c, a, n, r, 128).astype(F32)
                    at = slice(r, r + 128)
                    if a == 0:
                        fc_ref[at, (c * nf + n) * hw : (c * nf + n + 1) * hw] = value
                    elif a == 1:
                        proj_ref[n * hw + r : n * hw + r + 128, c * hw : (c + 1) * hw] = value
                    elif n == 0:
                        wo_ref[at, c * hw : (c + 1) * hw] = value
                    else:
                        tcols = width // THIRDS
                        cut, lead = hw - tcols, (n - 1) * tcols
                        if c == 0:
                            qkv_ref[at, lead : lead + tcols] = value[:, 0:tcols]
                            qkv_ref[at, width + lead : width + lead + cut] = value[:, tcols:hw]
                        else:
                            qkv_ref[at, width + lead + cut : width + lead + tcols] = value[:, 0:cut]
                            qkv_ref[at, 2 * width + lead : 2 * width + lead + tcols] = value[:, cut:hw]
        saves.append(save(4 + a, dst, out))
        saves[-1].start()
    saves.append(save(7, wo_ref, o_wo))
    saves[-1].start()
    for copy in saves:
        copy.wait()


def finish(lens, deal, sums, res, dx, dxr, out, outr, slots):
    rows, width = dx.shape
    hw = width // 2
    nf = res.shape[1] * PIECE // 3 // hw
    s = jax.ShapeDtypeStruct
    v = pltpu.VMEM
    vec, act = s((hw,), F32), s((slots, rows, width), BF)
    wide = lambda a, b: s((a, b), F32)
    vs, an = vspecs(1), anyspecs(1)
    return pl.pallas_call(
        finish_body,
        name="finish",
        out_shape=(act, act, vec, vec, wide(hw, 3 * width), vec, vec, wide(hw, width), vec, vec, vec, wide(hw, nf * width),
                   s((nf * hw,), F32), wide(nf * hw, width), vec),
        in_specs=[SMEM, SMEM] + vs + anyspecs(5),
        out_specs=tuple(an * 2 + vs * 2 + an + vs * 2 + an + vs * 3 + an + vs + an + vs),
        scratch_shapes=[
            v(res.shape, BF), v((4, rows, width), BF), v((2, slots, rows, width), BF),
            v((hw, 3 * width), F32), v((hw, width), F32), v((hw, nf * width), F32), v((nf * hw, width), F32), DMA((7,)), DMA((8,)),
        ],
        compiler_params=params(),
        cost_estimate=cost(8e9, 34e6),
    )(lens, deal, sums, res, dx, dxr, out, outr)


def local(bits, layer_in, cotangent, lengths, dealing, g1, b1, wqkv, qb, vb, wout, ob, g2, b2, wfc, bfc, wproj, pb):
    slots, rows, width = layer_in.shape
    own = (wqkv, wout, wfc, wproj)
    got = front(lengths, layer_in, cotangent, (g1, b1, qb, vb, ob, g2, b2, pb, bfc), *own)
    saved, oth, vecs = got[:10], got[10:14], got[14]
    res, dx, dxr, outr, sums = back(bits, lengths, vecs, saved, own, oth)
    return finish(lengths, dealing, sums, res, dx, dxr, saved[8], outr, slots)


def solution(mesh):
    both, one = P(("rep", "shard"), None, None), P("shard")
    mat = P("shard", None)
    in_specs = (both, both, P("rep", None), P("rep", None), one, one, mat, one, one, mat, one, one, one, mat, one, mat, one)
    out_specs = (both, both, one, one, mat, one, one, mat, one, one, one, mat, one, mat, one)
    bits = mesh.shape["rep"].bit_length() - 1
    return jax.shard_map(functools.partial(local, bits), mesh=mesh, in_specs=in_specs, out_specs=out_specs, check_vma=False)
```

```python
import functools

import jax
import jax.numpy as jnp
from jax import lax
from jax.experimental import pallas as pl
from jax.experimental.pallas import tpu as pltpu
from jax.sharding import PartitionSpec as P

HD = 64
BQ = 256
EPS = 1e-05
BF = jnp.bfloat16
F32 = jnp.float32
NEG = -1e30
LOG2E = 1.4426950408889634
SCALE = HD**-0.5
EXPC = SCALE * LOG2E
VLIM = 66_900_000
GELU_A = 0.7978845608028654
GELU_B = 0.044715
MESH = pl.DeviceIdType.MESH
PIECE = 512
WINDOW = 384
G1, B1, QB, VB, OB, G2, B2, PB, FB = range(9)
JB = 12


def dot(a, b):
    return jnp.dot(a, b, preferred_element_type=F32)


def dot_tn(a, b):
    return lax.dot_general(a, b, (((0,), (0,)), ((), ())), preferred_element_type=F32)


def dot_nt(a, b):
    return lax.dot_general(a, b, (((1,), (1,)), ((), ())), preferred_element_type=F32)


def norm_stats(v):
    mean = jnp.mean(v, axis=-1, keepdims=True)
    cen = v - mean
    inv = lax.rsqrt(jnp.mean(cen * cen, axis=-1, keepdims=True) + EPS)
    return cen * inv, inv


def norm_back(grad, unit, inv, gain):
    e = grad * gain
    m1 = jnp.mean(e, axis=-1, keepdims=True)
    m2 = jnp.mean(e * unit, axis=-1, keepdims=True)
    return inv * (e - m1 - unit * m2)


def rows_of(i, size):
    return pl.ds(pl.multiple_of(i * size, size), size)


def span(first, size):
    return pl.ds(first if isinstance(first, int) else pl.multiple_of(first, 128), size)


def lane_half(shape):
    return lax.broadcasted_iota(jnp.int32, shape, 1) < HD


def extra(base, v, first):
    hi = v.astype(BF).astype(F32)
    mid = (v - hi).astype(BF).astype(F32)
    lane = lax.broadcasted_iota(jnp.int32, base.shape, 1) % HD
    out = jnp.where(lane == first, hi, base)
    out = jnp.where(lane == first + 1, mid, out)
    return jnp.where(lane == first + 2, v - hi - mid, out)


def vspecs(n):
    return [pl.BlockSpec(memory_space=pltpu.VMEM)] * n


def anyspecs(n):
    return [pl.BlockSpec(memory_space=pl.ANY)] * n


SMEM = pl.BlockSpec(memory_space=pltpu.SMEM)
DMA = pltpu.SemaphoreType.DMA


def params(**kw):
    return pltpu.CompilerParams(vmem_limit_bytes=VLIM, **kw)


def cost(flops, moved, trans=0):
    return pl.CostEstimate(flops=int(flops), bytes_accessed=int(moved), transcendentals=int(trans))


class Plan:
    def __init__(self, lens_ref, shard, rows):
        group = lens_ref.shape[1]
        half = group // 2
        self.half, self.shard, self.rows = half, shard, rows
        self.lens = [lens_ref[0, q] for q in range(group)]
        long = jnp.int32(0)
        for q in range(1, group):
            long = jnp.where(self.lens[q] == rows, q, long)
        self.long = long
        self.home = lax.div(long, jnp.int32(half))
        self.stays = shard == self.home
        self.slot = long & 1
        self.first = half * (1 - self.home)
        self.s0, self.s1 = self.size(self.first), self.size(self.first + 1)
        self.moved = self.size(long ^ 1)

    def size(self, q):
        out = self.lens[0]
        for n in range(1, len(self.lens)):
            out = jnp.where(q == n, self.lens[n], out)
        return out

    def away(self):
        return jnp.where(self.stays, 1 - self.slot, 0)

    def bounds(self):
        return jnp.where(self.stays, self.rows, self.s0), jnp.where(self.stays, self.rows, self.s0 + self.s1)

    def where(self, q):
        start = jnp.where(q == self.first, 0, jnp.where(q == self.first + 1, self.s0, self.s0 + self.s1))
        start = jnp.where(q == self.long, 0, start)
        side = jnp.where(q == self.long, self.home, 1 - self.home) ^ self.shard
        return side, start, self.size(q)


def window_pick(total, first, count):
    low = jnp.clip((first >> 7) << 7, 0, total - WINDOW)
    want = first - low + lax.broadcasted_iota(jnp.int32, (count, WINDOW), 0)
    return pl.multiple_of(low, 128), want == lax.broadcasted_iota(jnp.int32, (count, WINDOW), 1)


def moved_pick(start, i, upto):
    want = i * BQ - start + lax.broadcasted_iota(jnp.int32, (BQ, upto), 0)
    return jnp.where(want == lax.broadcasted_iota(jnp.int32, (BQ, upto), 1), 1.0, 0.0).astype(BF)


def lane_and_segment(bounds, first, rows):
    row = first + lax.broadcasted_iota(jnp.int32, (rows, 128), 0)
    seg = (row >= bounds[0]).astype(jnp.int32) + (row >= bounds[1]).astype(jnp.int32)
    return lax.broadcasted_iota(jnp.int32, (rows, 128), 1) % HD, seg


def own_segment(bounds, first, rows):
    lane, seg = lane_and_segment(bounds, first, rows)
    return jnp.where(lane == seg, 1.0, 0.0)


def other_segment(bounds, first, rows):
    lane, seg = lane_and_segment(bounds, first, rows)
    return jnp.where((lane < 3) & (lane != seg), NEG, 0.0)


def gelu_both(v):
    v2 = v * v
    t = jnp.tanh(v * (GELU_A + (GELU_A * GELU_B) * v2))
    half = 0.5 + 0.5 * t
    return v * half, half + (0.5 * v) * (1.0 - t * t) * (GELU_A + (3.0 * GELU_A * GELU_B) * v2)


def place():
    return lax.axis_index("rep"), lax.axis_index("shard")


def greet(partners):
    barrier = pltpu.get_barrier_semaphore()
    for partner in partners:
        pl.semaphore_signal(barrier, inc=1, device_id=partner, device_id_type=MESH)
    pl.semaphore_wait(barrier, len(partners))


def remote(src, dst, ssem, rsem, to):
    return pltpu.make_async_remote_copy(
        src_ref=src, dst_ref=dst, send_sem=ssem, recv_sem=rsem, device_id=to, device_id_type=MESH
    )


def link_of(d):
    return ((d + 2) // 2 if d else 0), (2 if d > 2 and d % 2 else 1)


def timetable(points, chains, ready, busy):
    free, at, step = dict(busy), {}, {c: 0 for c in chains}
    plan, tail = {name: [] for name, _ in points}, []

    def take(c, now, dest):
        dest.append((c, step[c]))
        if step[c] < len(chains[c]):
            link, long, lag = chains[c][step[c]]
            free[link] = max(now, free.get(link, 0.0)) + long
            at[c] = free[link] + lag
        step[c] += 1

    left = lambda: [c for c in chains if c in at and step[c] <= len(chains[c])]
    for name, now in points:
        for c in chains:
            if ready[c] == name:
                at[c] = now
        while True:
            due = [c for c in left() if at[c] <= now]
            if not due:
                break
            take(min(due, key=lambda c: at[c]), now, plan[name])
    now = points[-1][1]
    while left():
        c = min(left(), key=lambda c: at[c])
        now = max(now, at[c])
        take(c, now, tail)
    return plan, tail


def front_body(
    lens_ref, xin_ref, cin_ref, g1_in, b1_in, qb_in, vb_in, ob_in, g2_in, b2_in, pb_in, fb_in, wq_in, wo_in, wf_in, wp_in,
    x_out, joined_out, att_out, ext_out, hid_out, n2_out, act_out, der_out, out_out, cot_out, wq_out, wo_out, wf_out, wp_out, vecs_ref,
    wq_ref, wo_ref, wf_ref, wp_ref, xo_ref, xs_ref, xr_ref, co_ref, cs_ref, cr_ref, x_ref, cot_ref, small_ref, sm_ref,
    jn_ref, ks_ref, vs_ref, att_ref, ext_ref, hid_ref, n2_ref, act_ref, der_ref, acc_ref, obf_ref,
    wsend, wrecv, wload, wsave, xsend, xrecv, csem, ssem, lsem, osem, jsem, asem,
):
    rep, shard = place()
    rows, width = x_ref.shape
    nb = rows // BQ
    npair = width // 128
    nf = act_out.shape[0]
    across = (rep, 1 - shard)
    peers = [(rep ^ (1 << d), shard) for d in range(4)]
    core = rep & 1
    plan = Plan(lens_ref, shard, rows)
    bounds, slot = plan.bounds(), plan.away()

    parts = []
    for src, dst, nrows, ncols in ((wq_in, wq_ref, 1, 3), (wo_in, wo_ref, 1, 1), (wf_in, wf_ref, 1, 2), (wp_in, wp_ref, 2, 1)):
        size, cols = src.shape[0] // nrows, src.shape[1] // ncols
        for n in range(nrows * ncols):
            parts.append((src, dst, n // ncols * size, size, n % ncols * cols, cols, WAYS[len(parts)]))
    nparts = len(parts)
    early = 4

    def chain(n, step):
        src, dst, row, size, col, cols, way = parts[n]
        half, unit = src.shape[0], size >> len(way)
        index = sum(((rep >> d) & 1) << i for i, d in enumerate(way))
        count = 1 if step == 0 else 1 << (step - 1)
        first = row + ((index & ~(count - 1)) * unit if step <= len(way) else 0)
        here = pl.ds(pl.multiple_of(first, 16), count * unit)
        side = pl.ds(pl.multiple_of(col + core * (cols // 2), 128), cols // 2)
        sems = (wsend.at[n, step], wrecv.at[n, step])
        if step == 0:
            into = pl.ds(pl.multiple_of(shard * half + first, 16), unit)
            return remote(src.at[here, side], dst.at[into, side], *sems, across)
        into = pl.ds(pl.multiple_of((1 - shard) * half + first, 16), count * unit)
        return remote(dst.at[into, side], dst.at[into, side], *sems, peers[(way + (0,))[step - 1]])

    def hops(n):
        return len(parts[n][-1]) + 2

    def act(n, step):
        if step:
            chain(n, step - 1).wait_recv()
        if step < hops(n):
            chain(n, step).start()

    def expected(n):
        _src, _dst, _row, size, _col, cols, way = parts[n]
        mb = size * cols * 1e-6
        out = [(0, mb / LINK_RATE / (1 << len(way)), 1.5)]
        for i, d in enumerate(way):
            out.append((link_of(d)[0], mb / LINK_RATE * link_of(d)[1] / (1 << (len(way) - i)), 1.5))
        return out + [("core", mb / CORE_RATE, 1.0)]

    points, now = [], 21.0
    for i in range(nb):
        for name, long in [(("b", i), 2.0)] + [(("h", i, h), 0.5 + 0.55 * i) for h in range(npair)]:
            now += long
            points.append((name, now))
    first_ones = {n: expected(n) for n in range(early)}
    late_ones = {n: expected(n) for n in range(early, nparts)}
    starts = [("start", 3.0)] + [(("sx", i), 5.0 + 1.8 * i) for i in range(nb)] + [(("pk", i), 13.5 + 2.7 * i) for i in range(nb)]
    opening, opened = timetable(starts, first_ones, {n: "start" for n in first_ones}, {})
    busy = {0: 3.0 + sum(c[0][1] for c in first_ones.values()) + 2 * BQ * width * 2e-6 / LINK_RATE}
    agenda, closing = timetable([("start", 20.0)] + points, late_ones, {n: "start" for n in late_ones}, busy)

    whole = [(wq_in, wq_ref, wq_out), (wo_in, wo_ref, wo_out), (wf_in, wf_ref, wf_out), (wp_in, wp_ref, wp_out)]

    def half_rows(src, which):
        return pl.ds(pl.multiple_of(which * src.shape[0], 16), src.shape[0])

    def own_load(n):
        src, dst, _ = whole[n]
        return pltpu.make_async_copy(src, dst.at[half_rows(src, shard), :], wload.at[n])

    def other_save(n):
        src, dst, save = whole[n]
        return pltpu.make_async_copy(dst.at[half_rows(src, 1 - shard), :], save, wsave.at[n])

    x_load = pltpu.make_async_copy(xin_ref, xo_ref, lsem.at[0])
    c_load = pltpu.make_async_copy(cin_ref, co_ref, lsem.at[1])
    x_load.start()
    for n in range(4):
        own_load(n).start()
    c_load.start()
    hw = width // 2
    for n, ref in enumerate((g1_in, b1_in, qb_in, vb_in, ob_in, g2_in, b2_in, pb_in)):
        small_ref[n, :] = ref[...].astype(F32)
    for n in range(nf):
        small_ref[8 + n, :] = fb_in[n * hw : (n + 1) * hw].astype(F32)
    greet([across] + peers)
    small = remote(small_ref, sm_ref.at[shard], ssem.at[0], ssem.at[1], across)
    small.start()
    for n, step in opening["start"]:
        act(n, step)

    tail = plan.s0 + plan.s1
    theirs = jnp.where(plan.stays, rows, tail)
    split = jnp.where(plan.stays, rows, plan.s0)
    whole_one = jnp.where(plan.stays & (plan.slot == 1), 1, 0)

    def pack_sent(dst_ref, src_ref, i, upto):
        total = None
        for k in range(2):
            part = dot(moved_pick(jnp.where(slot == k, tail, rows), i, upto), src_ref[k, 0:upto, :])
            total = part if total is None else total + part
        dst_ref[rows_of(i, BQ), :] = total.astype(BF)

    def pack_own(dst_ref, src_ref, i):
        r = rows_of(i, BQ)
        row = i * BQ + lax.broadcasted_iota(jnp.int32, (BQ, width), 0)
        base = jnp.where(whole_one == 1, src_ref[1, r, :].astype(F32), src_ref[0, r, :].astype(F32))
        dst_ref[r, :] = jnp.where(row >= split, dot(moved_pick(split, i, rows), src_ref[1]), base).astype(BF)

    def merged(own_ref, got_ref, i):
        r = rows_of(i, BQ)
        row = i * BQ + lax.broadcasted_iota(jnp.int32, (BQ, width), 0)
        return jnp.where(row >= theirs, got_ref[r, :].astype(F32), own_ref[r, :].astype(F32)).astype(BF)

    def x_chunk(i):
        r = rows_of(i, BQ)
        return remote(xs_ref.at[r, :], xr_ref.at[r, :], xsend.at[i], xrecv.at[i], across)

    c_copy = remote(cs_ref, cr_ref, csem.at[0], csem.at[1], across)
    x_load.wait()

    def opened_at(i, name):
        for ii in range(nb):
            if opening[(name, ii)]:

                @pl.when(i == ii)
                def _():
                    for n, step in opening[(name, ii)]:
                        act(n, step)

    pack_sent(xs_ref, xo_ref, 0, BQ)
    x_chunk(0).start()
    for n, step in opening[("sx", 0)]:
        act(n, step)

    @pl.loop(1, nb)
    def _(i):
        pack_sent(xs_ref, xo_ref, i, rows)

        @pl.when(i == 2)
        def _():
            for n, step in agenda["start"]:
                act(n, step)

        x_chunk(i).start()
        opened_at(i, "sx")

    sm_ref[shard] = small_ref[...]
    small.wait()
    for n in range(8):
        for which in range(2):
            vecs_ref[n : n + 1, which * hw : (which + 1) * hw] = sm_ref[which, n : n + 1, :]
    for n in range(nf):
        for part in range(2):
            which, row = (2 * n + part) // nf, 8 + (2 * n + part) % nf
            vecs_ref[8 + n : 9 + n, part * hw : (part + 1) * hw] = sm_ref[which, row : row + 1, :]
    vecs_ref[8 + nf : 16, :] = jnp.zeros((8 - nf, width), F32)
    vecs_ref[JB : JB + 1, :] = vecs_ref[QB : QB + 1, :]
    vecs_ref[JB + 2 : JB + 3, :] = vecs_ref[VB : VB + 1, :]
    c_load.wait()

    @pl.loop(0, nb)
    def _(i):
        pack_own(x_ref, xo_ref, i)
        pack_sent(cs_ref, co_ref, i, rows)
        opened_at(i, "pk")

    c_copy.start()
    for n, step in opened[:-early]:
        act(n, step)

    @pl.loop(0, nb)
    def _(i):
        pack_own(cot_ref, co_ref, i)

    for n, step in opened[-early:]:
        act(n, step)
    own_load(0).wait()
    own_load(1).wait()
    other_save(0).start()
    other_save(1).start()
    def at_point(name):
        for n, step in agenda[name]:
            act(n, step)

    gain, shift = vecs_ref[G1 : G1 + 1, :], vecs_ref[B1 : B1 + 1, :]
    lq = lane_half((BQ, 128))
    tri = lax.broadcasted_iota(jnp.int32, (BQ, BQ), 1) <= lax.broadcasted_iota(jnp.int32, (BQ, BQ), 0)
    def joined_save(i, b):
        r = pl.ds(i * BQ, BQ)
        return pltpu.make_async_copy(jn_ref.at[r, pl.ds(b * width, width)], joined_out.at[b, r, :], jsem.at[i, b])

    for i in range(nb):
        x_chunk(i).wait_recv()
        n = (i + 1) * BQ
        r = slice(i * BQ, n)
        xb = merged(x_ref, xr_ref, i)
        x_ref[r, :] = xb
        unit, _inv = norm_stats(xb.astype(F32))
        n1 = (unit * gain + shift).astype(BF)

        @pl.loop(0, 3)
        def _(b):
            c = span(b * width, width)
            jn_ref[r, c] = (dot(n1, wq_ref[:, c]) + vecs_ref[pl.ds(JB + b, 1), :]).astype(BF)

        for b in range(3):
            joined_save(i, b).start()
        at_point(("b", i))
        ohf = own_segment(bounds, i * BQ, BQ)
        oh = ohf.astype(BF)
        neg = other_segment(bounds, i * BQ, BQ).astype(BF)

        @pl.loop(0, npair)
        def _(h):
            k2 = jn_ref[r, pl.ds(pl.multiple_of(width + h * 128, 128), 128)]
            v2 = jn_ref[r, pl.ds(pl.multiple_of(2 * width + h * 128, 128), 128)]
            one = jnp.ones_like(v2)
            ks_ref[h, 0, r, :] = jnp.where(lq, k2, neg)
            ks_ref[h, 1, r, :] = jnp.where(lq, neg, k2)
            vs_ref[h, 0, r, :] = jnp.where(lq, v2, one)
            vs_ref[h, 1, r, :] = jnp.where(lq, one, v2)

        @pl.loop(0, npair)
        def _(h):
            cq = pl.ds(pl.multiple_of(h * 128, 128), 128)
            q2 = jn_ref[r, cq]
            qs = [jnp.where(lq, q2, oh), jnp.where(lq, oh, q2)]
            outs, exts = [], []
            for e in range(2):
                sd = jnp.where(tri, dot_nt(qs[e], ks_ref[h, e, r, :]), NEG)
                peak = jnp.max(sd, axis=1, keepdims=True)
                if i:
                    so = dot_nt(qs[e], ks_ref[h, e, 0 : n - BQ, :])
                    peak = jnp.maximum(peak, jnp.max(so, axis=1, keepdims=True))
                    po = jnp.exp2((so - peak) * EXPC).astype(BF)
                pd = jnp.exp2((sd - peak) * EXPC).astype(BF)
                acc = dot(pd, vs_ref[h, e, r, :])
                if i:
                    acc = acc + dot(po, vs_ref[h, e, 0 : n - BQ, :])
                outs.append(acc)
                tot = acc[:, HD : HD + 1] if e == 0 else acc[:, 0:1]
                exts.append(extra(ohf, -(peak + jnp.log(tot) * (1.0 / SCALE)), 3))
            num = jnp.where(lq, outs[0], outs[1])
            den = pltpu.roll(jnp.where(lq, outs[1], outs[0]), HD, 1)
            att_ref[r, cq] = (num / den).astype(BF)
            ext_ref[r, cq] = jnp.where(lq, exts[1], exts[0]).astype(BF)
            for hh in range(npair):
                if agenda[("h", i, hh)]:

                    @pl.when(h == hh)
                    def _():
                        at_point(("h", i, hh))

    x_save = pltpu.make_async_copy(x_ref, x_out, osem.at[0])
    att_save = pltpu.make_async_copy(att_ref, att_out, osem.at[1])
    ext_save = pltpu.make_async_copy(ext_ref, ext_out, osem.at[2])
    for copy in (x_save, att_save, ext_save):
        copy.start()

    gain2, shift2 = vecs_ref[G2 : G2 + 1, :], vecs_ref[B2 : B2 + 1, :]

    @pl.loop(0, nb)
    def _(i):
        r = rows_of(i, BQ)
        hid = x_ref[r, :].astype(F32) + (dot(att_ref[r, :], wo_ref[...]) + vecs_ref[OB : OB + 1, :])
        hid_ref[r, :] = hid
        unit, _inv = norm_stats(hid)
        n2_ref[r, :] = (unit * gain2 + shift2).astype(BF)
        acc_ref[r, :] = hid + vecs_ref[PB : PB + 1, :]

    hid_save = pltpu.make_async_copy(hid_ref, hid_out, osem.at[3])
    n2_save = pltpu.make_async_copy(n2_ref, n2_out, osem.at[4])
    hid_save.start()
    n2_save.start()

    def gelu_save(n):
        return (
            pltpu.make_async_copy(act_ref.at[n & 1], act_out.at[n], asem.at[0, n]),
            pltpu.make_async_copy(der_ref.at[n & 1], der_out.at[n], asem.at[1, n]),
        )

    for n, step in closing:
        act(n, step)
    own_load(2).wait()
    own_load(3).wait()
    other_save(2).start()
    other_save(3).start()

    @pl.loop(0, nf)
    def _(n):
        @pl.when(n >= 2)
        def _():
            for copy in gelu_save(n - 2):
                copy.wait()

        c = span(n * width, width)

        @pl.loop(0, nb)
        def _(i):
            r = rows_of(i, BQ)
            act, der = gelu_both(dot(n2_ref[r, :], wf_ref[:, c]) + vecs_ref[pl.ds(FB + n, 1), :])
            act = act.astype(BF)
            act_ref[n & 1, r, :] = act
            der_ref[n & 1, r, :] = der.astype(BF)
            acc_ref[r, :] += dot(act, wp_ref[c, :])

        for copy in gelu_save(n):
            copy.start()

    @pl.loop(0, nb)
    def _(i):
        r = rows_of(i, BQ)
        obf_ref[r, :] = acc_ref[r, :].astype(BF)

    out_save = pltpu.make_async_copy(obf_ref, out_out, osem.at[5])
    out_save.start()

    c_copy.wait_recv()

    @pl.loop(0, nb)
    def _(i):
        cot_ref[rows_of(i, BQ), :] = merged(cot_ref, cr_ref, i)

    cot_save = pltpu.make_async_copy(cot_ref, cot_out, osem.at[6])
    cot_save.start()
    for n in range(nparts):
        for step in range(hops(n)):
            chain(n, step).wait_send()
    for i in range(nb):
        x_chunk(i).wait_send()
        for b in range(3):
            joined_save(i, b).wait()
    c_copy.wait_send()
    for n in range(4):
        other_save(n).wait()
    for n in range(max(0, nf - 2), nf):
        for copy in gelu_save(n):
            copy.wait()
    for copy in (x_save, att_save, ext_save, hid_save, n2_save, out_save, cot_save):
        copy.wait()


WAYS = [(2, 1), (1, 2), (2, 1), (1, 2), (3, 2, 1), (3, 1, 2), (3, 2, 1), (3, 1, 2)]


def front(lens, xin, cin, small, wq, wo, wf, wp):
    slots, rows, width = xin.shape
    ff = wf.shape[1]
    nf = ff // width
    nb = rows // BQ
    s = jax.ShapeDtypeStruct
    v = pltpu.VMEM
    act = s((rows, width), BF)
    nparts = len(WAYS)
    return pl.pallas_call(
        front_body,
        name="front",
        out_shape=(
            act, s((3, rows, width), BF), act, act, s((rows, width), F32), act, s((nf, rows, width), BF), s((nf, rows, width), BF),
            act, act, s(wq.shape, BF), s(wo.shape, BF), s(wf.shape, BF), s(wp.shape, BF), s((16, width), F32),
        ),
        in_specs=[SMEM] + anyspecs(2) + vspecs(9) + anyspecs(4),
        out_specs=tuple(anyspecs(14) + vspecs(1)),
        scratch_shapes=[
            v((width, 3 * width), BF), v((width, width), BF), v((width, ff), BF), v((ff, width), BF),
            v((slots, rows, width), BF), v((rows, width), BF), v((rows, width), BF),
            v((slots, rows, width), BF), v((rows, width), BF), v((rows, width), BF),
            v((rows, width), BF), v((rows, width), BF), v((16, width // 2), F32), v((2, 16, width // 2), F32),
            v((rows, 3 * width), BF), v((width // 128, 2, rows, 128), BF), v((width // 128, 2, rows, 128), BF),
            v((rows, width), BF), v((rows, width), BF), v((rows, width), F32), v((rows, width), BF),
            v((2, rows, width), BF), v((2, rows, width), BF), v((rows, width), F32), v((rows, width), BF),
            DMA((nparts, 5)), DMA((nparts, 5)), DMA((4,)), DMA((4,)), DMA((nb,)), DMA((nb,)), DMA((2,)), DMA((2,)), DMA((2,)),
            DMA((7,)), DMA((nb, 3)), DMA((2, nf)),
        ],
        compiler_params=params(collective_id=0, has_side_effects=True),
        cost_estimate=cost(40e9, 60e6, 12e6),
    )(lens, xin, cin, *small, wq, wo, wf, wp)


def back_body(
    bits, lens_ref, vecs_ref, x_in, joined_in, att_in, ext_in, hid_in, n2_in, act_in, der_in, out_in, cot_in,
    wq_own, wo_own, wf_own, wp_own, wq_oth, wo_oth, wf_oth, wp_oth,
    res_out, dx_out, dxr_out, outr_out, sums_ref,
    wf_ref, wp_ref, wo_ref, wq_ref, cot_ref, n2_ref, act_ref, der_ref, gpre_ref, acc_ref, hid_ref, att_ref,
    gm_ref, r0_ref, rb_ref, res_ref, sm_ref, smb_ref, smr_ref,
    wsem, lsem, asem, hsem, ssem, rsem, msem, mrem, osem, dsem, drem, vsem, fsem,
):
    rep, shard = place()
    core = rep & 1
    rows, width = cot_ref.shape
    hw = width // 2
    nb = rows // BQ
    nf = act_in.shape[0]
    npair = width // 128
    m = bits - 1
    sibling, across = (rep ^ 1, shard), (rep, 1 - shard)
    peers = {0: across}
    for t in range(1, bits):
        peers[t] = (rep ^ (1 << t), shard)
    plan = Plan(lens_ref, shard, rows)
    bounds = plan.bounds()

    def weight_loads(own, oth, dst, into):
        half = own.shape[0]
        for n, (src, which) in enumerate(((own, shard), (oth, 1 - shard))):
            yield n, src, dst.at[pl.ds(pl.multiple_of(into + which * half, 16), half), :]

    def fc_loads(j):
        for n, src, dst in weight_loads(wf_own, wf_oth, wf_ref, j * width):
            for part in range(2):
                here = span((part * nf + j) * hw, hw)
                yield pltpu.make_async_copy(src.at[:, here], dst.at[:, pl.ds(part * hw, hw)], wsem.at[0, n, part, j])

    def proj_loads(j):
        for n, (src, which) in enumerate(((wp_own, shard), (wp_oth, 1 - shard))):
            into = pl.ds(pl.multiple_of(j * width + which * hw, 16), hw)
            yield pltpu.make_async_copy(src.at[span(j * hw, hw), :], wp_ref.at[into, :], wsem.at[1, n, 0, j])

    def gelu_loads(k, j):
        src, dst = ((act_in, act_ref), (der_in, der_ref))[k]
        for part in range(2):
            block = part * (nf // 2) + (j >> 1)
            here = span((j & 1) * hw, hw)
            yield pltpu.make_async_copy(src.at[block, :, here], dst.at[j & 1, :, pl.ds(part * hw, hw)], asem.at[k, part, j])

    def plain(n, src, dst):
        return pltpu.make_async_copy(src, dst, lsem.at[n])

    cot_load, n2_load, att_load = plain(0, cot_in, cot_ref), plain(1, n2_in, n2_ref), plain(2, att_in, att_ref)
    wo_loads = [pltpu.make_async_copy(s_, d_, wsem.at[2, n, 0, 0]) for n, s_, d_ in weight_loads(wo_own, wo_oth, wo_ref, 0)]
    wq_loads = [pltpu.make_async_copy(s_, d_, wsem.at[2, n, 0, 1]) for n, s_, d_ in weight_loads(wq_own, wq_oth, wq_ref, 0)]
    x_load, ext_load = plain(3, x_in, act_ref.at[0]), plain(4, ext_in, der_ref.at[0])
    joined_loads = [plain(5 + b, joined_in.at[b], wf_ref.at[pl.ds(b * rows, rows), :]) for b in range(3)]

    def hid_load(i):
        return pltpu.make_async_copy(hid_in.at[span(i * BQ, BQ), :], hid_ref.at[i & 1], hsem.at[i])

    cot_load.start()
    for j in range(2):
        for copy in list(gelu_loads(0, j)) + list(proj_loads(j)) + list(gelu_loads(1, j)) + list(fc_loads(j)):
            copy.start()
        if j == 0:
            n2_load.start()
    greet([sibling, across] + [peers[t] for t in range(1, bits)])

    per = gm_ref.shape[3] // PIECE
    pieces = pieces_of(per, hw)
    count = len(pieces)
    last = 3 + 2 * m
    orders = [PATHS[k] + tuple(range(4, bits)) for k in range(count)]

    def source(k, away):
        n, c = pieces[k]
        a, at = n // per, pl.ds((n % per) * PIECE, PIECE)
        return gm_ref.at[away, a, :, at, c] if a < 2 else gm_ref.at[1, away, :, at, c]

    def place_of(ref, k):
        n, c = pieces[k]
        return ref.at[n, :, :, c]

    def result_of(ref, k):
        n, c = pieces[k]
        return ref.at[n, :, c]

    def held(k, i):
        half, first, size = None, 0, PIECE
        for d in orders[k][:i]:
            if d == 0:
                half = shard
            else:
                size //= 2
                first = first + ((rep >> d) & 1) * size
        return half, first, size

    def at_rows(first, size):
        return pl.ds(pl.multiple_of(first, 16), size)

    def landing(k, i):
        d = orders[k][i]
        half, _first, size = held(k, i + 1)
        before = sum(PIECE >> (n + 1) for n in range(len([e for e in orders[k][:i] if e])))
        if d == 0:
            return place_of(rb_ref, k).at[0, pl.ds(before, size), :]
        at = pl.ds(before, size)
        return place_of(rb_ref, k).at[:, at, :] if half is None else place_of(rb_ref, k).at[1, at, :]

    def leaving(k, i):
        d = orders[k][i]
        half, first, size = held(k, i)
        own = source(k, 0)
        if d == 0:
            return own.at[1 - shard, at_rows(first, size), :]
        size //= 2
        at = at_rows(first + (1 - ((rep >> d) & 1)) * size, size)
        return own.at[:, at, :] if half is None else own.at[half, at, :]

    def copy(k, step):
        sems = (ssem.at[step, k], rsem.at[step, k])
        if step == 0:
            return remote(source(k, 1), place_of(r0_ref, k), *sems, sibling)
        if step <= m + 1:
            return remote(leaving(k, step - 1), landing(k, step - 1), *sems, peers[orders[k][step - 1]])
        if step <= 2 * m + 1:
            back = [d for d in orders[k] if d]
            t = m - (step - m - 2)
            size = PIECE >> t
            first = 0
            for n in range(t):
                first = first + ((rep >> back[n]) & 1) * (PIECE >> (n + 1))
            here = result_of(res_ref, k).at[at_rows(first, size), :]
            return remote(here, here, *sems, peers[back[t - 1]])
        return remote(result_of(res_ref, k), result_of(res_out.at[core], k), *sems, sibling)

    def keep(k):
        return pltpu.make_async_copy(result_of(res_ref, k), result_of(res_out.at[core], k), fsem.at[k])

    def add(dst, first, other, base, size, out=None):
        chunk = min(size, 64)

        @pl.loop(0, size // chunk)
        def _(i):
            at = pl.ds(pl.multiple_of(first + i * chunk, 16), chunk)
            total = dst[at, :].astype(F32) + other[pl.ds(pl.multiple_of(base + i * chunk, 16), chunk), :].astype(F32)
            (dst if out is None else out)[at, :] = total.astype(BF)

    def act_step(k, step):
        if step:
            copy(k, step - 1).wait_recv()
        own = source(k, 0)
        if step == 1:
            for h in range(2):
                add(own.at[h], 0, place_of(r0_ref, k).at[h], 0, PIECE)
        elif 2 <= step <= m + 2:
            i = step - 2
            half, first, size = held(k, i + 1)
            land = landing(k, i)
            if half is None:
                for h in range(2):
                    add(own.at[h], first, land.at[h], 0, size)
            else:
                add(own.at[half], first, land, 0, size, result_of(res_ref, k) if i == m else None)
        if step < last:
            copy(k, step).start()
        if step == last - 1:
            keep(k).start()

    def small_copy(step):
        src = sm_ref if step == 0 else smb_ref.at[step - 1]
        return remote(src, smr_ref.at[step], msem.at[step], mrem.at[step], small_peers[step])

    def small_step(step):
        if step:
            small_copy(step - 1).wait_recv()
            before = sm_ref[...] if step == 1 else smb_ref[step - 2]
            total = before + smr_ref[step - 1]
            if step == 2 + m:
                sums_ref[...] = total
            else:
                smb_ref[step - 1] = total
        if step < 2 + m:
            small_copy(step).start()

    def dx_chunk(i):
        at = pl.ds(i * BQ, BQ)
        return remote(dxb_ref.at[at, :], dxr_out.at[at, :], dsem.at[i], drem.at[i], across)

    def dx_step(i):
        if i:
            dx_chunk(i - 1).wait_send()
        if i < nb:
            dx_chunk(i).start()

    def out_chunk(i):
        at = pl.ds(i * BQ, BQ)
        return remote(out_in.at[at, :], outr_out.at[at, :], osem.at[0, i], osem.at[1, i], across)

    def out_step(i):
        if i:
            out_chunk(i - 1).wait_send()
        if i < nb:
            out_chunk(i).start()

    def act(c, step):
        if c == "out":
            out_step(step)
        elif c == "small":
            small_step(step)
        elif c == "dx":
            dx_step(step)
        else:
            act_step(c, step)

    small_peers = [sibling, across] + [peers[t] for t in range(1, bits)]
    xb_ref, eb_ref, n1_ref, dxb_ref = act_ref.at[0], der_ref.at[0], der_ref.at[1], act_ref.at[1]

    points, now = [], 5.0
    for name, long in (
        [(("gp", j), 1.9) for j in range(nf)]
        + [(("ff", j, n), (4.1, 2.2)[n]) for j in range(nf) for n in range(2)]
        + [(("hid", i), 1.6) for i in range(nb)]
        + [("go", 2.0)]
        + [p for t in range(THIRDS) for p in [(("at", t, p, i), 0.72 * (i + 1)) for p in range(npair // THIRDS) for i in range(nb)] + [(("gw", t), 2.0)]]
        + [(("dx", i), 2.0) for i in range(nb)]
    ):
        now += long
        points.append((name, now))
    chains, ready = {}, {}
    for k, (n, c) in enumerate(pieces):
        half_mb = 2 * PIECE * (c.stop - c.start) / 1e6
        steps, size = [("core", 2 * half_mb / CORE_RATE, 1.0)], 2 * half_mb
        for d in orders[k]:
            size /= 2
            steps.append((link_of(d)[0], size / LINK_RATE * link_of(d)[1], 1.5))
        size = half_mb / (1 << m)
        for d in reversed([d for d in orders[k] if d]):
            steps.append((link_of(d)[0], size / LINK_RATE * link_of(d)[1], 1.5))
            size *= 2
        chains[k] = steps + [("core", half_mb / CORE_RATE, 1.0)]
        ready[k] = ("ff", 1 + n, 1) if n < per else ("gp", 1 + n - per) if n < 2 * per else ("gw", n - 2 * per)
    small_us = 24 * width * 4e-6 / LINK_RATE
    chains["small"] = [("core", 0.5, 1.0), (0, small_us, 1.5)] + [(link_of(d)[0], small_us * link_of(d)[1], 1.5) for d in range(1, bits)]
    chains["dx"] = [(0, BQ * width * 2e-6 / LINK_RATE, 0.0)] * nb
    chains["out"] = chains["dx"]
    ready["small"], ready["dx"], ready["out"] = ("dx", nb - 1), ("dx", 0), OUT_AT
    agenda, tail = timetable(points, chains, ready, {})

    def at_point(name):
        for c, step in agenda[name]:
            act(c, step)

    gbase = 16
    sm_ref[...] = jnp.zeros_like(sm_ref)

    @pl.loop(0, nb)
    def _(i):
        acc_ref[rows_of(i, BQ), :] = jnp.zeros((BQ, width), F32)

    def at_step(j, name):
        for jj in range(nf):
            if agenda[name(jj)]:

                @pl.when(j == jj)
                def _():
                    at_point(name(jj))

    cot_load.wait()

    @pl.loop(0, nf)
    def _(j):
        for c in gelu_loads(0, j):
            c.wait()
        into = span(j * hw, hw)
        for h in range(2):
            gp = dot_tn(act_ref[j & 1, :, h * hw : (h + 1) * hw], cot_ref[...]).astype(BF)
            for c in range(2):
                gm_ref[c ^ core, 1, h, into, :] = gp[:, c * hw : (c + 1) * hw]

        @pl.when(j < nf - 2)
        def _():
            for c in gelu_loads(0, j + 2):
                c.start()

        at_step(j, lambda jj: ("gp", jj))

    n2_load.wait()

    @pl.loop(0, nf)
    def _(j):
        for c in list(proj_loads(j)) + list(gelu_loads(1, j)) + list(fc_loads(j)):
            c.wait()

        @pl.when(j < nf - 2)
        def _():
            for c in list(proj_loads(j + 2)) + list(fc_loads(j + 2)):
                c.start()

        here, into, bias = span(j * width, width), span(j * hw, hw), pl.ds(gbase + j, 1)

        @pl.loop(0, nb)
        def _(i):
            r = rows_of(i, BQ)
            gact = dot_nt(cot_ref[r, :], wp_ref[here, :])
            gpre = (gact * der_ref[j & 1, r, :].astype(F32)).astype(BF)
            gpre_ref[r, :] = gpre
            sm_ref[bias, :] += jnp.sum(gpre.astype(F32), axis=0, keepdims=True)
            acc_ref[r, :] += dot_nt(gpre, wf_ref[here, :])

        at_step(j, lambda jj: ("ff", jj, 0))
        for h in range(2):
            gf = dot_tn(n2_ref[:, h * hw : (h + 1) * hw], gpre_ref[...]).astype(BF)
            for c in range(2):
                gm_ref[c ^ core, 0, h, into, :] = gf[:, c * hw : (c + 1) * hw]

        @pl.when(j < nf - 2)
        def _():
            for c in gelu_loads(1, j + 2):
                c.start()

        @pl.when(j == nf - 2)
        def _():
            for c in [x_load, ext_load, att_load] + wo_loads + wq_loads:
                c.start()
            hid_load(0).start()
            hid_load(1).start()

        at_step(j, lambda jj: ("ff", jj, 1))

    for c in joined_loads:
        c.start()
    for c in [att_load] + wo_loads:
        c.wait()
    gain2 = vecs_ref[G2 : G2 + 1, :]
    gatt_ref = cot_ref

    def at_block(i, name):
        for ii in range(nb):
            if agenda[(name, ii)]:

                @pl.when(i == ii)
                def _():
                    at_point((name, ii))

    @pl.loop(0, nb)
    def _(i):
        r = rows_of(i, BQ)
        hid_load(i).wait()
        unit, inv = norm_stats(hid_ref[i & 1])
        gn2 = acc_ref[r, :]
        gy = cot_ref[r, :].astype(F32)
        ghid = gy + norm_back(gn2, unit, inv, gain2)

        @pl.when(i < nb - 2)
        def _():
            hid_load(i + 2).start()

        acc_ref[r, :] = ghid
        low = ghid.astype(BF)
        gpre_ref[r, :] = low
        gatt_ref[r, :] = dot_nt(low, wo_ref[...]).astype(BF)
        sm_ref[0:1, :] += jnp.sum(gn2 * unit, axis=0, keepdims=True)
        sm_ref[1:2, :] += jnp.sum(gn2, axis=0, keepdims=True)
        sm_ref[2:3, :] += jnp.sum(gy, axis=0, keepdims=True)
        sm_ref[3:4, :] += jnp.sum(low.astype(F32), axis=0, keepdims=True)
        at_block(i, "hid")

    x_load.wait()
    gain1, shift1 = vecs_ref[G1 : G1 + 1, :], vecs_ref[B1 : B1 + 1, :]

    @pl.loop(0, nb)
    def _(i):
        r = rows_of(i, BQ)
        unit, _inv = norm_stats(xb_ref[r, :].astype(F32))
        n1_ref[r, :] = (unit * gain1 + shift1).astype(BF)

    aways = [k for k, (n, _) in enumerate(pieces) if n < 2 * per]
    for k in aways:
        copy(k, 0).wait_send()
    for h in range(2):
        go = dot_tn(att_ref[:, h * hw : (h + 1) * hw], gpre_ref[...]).astype(BF)
        for c in range(2):
            gm_ref[1, c ^ core, h, 0:hw, :] = go[:, c * hw : (c + 1) * hw]
    at_point("go")
    for c in joined_loads + [ext_load]:
        c.wait()

    lq = lane_half((BQ, 128))
    tri = lax.broadcasted_iota(jnp.int32, (BQ, BQ), 0) <= lax.broadcasted_iota(jnp.int32, (BQ, BQ), 1)
    left = lane_half((rows, 128))
    ones = lax.broadcasted_iota(jnp.int32, (rows, 128), 1) % HD
    ones = (ones >= 3) & (ones < 6)
    tcols = width // THIRDS
    here_at = lambda t, p, i: agenda[("at", t, p, i)]

    def head_pair(t, p):
        h = t * (npair // THIRDS) + p
        col = pl.ds(pl.multiple_of(h * 128, 128), 128)
        k2 = wf_ref[rows : 2 * rows, col]
        v2 = wf_ref[2 * rows : 3 * rows, col]
        zero = jnp.zeros_like(k2)
        kx = jnp.where(ones, 1.0, other_segment(bounds, 0, rows)).astype(BF)
        vx = jnp.where(ones, 1.0, 0.0).astype(BF)
        ks = [jnp.where(left, k2, kx), jnp.where(left, kx, k2)]
        vs = [jnp.where(left, v2, vx), jnp.where(left, vx, v2)]
        km = [jnp.where(left, k2, zero), jnp.where(left, zero, k2)]
        hid_ref[...] = jnp.zeros_like(hid_ref)
        for i in range(nb):
            r = slice(i * BQ, (i + 1) * BQ)
            q2 = wf_ref[r, col]
            g2 = gatt_ref[r, col]
            ext = eb_ref[r, col]
            zq = jnp.zeros_like(q2)
            prod = g2.astype(F32) * att_ref[r, col].astype(F32)
            d0 = jnp.sum(jnp.where(lq, prod, 0.0), axis=1, keepdims=True)
            d1 = jnp.sum(jnp.where(lq, 0.0, prod), axis=1, keepdims=True)
            zf = jnp.zeros((BQ, 128), F32)
            qs = [jnp.where(lq, q2, ext), jnp.where(lq, ext, q2)]
            gs = [jnp.where(lq, g2, extra(zf, -d0, 3).astype(BF)), jnp.where(lq, extra(zf, -d1, 3).astype(BF), g2)]
            qm = [jnp.where(lq, q2, zq), jnp.where(lq, zq, q2)]
            gm = [jnp.where(lq, g2, zq), jnp.where(lq, zq, g2)]
            dq = None
            for u in range(i + 1):
                b = slice(u * BQ, (u + 1) * BQ)
                dk = dv = None
                for e in range(2):
                    st = dot_nt(ks[e][b], qs[e])
                    if u == i:
                        st = jnp.where(tri, st, NEG)
                    pt = jnp.exp2(st * EXPC)
                    dst = (pt * dot_nt(vs[e][b], gs[e])).astype(BF)
                    one, two, three = dot(pt.astype(BF), gm[e]), dot(dst, qm[e]), dot_tn(dst, km[e][b])
                    dv = one if dv is None else dv + one
                    dk = two if dk is None else dk + two
                    dq = three if dq is None else dq + three
                hid_ref[1, :, u * 128 : (u + 1) * 128] += dv
                hid_ref[0, :, u * 128 : (u + 1) * 128] += dk
            wp_ref[r, col] = (dq * SCALE).astype(BF)
            for tt in range(THIRDS):
                for pp in range(npair // THIRDS):
                    if here_at(tt, pp, i):

                        @pl.when((t == tt) & (p == pp))
                        def _():
                            for c, step in here_at(tt, pp, i):
                                act(c, step)

        for u in range(nb):
            wp_ref[rows + u * BQ : rows + (u + 1) * BQ, col] = (hid_ref[0, :, u * 128 : (u + 1) * 128] * SCALE).astype(BF)
            wp_ref[2 * rows + u * BQ : 2 * rows + (u + 1) * BQ, col] = hid_ref[1, :, u * 128 : (u + 1) * 128].astype(BF)

    @pl.loop(0, THIRDS)
    def _(t):
        @pl.loop(0, npair // THIRDS)
        def _(p):
            head_pair(t, p)

        cols = pl.ds(pl.multiple_of(t * tcols, 128), tcols)
        into = pl.ds(pl.multiple_of(hw + t * hw, 128), hw)
        cut = hw - tcols
        for h in range(2):
            n1h = n1_ref[:, h * hw : (h + 1) * hw]
            gq, gk, gv = [dot_tn(n1h, wp_ref[b * rows : (b + 1) * rows, cols]).astype(BF) for b in range(3)]
            gm_ref[1, core, h, into, 0:tcols] = gq
            gm_ref[1, core, h, into, tcols:hw] = gk[:, 0:cut]
            gm_ref[1, 1 - core, h, into, 0:cut] = gk[:, cut:tcols]
            gm_ref[1, 1 - core, h, into, cut:hw] = gv
        for b in (0, 2):
            sm_ref[8 + b : 9 + b, cols] = jnp.sum(wp_ref[b * rows : (b + 1) * rows, cols].astype(F32), axis=0, keepdims=True)
        for tt in range(THIRDS):
            if agenda[("gw", tt)]:

                @pl.when(t == tt)
                def _():
                    at_point(("gw", tt))

    for c in wq_loads:
        c.wait()

    @pl.loop(0, nb)
    def _(i):
        r = rows_of(i, BQ)
        gn1 = dot_nt(wp_ref[r, :], wq_ref[:, 0:width])
        for b in (1, 2):
            gn1 = gn1 + dot_nt(wp_ref[span(b * rows + i * BQ, BQ), :], wq_ref[:, b * width : (b + 1) * width])
        unit, inv = norm_stats(xb_ref[r, :].astype(F32))
        dxb_ref[r, :] = (acc_ref[r, :] + norm_back(gn1, unit, inv, gain1)).astype(BF)
        sm_ref[11:12, :] += jnp.sum(gn1 * unit, axis=0, keepdims=True)
        sm_ref[12:13, :] += jnp.sum(gn1, axis=0, keepdims=True)
        at_block(i, "dx")

    dx_save = plain(8, dxb_ref, dx_out)
    dx_save.start()

    for c, step in tail:
        act(c, step)
    for k in range(count):
        for step in range(last):
            if step or k not in aways:
                copy(k, step).wait_send()
        keep(k).wait()
    for step in range(2 + m):
        small_copy(step).wait_send()
    for i in range(nb):
        out_chunk(i).wait_recv()
        dx_chunk(i).wait_recv()
    dx_save.wait()


THIRDS = 3
CORE_RATE, LINK_RATE = 0.15, 0.045
OUT_AT = ("gp", 0)
PATHS = [(2, 1, 0, 3), (1, 0, 3, 2), (1, 0, 2, 3), (1, 2, 0, 3), (0, 1, 2, 3), (1, 2, 0, 3), (1, 0, 2, 3), (0, 1, 2, 3), (2, 1, 0, 3), (1, 2, 3, 0), (0, 1, 2, 3)]


def pieces_of(per, columns):
    out = [(n, slice(0, columns)) for n in range(3 * per - 1)]
    return out + [(3 * per - 1, slice(c, c + 128)) for c in range(0, columns, 128)]


def back(bits, lens, vecs, saved, own, oth):
    x, joined, att, ext, hid, n2, act, der, out, cot = saved
    rows, width = x.shape
    nf = act.shape[0]
    nb = rows // BQ
    hw = width // 2
    m = bits - 1
    per = nf * hw // PIECE
    wholes, count = 3 * per, len(pieces_of(per, hw))
    s = jax.ShapeDtypeStruct
    v = pltpu.VMEM
    sums = (24, width)
    return pl.pallas_call(
        functools.partial(back_body, bits),
        name="back",
        out_shape=(s((2, wholes, PIECE, hw), BF), s((rows, width), BF), s((rows, width), BF), s((rows, width), BF), s(sums, F32)),
        in_specs=[SMEM] + vspecs(1) + anyspecs(18),
        out_specs=tuple(anyspecs(4) + vspecs(1)),
        scratch_shapes=[
            v((nf * width, width), BF), v((nf * width, width), BF), v((width, width), BF), v((width, 3 * width), BF),
            v((rows, width), BF), v((rows, width), BF), v((2, rows, width), BF), v((2, rows, width), BF), v((rows, width), BF),
            v((rows, width), F32), v((2, BQ, width), F32), v((rows, width), BF),
            v((2, 2, 2, nf * hw, hw), BF), v((wholes, 2, PIECE, hw), BF), v((wholes, 2, PIECE, hw), BF), v((wholes, PIECE, hw), BF),
            v(sums, F32), v((m + 1,) + sums, F32), v((m + 2,) + sums, F32),
            DMA((3, 2, 2, nf)), DMA((9,)), DMA((2, 2, nf)), DMA((nb,)), DMA((3 + 2 * m, count)), DMA((3 + 2 * m, count)),
            DMA((m + 2,)), DMA((m + 2,)), DMA((2, nb)), DMA((nb,)), DMA((nb,)), DMA((1,)), DMA((count,)),
        ],
        compiler_params=params(collective_id=1, has_side_effects=True),
        cost_estimate=cost(60e9, 60e6, 8e6),
    )(lens, vecs, *saved, *own, *oth)


def finish_body(
    lens_ref, deal_ref, sums_ref, res_in, dx_in, dxr_in, out_in, outr_in, y_out, d_out, *rest
):
    outs, scratch = rest[:13], rest[13:]
    (o_g1, o_b1, o_qkv, o_qb, o_vb, o_wo, o_ob, o_g2, o_b2, o_fc, o_fb, o_proj, o_pb) = outs
    res_ref, src_ref, y_ref, qkv_ref, wo_ref, fc_ref, proj_ref, lsem, ssem = scratch
    shard = lax.axis_index("shard")
    rows, width = src_ref.shape[1:]
    hw = width // 2
    nb = rows // BQ
    slots = y_ref.shape[1]
    nf = fc_ref.shape[1] // width
    plan = Plan(lens_ref, shard, rows)
    loads = [pltpu.make_async_copy(a, src_ref.at[n], lsem.at[n]) for n, a in enumerate((out_in, outr_in, dx_in, dxr_in))]
    per = res_in.shape[1] // 3
    pieces = [pltpu.make_async_copy(res_in.at[:, pl.ds(per * a, per)], res_ref.at[:, pl.ds(per * a, per)], lsem.at[4 + a]) for a in range(3)]
    for copy in loads + pieces:
        copy.start()
    own = pl.ds(pl.multiple_of(shard * hw, 128), hw)
    for ref, row in ((o_g1, 11), (o_b1, 12), (o_qb, 8), (o_vb, 10), (o_ob, 3), (o_g2, 0), (o_b2, 1), (o_pb, 2)):
        ref[...] = sums_ref[row, own]
    for j in range(nf):
        o_fb[j * hw : (j + 1) * hw] = sums_ref[16 + j, own]

    def save(n, src, dst):
        return pltpu.make_async_copy(src, dst, ssem.at[n])

    saves = []
    for g in range(2):
        loads[2 * g].wait()
        loads[2 * g + 1].wait()
        for j in range(slots):
            q = slots * shard + j
            if g == 0:
                q = sum(jnp.where(q == n, deal_ref[0, n], 0) for n in range(2 * slots))
            side, offset, size = plan.where(q)

            @pl.loop(0, nb)
            def _(i):
                low, pick = window_pick(rows, i * BQ + offset, BQ)
                row = i * BQ + lax.broadcasted_iota(jnp.int32, pick.shape, 0)
                pick = jnp.where(pick & (row < size), 1.0, 0.0).astype(BF)
                y_ref[g, j, rows_of(i, BQ), :] = dot(pick, src_ref[2 * g + side, pl.ds(low, WINDOW), :]).astype(BF)

            saves.append(save(2 * g + j, y_ref.at[g, j], (y_out, d_out)[g].at[j]))
            saves[-1].start()
    block = lambda c, a, n, r, size: res_ref[c, a * per + (n * hw + r) // PIECE, (n * hw + r) % PIECE : (n * hw + r) % PIECE + size, :]
    for a, (dst, out) in enumerate(((fc_ref, o_fc), (proj_ref, o_proj), (qkv_ref, o_qkv))):
        pieces[a].wait()
        for n in range(nf):
            for c in range(2):
                for r in range(0, hw, 128):
                    value = block(c, a, n, r, 128).astype(F32)
                    at = slice(r, r + 128)
                    if a == 0:
                        fc_ref[at, (c * nf + n) * hw : (c * nf + n + 1) * hw] = value
                    elif a == 1:
                        proj_ref[n * hw + r : n * hw + r + 128, c * hw : (c + 1) * hw] = value
                    elif n == 0:
                        wo_ref[at, c * hw : (c + 1) * hw] = value
                    else:
                        tcols = width // THIRDS
                        cut, lead = hw - tcols, (n - 1) * tcols
                        if c == 0:
                            qkv_ref[at, lead : lead + tcols] = value[:, 0:tcols]
                            qkv_ref[at, width + lead : width + lead + cut] = value[:, tcols:hw]
                        else:
                            qkv_ref[at, width + lead + cut : width + lead + tcols] = value[:, 0:cut]
                            qkv_ref[at, 2 * width + lead : 2 * width + lead + tcols] = value[:, cut:hw]
        saves.append(save(4 + a, dst, out))
        saves[-1].start()
    saves.append(save(7, wo_ref, o_wo))
    saves[-1].start()
    for copy in saves:
        copy.wait()


def finish(lens, deal, sums, res, dx, dxr, out, outr, slots):
    rows, width = dx.shape
    hw = width // 2
    nf = res.shape[1] * PIECE // 3 // hw
    s = jax.ShapeDtypeStruct
    v = pltpu.VMEM
    vec, act = s((hw,), F32), s((slots, rows, width), BF)
    wide = lambda a, b: s((a, b), F32)
    vs, an = vspecs(1), anyspecs(1)
    return pl.pallas_call(
        finish_body,
        name="finish",
        out_shape=(act, act, vec, vec, wide(hw, 3 * width), vec, vec, wide(hw, width), vec, vec, vec, wide(hw, nf * width),
                   s((nf * hw,), F32), wide(nf * hw, width), vec),
        in_specs=[SMEM, SMEM] + vs + anyspecs(5),
        out_specs=tuple(an * 2 + vs * 2 + an + vs * 2 + an + vs * 3 + an + vs + an + vs),
        scratch_shapes=[
            v(res.shape, BF), v((4, rows, width), BF), v((2, slots, rows, width), BF),
            v((hw, 3 * width), F32), v((hw, width), F32), v((hw, nf * width), F32), v((nf * hw, width), F32), DMA((7,)), DMA((8,)),
        ],
        compiler_params=params(),
        cost_estimate=cost(8e9, 34e6),
    )(lens, deal, sums, res, dx, dxr, out, outr)


def local(bits, layer_in, cotangent, lengths, dealing, g1, b1, wqkv, qb, vb, wout, ob, g2, b2, wfc, bfc, wproj, pb):
    slots, rows, width = layer_in.shape
    own = (wqkv, wout, wfc, wproj)
    got = front(lengths, layer_in, cotangent, (g1, b1, qb, vb, ob, g2, b2, pb, bfc), *own)
    saved, oth, vecs = got[:10], got[10:14], got[14]
    res, dx, dxr, outr, sums = back(bits, lengths, vecs, saved, own, oth)
    return finish(lengths, dealing, sums, res, dx, dxr, saved[8], outr, slots)


def solution(mesh):
    both, one = P(("rep", "shard"), None, None), P("shard")
    mat = P("shard", None)
    in_specs = (both, both, P("rep", None), P("rep", None), one, one, mat, one, one, mat, one, one, one, mat, one, mat, one)
    out_specs = (both, both, one, one, mat, one, one, mat, one, one, one, mat, one, mat, one)
    bits = mesh.shape["rep"].bit_length() - 1
    return jax.shard_map(functools.partial(local, bits), mesh=mesh, in_specs=in_specs, out_specs=out_specs, check_vma=False)
```
